32 devices in a mesh: dp: 16 (over z, y, core), mp: 2 (over x).
Axes of the slice: x: 2, y: 2, z: 4, core: 2. Of those that a mesh axis runs over, the one named last changes fastest.
Arguments:
- latents: bfloat16 [16, 1024, 640], P('dp'), may hold values from -6 to 6
- out_grad: bfloat16 [16, 1024, 640], P('dp', 'mp'), may hold values from -6 to 6
- text_states: bfloat16 [16, 77, 768], P('dp'), may hold values from -6 to 6
- time_embed: float32 [16, 1280], P('dp'), may hold values from -6 to 6
- group_ids: int32 [16], P('dp'), may hold values 0 or 1
- group_weights: float32 [2], replicated, may hold values from 0.5 to 2
- timesteps: int32 [16], P('dp'), may hold values from 0 to 999
- step_weights: float32 [1000], replicated, may hold values from 0.2 to 1
- vectors: float32 [12, 640], replicated, may hold values from -1.5 to 1.5
- split_vectors: float32 [4, 640], P(None, 'mp'), may hold values from -1.5 to 1.5
- up_bias: float32 [2, 2560], P(None, 'mp'), may hold values from -1.5 to 1.5
- conv_one: bfloat16 [9, 640, 640], P(None, 'dp', 'mp'), may hold values from -0.078125 to 0.078125
- conv_two: bfloat16 [9, 640, 640], P(None, 'mp', 'dp'), may hold values from -0.078125 to 0.078125
- time_proj: bfloat16 [1280, 640], P('dp', 'mp'), may hold values from -0.15625 to 0.15625
- self_query: bfloat16 [640, 640], P('dp', 'mp'), may hold values from -0.25 to 0.25
- self_kv: bfloat16 [640, 2, 640], P('dp', None, 'mp'), may hold values from -0.25 to 0.25
- self_out: bfloat16 [640, 640], P('mp', 'dp'), may hold values from -6 to 6
- cross_query: bfloat16 [640, 640], P('dp', 'mp'), may hold values from -0.25 to 0.25
- cross_kv: bfloat16 [768, 2, 640], P('dp', None, 'mp'), may hold values from -0.21875 to 0.21875
- cross_out: bfloat16 [640, 640], P('mp', 'dp'), may hold values from -1.75 to 1.75
- ff_up: bfloat16 [640, 2, 2560], P('dp', None, 'mp'), may hold values from -0.25 to 0.25
- ff_down: bfloat16 [2560, 640], P('mp', 'dp'), may hold values from -0.125 to 0.125
- query_left_state: float32 [4, 2, 640, 8], replicated, as said below
- query_right_state: float32 [4, 2, 8, 640], P(None, None, None, 'mp'), as said below
- up_left_state: float32 [4, 2, 640, 8], replicated, as said below
- up_right_state: float32 [4, 2, 8, 2, 2560], P(None, None, None, None, 'mp'), as said below
Outputs:
- block_out: bfloat16 [16, 1024, 640], P('dp', 'mp')
- latents_grad: bfloat16 [16, 1024, 640], P('dp')
- query_left_new: float32 [2, 2, 640, 8], replicated
- query_left_copy: bfloat16 [2, 640, 8], replicated
- query_right_new: float32 [2, 2, 8, 640], P(None, None, None, 'mp')
- query_right_copy: bfloat16 [2, 8, 640], P(None, None, 'mp')
- up_left_new: float32 [4, 2, 640, 8], replicated
- up_left_copy: bfloat16 [2, 640, 8], replicated
- up_right_new: float32 [4, 2, 8, 2, 2560], P(None, None, None, None, 'mp')
- up_right_copy: bfloat16 [2, 8, 2, 2560], P(None, None, None, 'mp')
- query_moments: float32 [2, 2, 2, 8, 640], P(None, None, None, None, 'mp')
The draws below stay inside these ranges and needn't reach their ends.
Inputs may be any that keep to these rules, and one draw needn't show every extreme that they name: `query_left_state`: entry 0 of the first dimension holds the factor weights, 1 the first moment, 2 the second moment (positive), 3 the EMA. `query_right_state`: entry 0 of the first dimension holds the factor weights, 1 the first moment, 2 the second moment (positive), 3 the EMA. `up_left_state`: entry 0 of the first dimension holds the factor weights, 1 the first moment, 2 the second moment (positive), 3 the EMA. `up_right_state`: entry 0 of the first dimension holds the factor weights, 1 the first moment, 2 the second moment (positive), 3 the EMA.
All inputs are finite; a program needn't handle non-finite values. No bound on the sum of `group_ids` on one device may be relied on, other than what follows from the above.
Results may differ from the reference program's by a relative error of at most 0.025.
Values may be sent and summed in bfloat16 or wider, within the bound.
A program may use at most 192 MiB of HBM per device.

```python
import math
import jax
import jax.numpy as jnp
from jax import lax

D = 640
FF = 2560
HEADS = 8
HEAD_DIM = 80
GROUPS = 32
TEXT_LEN = 77
TEXT_WIDTH = 768
TIME_WIDTH = 1280
RANK = 8
SIDE = 32
LENGTH = 1024
TIMESTEPS = 1000
ADAM_STEP = 10
SEQS = 16


def factor_state(key, shape, grad_scale):
    keys = jax.random.split(key, 4)
    weight = 0.2 * jax.random.truncated_normal(keys[0], -3.0, 3.0, shape, jnp.float32)
    moment = grad_scale * 0.11 * jax.random.normal(keys[1], shape, jnp.float32)
    spread = jnp.exp(jax.random.uniform(keys[2], shape, jnp.float32, math.log(0.5), math.log(8.0)))
    second = grad_scale * grad_scale * 0.001 * spread
    average = weight + 0.04 * jax.random.normal(keys[3], shape, jnp.float32)
    return jnp.stack([weight, moment, second, average])


def draw_query_left_state(key, part):
    return factor_state(jax.random.fold_in(key, 21), (2, D, RANK), 0.04 * math.sqrt(SEQS * LENGTH * D))


def draw_query_right_state(key, part):
    return factor_state(jax.random.fold_in(key, 22), (2, RANK, D), 0.04 * math.sqrt(SEQS * LENGTH * D))


def draw_up_left_state(key, part):
    return factor_state(jax.random.fold_in(key, 23), (2, D, RANK), 0.004 * math.sqrt(SEQS * LENGTH * 2 * FF))


def draw_up_right_state(key, part):
    return factor_state(jax.random.fold_in(key, 24), (2, RANK, 2, FF), 0.004 * math.sqrt(SEQS * LENGTH * D))


def place_ends(drawn, key, smallest, top_value):
    longest = drawn.shape.index(max(drawn.shape))
    spots = []
    for shift in (0, 1):
        where = [jax.random.randint(jax.random.fold_in(key, axis), (), 0, length) for axis, length in enumerate(drawn.shape)]
        where[longest] = (where[longest] + shift) % drawn.shape[longest]
        spots.append(tuple(where))
    return drawn.at[spots[0]].set(smallest).at[spots[1]].set(top_value)


def levels(stream_key, shape, cuts, smallest, largest):
    level = 1.0
    for dim, blocks in cuts:
        heights = jax.random.uniform(jax.random.fold_in(jax.random.fold_in(stream_key, 6), dim), (blocks,), jnp.float32, smallest / len(cuts), largest / len(cuts))
        level = level * jnp.repeat(jnp.exp(heights), shape[dim] // blocks).reshape((-1,) + (1,) * (len(shape) - 1 - dim))
    return level


def gaussian(stream_key, dims, width, limit, shards=(), dtype=jnp.bfloat16):
    array = width * jax.random.normal(stream_key, dims, jnp.float32)
    if shards:
        array = array * levels(stream_key, dims, shards, -0.22, 0.18)
    return jnp.clip(array, -limit, limit).astype(dtype)


def setup_inputs(seed: int = 0) -> dict:
    splits = jax.random.split(jax.random.key(seed), 27)
    return {
        "latents": gaussian(splits[0], (SEQS, LENGTH, D), 1.0, 6.0, ((0, 16),)),
        "out_grad": gaussian(splits[1], (SEQS, LENGTH, D), 1.0, 6.0, ((0, 16), (1, 2))),
        "text_states": gaussian(splits[2], (SEQS, TEXT_LEN, TEXT_WIDTH), 1.0, 6.0, ((0, 16),)),
        "time_embed": gaussian(splits[3], (SEQS, TIME_WIDTH), 1.0, 6.0, ((0, 16),), jnp.float32),
        "group_ids": place_ends((jax.random.randint(splits[4], (SEQS,), 0, 4) < 1).astype(jnp.int32), jax.random.fold_in(splits[4], 1), 0, 1),
        "group_weights": jnp.clip(jnp.exp(jax.random.uniform(splits[5], (2,), jnp.float32, math.log(0.5), math.log(2.0))), 0.5, 2.0),
        "timesteps": place_ends(jax.random.randint(splits[6], (SEQS,), 0, TIMESTEPS), jax.random.fold_in(splits[6], 1), 0, TIMESTEPS - 1).astype(jnp.int32),
        "step_weights": jnp.clip(jnp.exp(jax.random.uniform(splits[7], (TIMESTEPS,), jnp.float32, math.log(0.2), math.log(1.0))), 0.2, 1.0),
        "vectors": gaussian(splits[8], (12, D), 0.3, 1.5, (), jnp.float32),
        "split_vectors": gaussian(splits[9], (4, D), 0.3, 1.5, ((1, 2),), jnp.float32),
        "up_bias": gaussian(splits[10], (2, FF), 0.3, 1.5, ((1, 2),), jnp.float32),
        "conv_one": gaussian(splits[11], (9, D, D), (9 * D) ** -0.5, 0.078125, ((1, 16), (2, 2))),
        "conv_two": gaussian(splits[12], (9, D, D), (9 * D) ** -0.5, 0.078125, ((1, 2), (2, 16))),
        "time_proj": gaussian(splits[13], (TIME_WIDTH, D), TIME_WIDTH ** -0.5, 0.15625, ((0, 16), (1, 2))),
        "self_query": gaussian(splits[14], (D, D), D ** -0.5, 0.25, ((0, 16), (1, 2))),
        "self_kv": gaussian(splits[15], (D, 2, D), D ** -0.5, 0.25, ((0, 16), (2, 2))),
        "self_out": gaussian(splits[16], (D, D), (max(D * 3 // LENGTH, 1)) ** -0.5, 6.0, ((0, 2), (1, 16))),
        "cross_query": gaussian(splits[17], (D, D), D ** -0.5, 0.25, ((0, 16), (1, 2))),
        "cross_kv": gaussian(splits[18], (TEXT_WIDTH, 2, D), TEXT_WIDTH ** -0.5, 0.21875, ((0, 16), (2, 2))),
        "cross_out": gaussian(splits[19], (D, D), (max(D * 3 // (2 * TEXT_LEN), 1)) ** -0.5, 1.75, ((0, 2), (1, 16))),
        "ff_up": gaussian(splits[20], (D, 2, FF), D ** -0.5, 0.25, ((0, 16), (2, 2))),
        "ff_down": gaussian(splits[21], (FF, D), FF ** -0.5, 0.125, ((0, 2), (1, 16))),
        "query_left_state": draw_query_left_state(jax.random.fold_in(splits[26], 71), 0),
        "query_right_state": draw_query_right_state(jax.random.fold_in(splits[26], 71), 0),
        "up_left_state": draw_up_left_state(jax.random.fold_in(splits[26], 71), 0),
        "up_right_state": draw_up_right_state(jax.random.fold_in(splits[26], 71), 0),
    }


@jax.custom_vjp
def low(v):
    return lax.optimization_barrier(v.astype(jnp.bfloat16)).astype(jnp.float32)

@jax.custom_vjp
def low_back(v):
    return v

def low_keep(v):
    return (low(v), None)

def low_pass(kept, grad):
    return (grad,)

def back_keep(v):
    return (v, None)

def back_low(kept, grad):
    return (low(grad),)
low.defvjp(low_keep, low_pass)
low_back.defvjp(back_keep, back_low)
NORM_EPS = 1e-05
BETA_ONE = 0.9
BETA_TWO = 0.999
ADAM_EPS = 1e-08
DECAY_RATE = 0.01
LEARN_RATE = 0.06
EMA_KEEP = 0.995
INV_ROOT_TWO = 0.7071067811865476

def both(values):
    return low(low_back(values))

def silu(values):
    return values * jax.nn.sigmoid(values)

def gelu(values):
    return values * 0.5 * (1.0 + lax.erf(values * INV_ROOT_TWO))

def group_stat(values):
    members = D // GROUPS
    column = lax.optimization_barrier(jnp.mean(values, axis=0))
    return jnp.repeat(lax.optimization_barrier(jnp.mean(column.reshape(-1, members), axis=1)), members)

def group_norm(values, gain, bias):
    centred = values - group_stat(values)
    return centred * lax.rsqrt(group_stat(centred * centred) + NORM_EPS) * gain + bias

def layer_norm(values, gain, bias):
    centred = values - lax.optimization_barrier(jnp.mean(values, axis=1, keepdims=True))
    row_var = lax.optimization_barrier(jnp.mean(centred * centred, axis=1, keepdims=True))
    return centred * lax.rsqrt(row_var + NORM_EPS) * gain + bias

def conv_taps(rows, weight):
    channels = rows.shape[1]
    image = jnp.pad(rows.reshape(SIDE, SIDE, channels), ((1, 1), (1, 1), (0, 0)))
    total = jnp.zeros((SIDE * SIDE, weight.shape[2]), jnp.float32)
    for stencil in range(9):
        piece = image[stencil // 3:stencil // 3 + SIDE, stencil % 3:stencil % 3 + SIDE].reshape(SIDE * SIDE, channels)
        total = total + jnp.dot(piece, weight[stencil], precision=lax.Precision.HIGHEST)
    return total

def attend(query, keys, values):
    precise = lax.Precision.HIGHEST
    queries = query.reshape(query.shape[0], HEADS, HEAD_DIM)
    key_heads = keys.reshape(keys.shape[0], HEADS, HEAD_DIM)
    value_heads = values.reshape(values.shape[0], HEADS, HEAD_DIM)
    scores = low_back(jnp.einsum('qhe,khe->hqk', queries, key_heads, precision=precise) * HEAD_DIM ** (-0.5))
    expo = jnp.exp(scores)
    probs = expo / lax.optimization_barrier(jnp.sum(expo, axis=2, keepdims=True))
    result = jnp.einsum('hqk,khe->qhe', low(probs), value_heads, precision=precise)
    return result.reshape(query.shape[0], HEADS * HEAD_DIM)

def adamw_parts(state, grads):
    weight, moment, second, average = (state[0], state[1], state[2], state[3])
    moment = BETA_ONE * moment + (1.0 - BETA_ONE) * grads
    second = BETA_TWO * second + (1.0 - BETA_TWO) * grads * grads
    moment_hat = moment / (1.0 - BETA_ONE ** ADAM_STEP)
    second_hat = second / (1.0 - BETA_TWO ** ADAM_STEP)
    weight = weight - LEARN_RATE * (moment_hat / (jnp.sqrt(second_hat) + ADAM_EPS) + DECAY_RATE * weight)
    average = EMA_KEEP * average + (1.0 - EMA_KEEP) * weight
    return (weight, moment, second, average)

def adamw(state, grads):
    weight, moment, second, average = adamw_parts(state, grads)
    return (jnp.stack([weight, moment, second, average]), weight.astype(jnp.bfloat16))

def reference(latents, out_grad, text_states, time_embed, group_ids, group_weights, timesteps, step_weights, vectors, split_vectors, up_bias, conv_one, conv_two, time_proj, self_query, self_kv, self_out, cross_query, cross_kv, cross_out, ff_up, ff_down, query_left_state, query_right_state, up_left_state, up_right_state):
    precise = lax.Precision.HIGHEST
    scales = step_weights[timesteps] * group_weights[group_ids]
    cotangent = out_grad.astype(jnp.float32) * scales[:, None, None]
    base_conv_one = conv_one.astype(jnp.float32)
    base_conv_two = conv_two.astype(jnp.float32)
    base_time = time_proj.astype(jnp.float32)
    base_query = self_query.astype(jnp.float32)
    base_self_kv = self_kv.astype(jnp.float32)
    base_self_out = self_out.astype(jnp.float32)
    base_cross_query = cross_query.astype(jnp.float32)
    base_cross_kv = cross_kv.astype(jnp.float32)
    base_cross_out = cross_out.astype(jnp.float32)
    base_up = ff_up.astype(jnp.float32)
    base_down = ff_down.astype(jnp.float32)
    context_all = text_states.astype(jnp.float32)

    def forward(inputs, query_left, query_right, up_left, up_right):
        query_eff = low(base_query + jnp.dot(query_left[0], query_right[0], precision=precise) * jnp.dot(query_left[1], query_right[1], precision=precise))
        first = jnp.einsum('dr,rkf->dkf', up_left[0], up_right[0], precision=precise)
        second = jnp.einsum('dr,rkf->dkf', up_left[1], up_right[1], precision=precise)
        up_eff = low(base_up + first * second)

        def block(operands):
            rows, context, embed = operands
            act_one = low(silu(group_norm(rows, 1.0 + vectors[0], vectors[1])))
            shift = jnp.dot(low(silu(embed)), base_time, precision=precise) + split_vectors[1]
            inner = low_back(conv_taps(act_one, base_conv_one) + split_vectors[0] + shift)
            act_two = low(silu(group_norm(inner, 1.0 + split_vectors[2], split_vectors[3])))
            stream = rows + low_back(conv_taps(act_two, base_conv_two) + vectors[2])
            normed = low(layer_norm(stream, 1.0 + vectors[3], vectors[4]))
            query = both(jnp.dot(normed, query_eff, precision=precise))
            key_value = both(jnp.einsum('td,dkc->tkc', normed, base_self_kv, precision=precise))
            attended = both(attend(query, key_value[:, 0], key_value[:, 1]))
            stream = stream + low_back(jnp.dot(attended, base_self_out, precision=precise) + vectors[9])
            normed = low(layer_norm(stream, 1.0 + vectors[5], vectors[6]))
            cross_q = both(jnp.dot(normed, base_cross_query, precision=precise))
            cross_values = low(jnp.einsum('sd,dkc->skc', context, base_cross_kv, precision=precise))
            attended = both(attend(cross_q, cross_values[:, 0], cross_values[:, 1]))
            stream = stream + low_back(jnp.dot(attended, base_cross_out, precision=precise) + vectors[10])
            normed = low(layer_norm(stream, 1.0 + vectors[7], vectors[8]))
            mixed = low_back(jnp.einsum('td,dkf->tkf', normed, up_eff, precision=precise) + up_bias)
            hidden = low(mixed[:, 0] * gelu(mixed[:, 1]))
            return stream + low_back(jnp.dot(hidden, base_down, precision=precise) + vectors[11])
        return lax.map(jax.checkpoint(block), (inputs, context_all, time_embed))
    block_out, pullback = jax.vjp(forward, latents.astype(jnp.float32), query_left_state[0], query_right_state[0], up_left_state[0], up_right_state[0])
    grads = pullback(cotangent)
    left_weight, left_moment, left_second, left_average = adamw_parts(query_left_state, grads[1])
    right_weight, right_moment, right_second, right_average = adamw_parts(query_right_state, grads[2])
    query_left_new = jnp.stack([left_weight, left_average])
    query_left_copy = left_weight.astype(jnp.bfloat16)
    query_right_new = jnp.stack([right_weight, right_average])
    query_right_copy = right_weight.astype(jnp.bfloat16)
    left_pair = jnp.stack([left_moment, left_second]).transpose(0, 1, 3, 2)
    right_pair = jnp.stack([right_moment, right_second])
    query_moments = jnp.stack([left_pair, right_pair])
    up_left_new, up_left_copy = adamw(up_left_state, grads[3])
    up_right_new, up_right_copy = adamw(up_right_state, grads[4])
    return (block_out.astype(jnp.bfloat16), grads[0].astype(jnp.bfloat16), query_left_new, query_left_copy, query_right_new, query_right_copy, up_left_new, up_left_copy, up_right_new, up_right_copy, query_moments)
```

```python
import functools

import jax
import jax.numpy as jnp
from jax import lax
from jax.experimental import pallas as pl
from jax.experimental.pallas import tpu as pltpu
from jax.sharding import PartitionSpec as P

D = 640
HEAD_DIM = 80
GROUPS = 32
SIDE = 32
ADAM_STEP = 10
LANES = 128

NORM_EPS = 1e-05
BETA_ONE = 0.9
BETA_TWO = 0.999
ADAM_EPS = 1e-08
DECAY_RATE = 0.01
LEARN_RATE = 0.06
EMA_KEEP = 0.995
INV_ROOT_TWO = 0.7071067811865476
INV_ROOT_TWOPI = 0.3989422804014327

MESH = pl.DeviceIdType.MESH
BF = jnp.bfloat16
F32 = jnp.float32


def adamw_parts(state, grads):
    weight, moment, second, average = (state[0], state[1], state[2], state[3])
    moment = BETA_ONE * moment + (1.0 - BETA_ONE) * grads
    second = BETA_TWO * second + (1.0 - BETA_TWO) * grads * grads
    moment_hat = moment / (1.0 - BETA_ONE**ADAM_STEP)
    second_hat = second / (1.0 - BETA_TWO**ADAM_STEP)
    weight = weight - LEARN_RATE * (
        moment_hat / (jnp.sqrt(second_hat) + ADAM_EPS) + DECAY_RATE * weight
    )
    average = EMA_KEEP * average + (1.0 - EMA_KEEP) * weight
    return (weight, moment, second, average)


def adamw(state, grads):
    weight, moment, second, average = adamw_parts(state, grads)
    return (jnp.stack([weight, moment, second, average]), weight.astype(BF))


def dot_nn(left, right):
    return jnp.dot(left, right, preferred_element_type=F32)


def dot_nt(left, right):
    return lax.dot_general(left, right, (((1,), (1,)), ((), ())), preferred_element_type=F32)


def dot_tn(left, right):
    return lax.dot_general(left, right, (((0,), (0,)), ((), ())), preferred_element_type=F32)


def silu_slope(values):
    sigma = jax.nn.sigmoid(values)
    return sigma * (1.0 + values * (1.0 - sigma))


def layer_norm(values, gain, bias):
    centred = values - jnp.mean(values, axis=1, keepdims=True)
    inv_std = lax.rsqrt(jnp.mean(centred * centred, axis=1, keepdims=True) + NORM_EPS)
    normal = centred * inv_std
    return (normal * gain + bias, normal, inv_std)


def layer_back(grads, normal, inv_std, gain):
    scaled = grads * gain
    return inv_std * (
        scaled
        - jnp.mean(scaled, axis=1, keepdims=True)
        - normal * jnp.mean(scaled * normal, axis=1, keepdims=True)
    )


def ring_chip(place, chips):
    place = lax.rem(place + 2 * chips, chips)
    return jnp.where(place < chips // 2, 2 * place, 2 * (chips - 1 - place) + 1)


def ring_place(chip, chips):
    column = chip // 2
    return jnp.where(lax.rem(chip, 2) == 0, column, chips - 1 - column)


WHOLE = pl.BlockSpec(memory_space=pltpu.VMEM)
VMEM_BYTES = 63 * 1024 * 1024
FACTOR = HEAD_DIM**-0.5
LOG_TWO_E = 1.4426950408889634
HEADS = D // HEAD_DIM
RANK_SQ = 64


def split_low(values):
    high = values.astype(BF)
    return high, (values - high.astype(F32)).astype(BF)


def to_heads(slots, values):
    blank = jnp.zeros((values.shape[0], LANES - HEAD_DIM), BF)
    for head in range(HEADS):
        part = values[:, HEAD_DIM * head : HEAD_DIM * (head + 1)]
        slots[head] = jnp.concatenate([part, blank], axis=1)


def from_heads(slots):
    return jnp.concatenate([slots[head][:, :HEAD_DIM] for head in range(HEADS)], axis=1)


def ff_kernel(
    h3_ref,
    cot_ref,
    scale_ref,
    vec_ref,
    weights_ref,
    bias_ref,
    left_ref,
    right_ref,
    out_ref,
    g2_ref,
    outer_ref,
    inner_ref,
    act,
    cot_low,
    wide,
    down_acc,
    back_acc,
):
    tile = pl.program_id(0)
    down_ref = weights_ref.at[2]
    cols = down_ref.shape[1]
    gain = 1.0 + vec_ref[7:8, :]

    @pl.when(tile == 0)
    def _():
        norm, _, _ = layer_norm(h3_ref[...], gain, vec_ref[8:9, :])
        low = norm.astype(BF)
        act[:, :D] = low
        act[:, D:] = dot_nn(low, left_ref[...]).astype(BF)
        cot_low[...] = (cot_ref[...].astype(F32) * scale_ref[0, 0]).astype(BF)

    for part in range(2):
        wide[:D, part * cols : (part + 1) * cols] = weights_ref[part]
        wide[D:, part * cols : (part + 1) * cols] = right_ref[part]
    mixed = dot_nn(act[...], wide[...])
    value = mixed[:, :cols] + bias_ref[0:1, :]
    gate = mixed[:, cols:] + bias_ref[1:2, :]
    cdf = 0.5 * (1.0 + lax.erf(gate * INV_ROOT_TWO))
    gelu = gate * cdf
    hidden = (value * gelu).astype(BF)
    down = dot_nt(hidden, down_ref[...])
    hidden_grad = dot_nn(cot_low[...], down_ref[...])
    slope = cdf + gate * jnp.exp(-0.5 * gate * gate) * INV_ROOT_TWOPI
    grads = jnp.concatenate(
        [(hidden_grad * gelu).astype(BF), (hidden_grad * value * slope).astype(BF)], axis=1
    )
    outer = dot_tn(act[:, D:], grads)
    outer_ref[0] = outer[:, :cols]
    outer_ref[1] = outer[:, cols:]
    back = dot_nt(grads, wide[...])

    @pl.when(tile == 0)
    def _():
        down_acc[...] = down
        back_acc[...] = back

    @pl.when(tile > 0)
    def _():
        down_acc[...] += down
        back_acc[...] += back

    @pl.when(tile == pl.num_programs(0) - 1)
    def _():
        out_ref[...] = (h3_ref[...] + (down_acc[...] + vec_ref[11:12, :])).astype(BF)
        low_rank = back_acc[:, D:].astype(BF)
        inner_ref[...] = dot_tn(act[:, :D], low_rank)
        normed_grad = back_acc[:, :D] + dot_nt(low_rank, left_ref[...])
        _, normal, inv = layer_norm(h3_ref[...], gain, vec_ref[8:9, :])
        cot = cot_ref[...].astype(F32) * scale_ref[0, 0]
        g2_ref[...] = cot + layer_back(normed_grad, normal, inv, gain)


def feed_forward(h3, cot, scale, vectors, weights, bias, left, right):
    share = h3.shape[0]
    hidden = weights.shape[2]
    cols = 256
    return pl.pallas_call(
        ff_kernel,
        grid=(hidden // cols,),
        out_shape=[
            jax.ShapeDtypeStruct((share, D), BF),
            jax.ShapeDtypeStruct((share, D), F32),
            jax.ShapeDtypeStruct((2, RANK_SQ, hidden), F32),
            jax.ShapeDtypeStruct((D, RANK_SQ), F32),
        ],
        in_specs=[
            WHOLE,
            WHOLE,
            pl.BlockSpec(memory_space=pltpu.SMEM),
            WHOLE,
            pl.BlockSpec((3, D, cols), lambda i: (0, 0, i)),
            pl.BlockSpec((2, cols), lambda i: (0, i)),
            WHOLE,
            pl.BlockSpec((2, RANK_SQ, cols), lambda i: (0, 0, i)),
        ],
        out_specs=[WHOLE, WHOLE, pl.BlockSpec((2, RANK_SQ, cols), lambda i: (0, 0, i)), WHOLE],
        scratch_shapes=[
            pltpu.VMEM((share, D + RANK_SQ), BF),
            pltpu.VMEM((share, D), BF),
            pltpu.VMEM((D + RANK_SQ, 2 * cols), BF),
            pltpu.VMEM((share, D), F32),
            pltpu.VMEM((share, D + RANK_SQ), F32),
        ],
        compiler_params=pltpu.CompilerParams(vmem_limit_bytes=VMEM_BYTES),
        name="feed_forward",
    )(h3, cot, scale, vectors, weights, bias, left, right)


def partner_barrier():
    index = lax.axis_index("dp")
    where = (index + 1 - 2 * lax.rem(index, 2), lax.axis_index("mp"))
    barrier = pltpu.get_barrier_semaphore()
    pl.semaphore_signal(barrier, inc=1, device_id=where, device_id_type=MESH)
    return lax.rem(index, 2), where, barrier


def send_to(where, src, dst, sems, slot):
    return pltpu.make_async_remote_copy(
        src_ref=src,
        dst_ref=dst,
        send_sem=sems.at[0, slot],
        recv_sem=sems.at[1, slot],
        device_id=where,
        device_id_type=MESH,
    )


def attention_kernel(
    chips,
    h_ref,
    vec_ref,
    wq_ref,
    left_ref,
    right_ref,
    wkv_ref,
    wso_ref,
    wcq_ref,
    wckv_ref,
    wco_ref,
    text_ref,
    ff_ref,
    h2_ref,
    h3_ref,
    q_out,
    kv_out,
    o_out,
    lse_out,
    cq_out,
    ckv_out,
    ff_out,
    wide,
    act,
    heads,
    lse,
    sems,
    ring_sems,
    pair_sems,
    own_sems,
):
    ring = Ring(chips, ring_sems, pair_sems, own_sems)
    core, where = ring.core, (ring.partner, ring.plane)
    barrier = pltpu.get_barrier_semaphore()
    gathers = ff_ref.shape[1] * 2 * chips == ff_out.shape[1]
    others = [where]
    if gathers:
        others += [(ring.right, ring.plane), (ring.left, ring.plane)]
    for other in others:
        pl.semaphore_signal(barrier, inc=1, device_id=other, device_id_type=MESH)
    pl.semaphore_wait(barrier, len(others))
    rows = ff_ref.shape[1]
    events = []
    if gathers:
        for part in range(3):

            def target(owner, part=part):
                at = pl.multiple_of(owner * rows, 8)
                return ff_out.at[part : part + 1, pl.ds(at, rows), :]

            ring.begin(ring.add(ff_ref.at[part : part + 1], target))
        events = [
            (which, way, step)
            for step in range(1, ring.half + 1)
            for which in range(3)
            for way in (0, 1)
            if step <= ring.last(which)[way]
        ]

    def poll(limit):
        for _ in range(min(limit, len(events))):
            ring.event(*events.pop(0))

    share = h_ref.shape[0]
    mine = pl.ds(pl.multiple_of(core * share, share), share)
    norm, _, _ = layer_norm(h_ref[...], 1.0 + vec_ref[3:4, :], vec_ref[4:5, :])
    low = norm.astype(BF)
    for part in range(2):
        proj = dot_nn(low, wkv_ref[part]).astype(BF)
        blank = jnp.zeros((share, LANES - HEAD_DIM), BF)
        for head in range(HEADS):
            piece = proj[:, HEAD_DIM * head : HEAD_DIM * (head + 1)]
            kv_out[part, head, mine, :] = jnp.concatenate([piece, blank], axis=1)
    copy = send_to(where, kv_out.at[:, :, mine, :], kv_out.at[:, :, mine, :], sems, 0)
    copy.start()
    poll(2)
    wide[:D, :] = wq_ref[...]
    wide[D:, :] = right_ref[...]
    act[:, :D] = low
    act[:, D:] = dot_nn(low, left_ref[...]).astype(BF)
    to_heads(q_out, dot_nn(act[...], wide[...]).astype(BF))
    for part in range(2):
        to_heads(ckv_out.at[part], dot_nn(text_ref[...], wckv_ref[part]).astype(BF))
    copy.wait()
    poll(2)
    lane = lax.broadcasted_iota(jnp.int32, (share, LANES), 1)
    lse[...] = jnp.zeros_like(lse)

    def one_head(head, carry):
        scores = dot_nt(q_out[head], kv_out[0, head])
        top = jnp.max(scores, axis=1, keepdims=True)
        expo = jnp.exp2((scores - top) * (FACTOR * LOG_TWO_E))
        total = jnp.sum(expo, axis=1, keepdims=True)
        probs = (expo * (1.0 / total)).astype(BF)
        heads[head] = dot_nn(probs, kv_out[1, head]).astype(BF)
        row = top * (FACTOR * LOG_TWO_E) + jnp.log2(total)
        lse[...] = jnp.where(lane == head, row, lse[...])
        return carry

    for first in range(0, HEADS, 2):
        lax.fori_loop(first, first + 2, one_head, 0)
        poll(2)
    lse_out[...] = lse[...].T
    merged = from_heads(heads)
    o_out[...] = merged
    h2 = h_ref[...] + (dot_nt(merged, wso_ref[...]) + vec_ref[9:10, :])
    h2_ref[...] = h2
    poll(2)
    norm, _, _ = layer_norm(h2, 1.0 + vec_ref[5:6, :], vec_ref[6:7, :])
    to_heads(cq_out, dot_nn(norm.astype(BF), wcq_ref[...]).astype(BF))

    def cross_head(head, carry):
        probs = cross_probs(cq_out[head], ckv_out[0, head])
        heads[head] = dot_nn(probs.astype(BF), ckv_out[1, head]).astype(BF)
        return carry

    lax.fori_loop(0, HEADS, cross_head, 0)
    h3_ref[...] = h2_ref[...] + (dot_nt(from_heads(heads), wco_ref[...]) + vec_ref[10:11, :])
    poll(len(events))
    for which in range(len(ring.pieces)):
        ring.arrived(which)
        ring.drain(which)


TEXT = 77


def cross_probs(query, keys):
    scores = dot_nt(query, keys)
    column = lax.broadcasted_iota(jnp.int32, scores.shape, 1)
    scores = jnp.where(column < TEXT, scores, -1e30)
    top = jnp.max(scores, axis=1, keepdims=True)
    expo = jnp.exp2((scores - top) * (FACTOR * LOG_TWO_E))
    return expo * (1.0 / jnp.sum(expo, axis=1, keepdims=True))


def attention(h, vectors, wq, left, right, wkv, wso, wcq, wckv, wco, text, ff, chips, gathers):
    share = h.shape[0]
    full = (3, ff.shape[1] * 2 * chips, ff.shape[2]) if gathers else (1, 8, LANES)
    dma = pltpu.SemaphoreType.DMA
    return pl.pallas_call(
        functools.partial(attention_kernel, chips),
        out_shape=[
            jax.ShapeDtypeStruct((share, D), F32),
            jax.ShapeDtypeStruct((share, D), F32),
            jax.ShapeDtypeStruct((HEADS, share, LANES), BF),
            jax.ShapeDtypeStruct((2, HEADS, 2 * share, LANES), BF),
            jax.ShapeDtypeStruct((share, D), BF),
            jax.ShapeDtypeStruct((LANES, share), F32),
            jax.ShapeDtypeStruct((HEADS, share, LANES), BF),
            jax.ShapeDtypeStruct((2, HEADS, LANES, LANES), BF),
            jax.ShapeDtypeStruct(full, BF),
        ],
        in_specs=[WHOLE] * 12,
        out_specs=[WHOLE] * 8 + [pl.BlockSpec(memory_space=pl.ANY)],
        scratch_shapes=[
            pltpu.VMEM((D + RANK_SQ, D), BF),
            pltpu.VMEM((share, D + RANK_SQ), BF),
            pltpu.VMEM((HEADS, share, LANES), BF),
            pltpu.VMEM((share, LANES), F32),
            dma((2, 1)),
            dma((2, 2, 3, chips // 2)),
            dma((2, 3, chips)),
            dma((3,)),
        ],
        compiler_params=pltpu.CompilerParams(
            collective_id=3, has_side_effects=True, vmem_limit_bytes=VMEM_BYTES
        ),
        name="attention",
    )(h, vectors, wq, left, right, wkv, wso, wcq, wckv, wco, text, ff)


def attention_back_kernel(
    g2_ref,
    h_ref,
    h2_ref,
    vec_ref,
    wq_ref,
    left_ref,
    right_ref,
    wkv_ref,
    wso_ref,
    wcq_ref,
    wco_ref,
    q_ref,
    kv_ref,
    o_ref,
    lse_ref,
    cq_ref,
    ckv_ref,
    g0_ref,
    outer_ref,
    inner_ref,
    wide,
    act,
    dout,
    cot,
    delta,
    dq_acc,
    dkv_acc,
    give,
    take,
    sems,
):
    core, where, barrier = partner_barrier()
    share = h_ref.shape[0]
    dco = dot_nn(g2_ref[...].astype(BF), wco_ref[...]).astype(BF)
    to_heads(dout, dco)

    def cross_head(head, carry):
        probs = cross_probs(cq_ref[head], ckv_ref[0, head])
        dprobs = dot_nt(dout[head], ckv_ref[1, head])
        shift = jnp.sum(dprobs * probs, axis=1, keepdims=True)
        dscores = (probs * (dprobs - shift)).astype(BF)
        dout[head] = (dot_nn(dscores, ckv_ref[0, head]) * FACTOR).astype(BF)
        return carry

    lax.fori_loop(0, HEADS, cross_head, 0)
    gain = 1.0 + vec_ref[5:6, :]
    _, normal, inv = layer_norm(h2_ref[...], gain, vec_ref[6:7, :])
    cot[...] = g2_ref[...] + layer_back(
        dot_nt(from_heads(dout), wcq_ref[...]), normal, inv, gain
    )
    dso = dot_nn(cot[...].astype(BF), wso_ref[...]).astype(BF)
    to_heads(dout, dso)
    prod = dso.astype(F32) * o_ref[...].astype(F32)
    head_row = lax.broadcasted_iota(jnp.int32, (HEADS, D), 0)
    head_col = lax.broadcasted_iota(jnp.int32, (HEADS, D), 1)
    low_edge = head_row * HEAD_DIM
    mark = jnp.where((head_col >= low_edge) & (head_col < low_edge + HEAD_DIM), 1.0, 0.0).astype(BF)
    high, rest = split_low(prod)
    delta[...] = dot_nt(mark, high) + dot_nt(mark, rest)
    for turn in range(2):
        half = core if turn == 1 else 1 - core
        span = pl.ds(pl.multiple_of(half * share, share), share)

        def one_head(head, carry, turn=turn, span=span):
            keys = kv_ref[0, head, span, :]
            vals = kv_ref[1, head, span, :]
            query = q_ref[head]
            grad = dout[head]
            scores = dot_nt(keys, query)
            probs = jnp.exp2(scores * (FACTOR * LOG_TWO_E) - lse_ref[pl.ds(head, 1), :])
            dprobs = dot_nt(vals, grad)
            dscores = (probs * (dprobs - delta[pl.ds(head, 1), :])).astype(BF)
            dval = dot_nn(probs.astype(BF), grad)
            dkey = dot_nn(dscores, query) * FACTOR
            dquery = dot_tn(keys, dscores)
            if turn == 0:
                dq_acc[head] = dquery
                give[0, head] = dkey.astype(BF)
                give[1, head] = dval.astype(BF)
            else:
                dq_acc[head] += dquery
                dkv_acc[0, head] = dkey
                dkv_acc[1, head] = dval
            return carry

        lax.fori_loop(0, HEADS, one_head, 0)
        if turn == 0:
            pl.semaphore_wait(barrier, 1)
            copy = send_to(where, give, take, sems, 0)
            copy.start()
    for head in range(HEADS):
        dout[head] = (dq_acc[head].T * FACTOR).astype(BF)
    dq = from_heads(dout)
    gain = 1.0 + vec_ref[3:4, :]
    norm, normal, inv = layer_norm(h_ref[...], gain, vec_ref[4:5, :])
    low = norm.astype(BF)
    wide[:D, :] = wq_ref[...]
    wide[D:, :] = right_ref[...]
    back = dot_nt(dq, wide[...])
    low_rank = back[:, D:].astype(BF)
    outer_ref[...] = dot_tn(dot_nn(low, left_ref[...]).astype(BF), dq)
    inner_ref[...] = dot_tn(low, low_rank)
    total = back[:, :D] + dot_nt(low_rank, left_ref[...])
    copy.wait()
    for part in range(2):
        for head in range(HEADS):
            dout[head] = (dkv_acc[part, head] + take[part, head].astype(F32)).astype(BF)
        total += dot_nt(from_heads(dout), wkv_ref[part])
    g0_ref[...] = cot[...] + layer_back(total, normal, inv, gain)


def attention_back(g2, h, h2, vectors, wq, left, right, wkv, wso, wcq, wco, q, kv, o, lse, cq, ckv):
    share = h.shape[0]
    return pl.pallas_call(
        attention_back_kernel,
        out_shape=[
            jax.ShapeDtypeStruct((share, D), F32),
            jax.ShapeDtypeStruct((RANK_SQ, D), F32),
            jax.ShapeDtypeStruct((D, RANK_SQ), F32),
        ],
        in_specs=[WHOLE] * 17,
        out_specs=[WHOLE] * 3,
        scratch_shapes=[
            pltpu.VMEM((D + RANK_SQ, D), BF),
            pltpu.VMEM((share, D + RANK_SQ), BF),
            pltpu.VMEM((HEADS, share, LANES), BF),
            pltpu.VMEM((share, D), F32),
            pltpu.VMEM((HEADS, share), F32),
            pltpu.VMEM((HEADS, LANES, share), F32),
            pltpu.VMEM((2, HEADS, share, LANES), F32),
            pltpu.VMEM((2, HEADS, share, LANES), BF),
            pltpu.VMEM((2, HEADS, share, LANES), BF),
            pltpu.SemaphoreType.DMA((2, 1)),
        ],
        compiler_params=pltpu.CompilerParams(
            collective_id=4, has_side_effects=True, vmem_limit_bytes=VMEM_BYTES
        ),
        name="attention_back",
    )(g2, h, h2, vectors, wq, left, right, wkv, wso, wcq, wco, q, kv, o, lse, cq, ckv)


def pair_left(left):
    return (left[0][:, :, None] * left[1][:, None, :]).reshape(left.shape[1], RANK_SQ)


def pair_right(right):
    return (right[0][:, None] * right[1][None, :]).reshape((RANK_SQ,) + right.shape[2:])


def left_grads(inner, left):
    cube = inner.reshape(inner.shape[0], 8, 8)
    return jnp.stack(
        [jnp.sum(cube * left[1][:, None, :], axis=2), jnp.sum(cube * left[0][:, :, None], axis=1)]
    )


def right_grads(outer, right):
    cube = outer.reshape((8, 8) + outer.shape[1:])
    return jnp.stack(
        [jnp.sum(cube * right[1][None, :], axis=1), jnp.sum(cube * right[0][:, None], axis=0)]
    )


class Ring:
    def __init__(self, chips, ring_sems, core_sems, own_sems):
        self.chips = chips
        self.half = chips // 2
        index = lax.axis_index("dp")
        self.plane = lax.axis_index("mp")
        self.core = lax.rem(index, 2)
        self.place = ring_place(index // 2, chips)
        self.right = ring_chip(self.place + 1, chips) * 2 + self.core
        self.left = ring_chip(self.place - 1, chips) * 2 + self.core
        self.partner = index + 1 - 2 * self.core
        self.ring_sems, self.core_sems, self.own_sems = ring_sems, core_sems, own_sems
        self.pieces = []

    def add(self, source, target):
        self.pieces.append((source, target))
        return len(self.pieces) - 1

    def last(self, which):
        return (self.half, self.half - 1) if which % 2 == 0 else (self.half - 1, self.half)

    def spot(self, which, hop):
        return self.pieces[which][1](ring_chip(self.place - hop, self.chips) * 2 + self.core)

    def ring_copy(self, which, way, step):
        sign = 1 if way == 0 else -1
        spot = self.spot(which, sign * (step - 1))
        return pltpu.make_async_remote_copy(
            src_ref=self.pieces[which][0] if step == 1 else spot,
            dst_ref=spot,
            send_sem=self.ring_sems.at[0, way, which, step - 1],
            recv_sem=self.ring_sems.at[1, way, which, step - 1],
            device_id=(self.right if way == 0 else self.left, self.plane),
            device_id_type=MESH,
        )

    def core_copy(self, which, slot, hop):
        spot = self.spot(which, hop)
        return pltpu.make_async_remote_copy(
            src_ref=self.pieces[which][0] if slot == 0 else spot,
            dst_ref=spot,
            send_sem=self.core_sems.at[0, which, slot],
            recv_sem=self.core_sems.at[1, which, slot],
            device_id=(self.partner, self.plane),
            device_id_type=MESH,
        )

    def own_copy(self, which):
        return pltpu.make_async_copy(
            self.pieces[which][0], self.spot(which, 0), self.own_sems.at[which]
        )

    def begin(self, which):
        self.ring_copy(which, 0, 1).start()
        self.ring_copy(which, 1, 1).start()
        self.core_copy(which, 0, 0).start()
        self.own_copy(which).start()

    def event(self, which, way, step):
        self.ring_copy(which, way, step).wait_recv()
        if step < self.last(which)[way]:
            self.ring_copy(which, way, step + 1).start()
        slot = step if way == 0 else self.last(which)[0] + step
        self.core_copy(which, slot, step if way == 0 else -step).start()

    def arrived(self, which):
        for slot in range(self.chips):
            self.core_copy(which, slot, 0).wait_recv()
        self.own_copy(which).wait()

    def drain(self, which):
        last = self.last(which)
        for way in (0, 1):
            for step in range(1, last[way] + 1):
                self.ring_copy(which, way, step).wait_send()
        for slot in range(self.chips):
            self.core_copy(which, slot, 0).wait_send()


def remote(src, dst, where, sems, slot):
    return pltpu.make_async_remote_copy(
        src_ref=src,
        dst_ref=dst,
        send_sem=sems.at[0, slot],
        recv_sem=sems.at[1, slot],
        device_id=where,
        device_id_type=MESH,
    )


MEMBERS = D // GROUPS


def group_mean(column):
    column = jnp.broadcast_to(column, (8, D))
    lane = lax.broadcasted_iota(jnp.int32, (8, D), 1)
    first = lane == 0
    for group in range(1, GROUPS):
        first = first | (lane == group * MEMBERS)

    def shift(values, count):
        return pltpu.roll(values, count % D, 1)

    two = column + shift(column, -1)
    four = two + shift(two, -2)
    eight = four + shift(four, -4)
    whole = eight + shift(eight, -8) + shift(four, -16)
    whole = jnp.where(first, whole, 0.0)
    two = whole + shift(whole, 1)
    four = two + shift(two, 2)
    eight = four + shift(four, 4)
    spread = eight + shift(eight, 8) + shift(four, 16)
    return spread[0:1, :] * (1.0 / MEMBERS)


def col_mean(values):
    return jnp.sum(values, axis=0, keepdims=True) * (1.0 / values.shape[0])


def side_by_side(wide, values, order):
    rows = values.shape[0]
    column = lax.broadcasted_iota(jnp.int32, (rows, D), 0) & (SIDE - 1)
    before = jnp.where(column == 0, 0.0, pltpu.roll(values, 1, 0)).astype(BF)
    after = jnp.where(column == SIDE - 1, 0.0, pltpu.roll(values, rows - 1, 0)).astype(BF)
    parts = (before, values.astype(BF), after)
    for spot, part in enumerate(order):
        wide[:, spot * D : (spot + 1) * D] = parts[part]


CONV_SHARDS = ("one", "time", "two", "q", "kv", "so", "cq", "ckv", "co", "ff")


def conv_kernel(chips, gathers, *refs):
    count = len(CONV_SHARDS)
    lat_ref, emb_ref, split_ref, vec_ref = refs[:4]
    if gathers:
        shard = dict(zip(CONV_SHARDS, refs[4 : 4 + count]))
        refs = refs[4 + count :]
    else:
        full = dict(zip(CONV_SHARDS[:-1], refs[4 : 3 + count]))
        refs = refs[3 + count :]
    h_ref, h1_ref, img_ref, stat_ref, split_out = refs[:5]
    refs = refs[5:]
    if gathers:
        ff_ref = refs[0]
        full = dict(zip(CONV_SHARDS[:-1], refs[1:count]))
        refs = refs[count:]
        got = dict(zip(CONV_SHARDS, refs[:count]))
        joined = dict(zip(CONV_SHARDS[:-1], refs[count : 2 * count - 1]))
        joined["ff"] = ff_ref
        refs = refs[2 * count - 1 :]
    (
        got_split,
        got_lat,
        got_emb,
        image,
        kernel_buf,
        time_buf,
        wide,
        act,
        stat_send,
        stat_got,
        edge_send,
        edge_got,
        side_sems,
        core_sems,
        load_sems,
        ring_sems,
        pair_sems,
        own_sems,
    ) = refs
    ring = Ring(chips, ring_sems, pair_sems, own_sems)
    index = lax.axis_index("dp")
    core, side = ring.core, ring.plane
    neighbour = (index, 1 - side)
    partner = (ring.partner, side)
    barrier = pltpu.get_barrier_semaphore()
    others = [partner, neighbour]
    if gathers:
        others += [(ring.right, side), (ring.left, side)]
    for where in others:
        pl.semaphore_signal(barrier, inc=1, device_id=where, device_id_type=MESH)
    pl.semaphore_wait(barrier, len(others))

    side_copies = {}
    for slot, name in enumerate(CONV_SHARDS if gathers else ()):
        side_copies[name] = remote(shard[name], got[name], neighbour, side_sems, slot)
    split_copy = remote(split_ref, got_split, neighbour, side_sems, count)
    if gathers:
        side_copies["one"].start()
    lat_copy = remote(lat_ref, got_lat, partner, core_sems, 0)
    emb_copy = remote(emb_ref, got_emb, partner, core_sems, 1)
    lat_copy.start()
    emb_copy.start()
    split_copy.start()
    for name in list(side_copies)[1:]:
        side_copies[name].start()

    def join(name):
        side_copies[name].wait_recv()
        mine, theirs, out = shard[name], got[name], joined[name]
        for lead in range(mine.shape[0]):

            @pl.when(side == 0)
            def _():
                out[lead] = jnp.concatenate([mine[lead], theirs[lead]], axis=1)

            @pl.when(side == 1)
            def _():
                out[lead] = jnp.concatenate([theirs[lead], mine[lead]], axis=1)

    def piece(name, start, size):
        rows = shard[name].shape[1]

        def target(owner):
            at = pl.multiple_of(owner * rows, 8)
            return full[name].at[start : start + size, pl.ds(at, rows), :]

        return ring.add(joined[name].at[start : start + size], target)

    groups = []
    if gathers:
        groups = [
            [piece("one", 3 * u, 3) for u in range(3)],
            [piece("time", 0, 1)] + [piece("two", 3 * u, 3) for u in range(3)],
            [piece("q", 0, 1), piece("kv", 0, 2), piece("so", 0, 1)],
            [piece("cq", 0, 1), piece("ckv", 0, 2), piece("co", 0, 1)],
        ]
    events = []
    for number, group in enumerate(groups):
        for step in range(1, ring.half + 1):
            for which in group:
                for way in (0, 1):
                    if step <= ring.last(which)[way]:
                        events.append((number, which, way, step))
    spot = [0]

    def poll(limit):
        for number, which, way, step in events[spot[0] : spot[0] + limit]:
            ring.event(which, way, step)
            spot[0] += 1
            later = [e for e in events[spot[0] :] if e[0] == number and e[3] < ring.last(e[1])[e[2]]]
            if not later and number + 1 < len(groups) and number + 1 not in begun:
                begun.add(number + 1)
                for other in groups[number + 1]:
                    ring.begin(other)

    begun = {0}

    def poll_group(number):
        poll(len([e for e in events[spot[0] :] if e[0] <= number]))

    lat_copy.wait_recv()

    @pl.when(core == side)
    def _():
        image[...] = lat_ref[...]

    @pl.when(core != side)
    def _():
        image[...] = got_lat[...]

    if gathers:
        join("one")
        for which in groups[0]:
            ring.begin(which)
    share = image.shape[0] // 2
    rows = share // SIDE
    mine = pl.ds(pl.multiple_of(core * share, share), share)
    pixels = image[...].astype(F32)
    mean_one = group_mean(col_mean(pixels))
    centred = pixels - mean_one
    inv_one = lax.rsqrt(group_mean(col_mean(centred * centred)) + NORM_EPS)
    slope = inv_one * (1.0 + vec_ref[0:1, :])

    def first_act(values):
        pre = (values.astype(F32) - mean_one) * slope + vec_ref[1:2, :]
        return pre * jax.nn.sigmoid(pre)

    img_ref[...] = image[mine, :]
    act[SIDE : SIDE + share, :] = first_act(image[mine, :])
    border = first_act(image[pl.ds(pl.multiple_of(share - SIDE * core, SIDE), SIDE), :])
    top = (core == 1).astype(F32)
    act[:SIDE, :] = border * top
    act[SIDE + share :, :] = border * (1.0 - top)
    side_by_side(wide, act[...], (0, 1, 2))
    for name in list(side_copies)[1:]:
        join(name)
    split_copy.wait_recv()

    @pl.when(side == 0)
    def _():
        split_out[0:4, :] = jnp.concatenate([split_ref[...], got_split[...]], axis=1)

    @pl.when(side == 1)
    def _():
        split_out[0:4, :] = jnp.concatenate([got_split[...], split_ref[...]], axis=1)

    split_out[4:8, :] = jnp.zeros((4, D), F32)
    emb_copy.wait_recv()
    poll_group(0)
    loads = []
    for u in range(3):
        if gathers:
            ring.arrived(groups[0][u])
        load = pltpu.make_async_copy(
            full["one"].at[3 * u : 3 * u + 3], kernel_buf.at[3 * u : 3 * u + 3], load_sems.at[u]
        )
        load.start()
        loads.append(load)
    for u in range(3):
        loads[u].wait()
        term = dot_nn(
            wide[u * SIDE : u * SIDE + share, :],
            kernel_buf[3 * u : 3 * u + 3].reshape(3 * D, D),
        )
        if u == 0:
            h1_ref[...] = term
        else:
            h1_ref[...] += term
        poll(2)
    if gathers:
        while any(e[1] == groups[1][0] for e in events[spot[0] :]):
            poll(1)
        ring.arrived(groups[1][0])
    time_load = pltpu.make_async_copy(full["time"].at[0], time_buf, load_sems.at[3])
    time_load.start()
    time_load.wait()
    home = (core == side).astype(F32)
    embed = emb_ref[...] * home + got_emb[...] * (1.0 - home)
    embed = (embed * jax.nn.sigmoid(embed)).astype(BF)
    shift = dot_nn(jnp.broadcast_to(embed, (8, embed.shape[1])), time_buf[...])[0:1, :]
    inner = h1_ref[...] + (split_out[0:1, :] + (shift + split_out[1:2, :]))
    h1_ref[...] = inner
    local_mean = group_mean(col_mean(inner))
    local_dev = inner - local_mean
    local_var = group_mean(col_mean(local_dev * local_dev))
    stat_send[0:1, :] = local_mean
    stat_send[1:2, :] = local_var
    stat_copy = remote(stat_send, stat_got, partner, core_sems, 2)
    stat_copy.start()
    stat_copy.wait()
    other_mean, other_var = stat_got[0:1, :], stat_got[1:2, :]
    mean_two = 0.5 * (local_mean + other_mean)
    gap = 0.5 * (local_mean - other_mean)
    inv_two = lax.rsqrt(0.5 * (local_var + other_var) + gap * gap + NORM_EPS)
    stat_ref[0:1, :] = mean_one
    stat_ref[1:2, :] = inv_one
    stat_ref[2:3, :] = mean_two
    stat_ref[3:4, :] = inv_two
    stat_ref[4:8, :] = jnp.zeros((4, D), F32)
    pre = (h1_ref[...] - mean_two) * (inv_two * (1.0 + split_out[2:3, :])) + split_out[3:4, :]
    act[SIDE : SIDE + share, :] = pre * jax.nn.sigmoid(pre)
    swap_edges(act, edge_send, edge_got, core, partner, core_sems, 3)
    side_by_side(wide, act[...], (0, 1, 2))
    poll_group(1)
    loads = []
    for u in range(3):
        if gathers:
            ring.arrived(groups[1][1 + u])
        load = pltpu.make_async_copy(
            full["two"].at[3 * u : 3 * u + 3], kernel_buf.at[3 * u : 3 * u + 3], load_sems.at[u]
        )
        load.start()
        loads.append(load)
    for u in range(3):
        loads[u].wait()
        term = None
        for w in range(3):
            part = dot_nt(
                wide[u * SIDE : u * SIDE + share, w * D : (w + 1) * D], kernel_buf[3 * u + w]
            )
            term = part if term is None else term + part
        if u == 0:
            h_ref[...] = term
        else:
            h_ref[...] += term
        poll(2)
    h_ref[...] = img_ref[...].astype(F32) + (h_ref[...] + vec_ref[2:3, :])
    poll_group(len(groups) - 1)
    for group in groups[2:]:
        for which in group:
            ring.arrived(which)
    for group in groups:
        for which in group:
            ring.drain(which)
    for copy in list(side_copies.values()) + [split_copy, lat_copy, emb_copy]:
        copy.wait_send()


def swap_edges(act, edge_send, edge_got, core, partner, sems, slot):
    share = act.shape[0] - 2 * SIDE
    start = pl.multiple_of(share - (share - SIDE) * core, SIDE)
    edge_send[...] = act[pl.ds(start, SIDE), :].astype(BF)
    copy = remote(edge_send, edge_got, partner, sems, slot)
    copy.start()
    copy.wait()
    border = edge_got[...].astype(F32)
    top = (core == 1).astype(F32)
    act[:SIDE, :] = border * top
    act[SIDE + share :, :] = border * (1.0 - top)


def conv_block(lat, emb, split, vectors, shards, chips, gathers):
    length = lat.shape[0]
    share = length // 2
    count = len(CONV_SHARDS)
    names = CONV_SHARDS[:-1]
    by_name = dict(zip(CONV_SHARDS, shards))

    def wide_shape(name):
        lead, rows, cols = by_name[name].shape
        return (lead, rows, 2 * cols)

    def full_shape(name):
        lead, rows, cols = by_name[name].shape
        return (lead, rows * chips * 2, 2 * cols) if gathers else (lead, rows, cols)

    pieces = 13 if gathers else 1
    dma = pltpu.SemaphoreType.DMA
    outs = [
        jax.ShapeDtypeStruct((share, D), F32),
        jax.ShapeDtypeStruct((share, D), F32),
        jax.ShapeDtypeStruct((share, D), BF),
        jax.ShapeDtypeStruct((8, D), F32),
        jax.ShapeDtypeStruct((8, D), F32),
    ]
    anywhere = pl.BlockSpec(memory_space=pl.ANY)
    if gathers:
        in_specs = [WHOLE] * (4 + count)
        out_specs = [WHOLE] * 6 + [anywhere] * (count - 1)
        outs.append(jax.ShapeDtypeStruct(wide_shape("ff"), BF))
        outs += [jax.ShapeDtypeStruct(full_shape(n), BF) for n in names]
        buffers = [pltpu.VMEM(s.shape, BF) for s in shards]
        buffers += [pltpu.VMEM(wide_shape(n), BF) for n in names]
    else:
        shards = shards[:-1]
        in_specs = [WHOLE] * 4 + [anywhere] * (count - 1)
        out_specs = [WHOLE] * 5
        buffers = []
    return pl.pallas_call(
        functools.partial(conv_kernel, chips, gathers),
        out_shape=outs,
        in_specs=in_specs,
        out_specs=out_specs,
        scratch_shapes=buffers
        + [
            pltpu.VMEM(split.shape, F32),
            pltpu.VMEM(lat.shape, BF),
            pltpu.VMEM(emb.shape, F32),
            pltpu.VMEM(lat.shape, BF),
            pltpu.VMEM((9, D, D), BF),
            pltpu.VMEM(full_shape("time")[1:], BF),
            pltpu.VMEM((share + 2 * SIDE, 3 * D), BF),
            pltpu.VMEM((share + 2 * SIDE, D), F32),
            pltpu.VMEM((8, D), F32),
            pltpu.VMEM((8, D), F32),
            pltpu.VMEM((SIDE, D), BF),
            pltpu.VMEM((SIDE, D), BF),
            dma((2, count + 1)),
            dma((2, 4)),
            dma((4,)),
            dma((2, 2, pieces, chips // 2)),
            dma((2, pieces, chips)),
            dma((pieces,)),
        ],
        compiler_params=pltpu.CompilerParams(
            collective_id=1, has_side_effects=True, vmem_limit_bytes=VMEM_BYTES
        ),
        name="conv_block",
    )(lat, emb, split, vectors, *shards)


class Halving:
    def __init__(self, steps, acc, got, out, sems):
        self.acc, self.got, self.out, self.sems, self.steps = acc, got, out, sems, steps
        index = lax.axis_index("dp")
        plane = lax.axis_index("mp")
        core = lax.rem(index, 2)
        chip = index // 2
        self.partners = [((index + 1 - 2 * core, plane), core), ((index, 1 - plane), plane)]
        span = 1
        for _ in range(steps - 2):
            bit = lax.rem(chip // span, 2)
            self.partners.append((((chip + span - 2 * span * bit) * 2 + core, plane), bit))
            span *= 2
        self.offset, self.size, self.base = 0, acc.shape[0], 0
        self.trail = []
        self.flight = None
        self.done = 0

    def begin(self):
        self._down(0)

    def _down(self, step):
        where, bit = self.partners[step]
        size = self.size // 2
        mine = pl.multiple_of(self.offset + bit * size, 8)
        theirs = pl.multiple_of(self.offset + (1 - bit) * size, 8)
        copy = remote(
            self.acc.at[pl.ds(theirs, size), :],
            self.got.at[pl.ds(self.base, size), :],
            where,
            self.sems,
            step,
        )
        copy.start()
        self.flight = (copy, mine, size)

    def _up(self, step):
        mine, size, where = self.trail[step]
        part = self.out.at[pl.ds(mine, size), :]
        copy = remote(part, part, where, self.sems, self.steps + step)
        copy.start()
        self.flight = (copy, mine, size)

    def step(self):
        steps = self.steps
        if self.done >= 2 * steps:
            return
        copy, mine, size = self.flight
        copy.wait()
        if self.done < steps:
            self.acc[pl.ds(mine, size), :] += self.got[pl.ds(self.base, size), :]
            self.trail.append((mine, size, self.partners[self.done][0]))
            self.offset, self.size = mine, size
            self.base += size
            if self.done + 1 < steps:
                self._down(self.done + 1)
            else:
                self.out[pl.ds(mine, size), :] = self.acc[pl.ds(mine, size), :]
                self._up(steps - 1)
        elif self.done + 1 < 2 * steps:
            self._up(2 * steps - 2 - self.done)
        self.done += 1


def conv_back_kernel(
    steps,
    g0_ref,
    h1_ref,
    img_ref,
    stat_ref,
    split_ref,
    vec_ref,
    flat_ref,
    one_ref,
    two_ref,
    grad_ref,
    sum_ref,
    one_buf,
    two_buf,
    wide,
    act,
    half_back,
    stat_send,
    stat_got,
    edge_send,
    edge_got,
    acc,
    got,
    load_sems,
    core_sems,
    sum_sems,
    back_sems,
):
    index = lax.axis_index("dp")
    side = lax.axis_index("mp")
    core = lax.rem(index, 2)
    partner = (index + 1 - 2 * core, side)
    neighbour = (index, 1 - side)
    diagonal = (index + 1 - 2 * core, 1 - side)
    share = g0_ref.shape[0]
    loads = []
    for slot, (src, dst) in enumerate(((two_ref, two_buf), (one_ref, one_buf))):
        load = pltpu.make_async_copy(src, dst, load_sems.at[slot])
        load.start()
        loads.append(load)
    total = Halving(steps, acc, got, sum_ref, sum_sems)
    barrier = pltpu.get_barrier_semaphore()
    for where, _ in total.partners:
        pl.semaphore_signal(barrier, inc=1, device_id=where, device_id_type=MESH)
    pl.semaphore_signal(barrier, inc=1, device_id=diagonal, device_id_type=MESH)
    acc[...] = flat_ref[...]
    act[SIDE : SIDE + share, :] = g0_ref[...]
    pl.semaphore_wait(barrier, steps + 1)
    total.begin()
    swap_edges(act, edge_send, edge_got, core, partner, core_sems, 0)
    side_by_side(wide, act[...], (2, 1, 0))
    total.step()
    inner = act.at[SIDE : SIDE + share, :]
    loads[0].wait()
    for u in range(3):
        term = dot_nn(
            wide[u * SIDE : u * SIDE + share, :],
            two_buf[3 * (2 - u) : 3 * (2 - u) + 3].reshape(3 * D, D),
        )
        if u == 0:
            inner[...] = term
        else:
            inner[...] += term
        total.step()
    mean_two, inv_two = stat_ref[2:3, :], stat_ref[3:4, :]
    gain_two = 1.0 + split_ref[2:3, :]
    normal = (h1_ref[...] - mean_two) * inv_two
    scaled = inner[...] * silu_slope(normal * gain_two + split_ref[3:4, :]) * gain_two
    means = pair_means(scaled, normal, stat_send, stat_got, partner, core_sems, 1)
    inner[...] = inv_two * (scaled - means[0] - normal * means[1])
    swap_edges(act, edge_send, edge_got, core, partner, core_sems, 2)
    side_by_side(wide, act[...], (2, 1, 0))
    total.step()
    loads[1].wait()
    for u in range(3):
        term = None
        for spot in range(3):
            part = dot_nt(
                wide[u * SIDE : u * SIDE + share, spot * D : (spot + 1) * D],
                one_buf[3 * (2 - u) + spot],
            )
            term = part if term is None else term + part
        if u == 0:
            inner[...] = term
        else:
            inner[...] += term
        total.step()
    mean_one, inv_one = stat_ref[0:1, :], stat_ref[1:2, :]
    gain_one = 1.0 + vec_ref[0:1, :]
    normal = (img_ref[...].astype(F32) - mean_one) * inv_one
    scaled = inner[...] * silu_slope(normal * gain_one + vec_ref[1:2, :]) * gain_one
    means = pair_means(scaled, normal, stat_send, stat_got, partner, core_sems, 3)
    half_back[...] = (
        g0_ref[...] + inv_one * (scaled - means[0] - normal * means[1])
    ).astype(BF)
    mine = grad_ref.at[pl.ds(pl.multiple_of(core * share, share), share), :]
    home = core == side

    @pl.when(home)
    def _():
        remote(half_back, mine, neighbour, back_sems, core).start()
        pltpu.make_async_copy(half_back, mine, load_sems.at[2]).start()

    @pl.when(jnp.logical_not(home))
    def _():
        remote(half_back, mine, diagonal, back_sems, core).start()
        remote(half_back, mine, partner, back_sems, 2 + core).start()

    for _ in range(2 * steps):
        total.step()

    def part(which):
        return grad_ref.at[pl.ds(pl.multiple_of(which * share, share), share), :]

    @pl.when(home)
    def _():
        remote(half_back, mine, neighbour, back_sems, core).wait_send()
        pltpu.make_async_copy(half_back, mine, load_sems.at[2]).wait()
        remote(half_back, part(1 - core), partner, back_sems, 3 - core).wait_recv()

    @pl.when(jnp.logical_not(home))
    def _():
        remote(half_back, mine, diagonal, back_sems, core).wait_send()
        remote(half_back, mine, partner, back_sems, 2 + core).wait_send()
        remote(half_back, part(core), neighbour, back_sems, core).wait_recv()
        remote(half_back, part(1 - core), diagonal, back_sems, 1 - core).wait_recv()


def pair_means(scaled, normal, stat_send, stat_got, partner, sems, slot):
    stat_send[0:1, :] = group_mean(col_mean(scaled))
    stat_send[1:2, :] = group_mean(col_mean(scaled * normal))
    copy = remote(stat_send, stat_got, partner, sems, slot)
    copy.start()
    copy.wait()
    both = 0.5 * (stat_send[...] + stat_got[...])
    return both[0:1, :], both[1:2, :]


def conv_back(g0, h1, img, stats, split, vectors, flat, one, two, devices):
    share = g0.shape[0]
    steps = devices.bit_length() - 1
    dma = pltpu.SemaphoreType.DMA
    return pl.pallas_call(
        functools.partial(conv_back_kernel, steps),
        out_shape=[
            jax.ShapeDtypeStruct((2 * share, D), BF),
            jax.ShapeDtypeStruct(flat.shape, F32),
        ],
        in_specs=[WHOLE] * 7 + [pl.BlockSpec(memory_space=pl.ANY)] * 2,
        out_specs=[WHOLE] * 2,
        scratch_shapes=[
            pltpu.VMEM((9, D, D), BF),
            pltpu.VMEM((9, D, D), BF),
            pltpu.VMEM((share + 2 * SIDE, 3 * D), BF),
            pltpu.VMEM((share + 2 * SIDE, D), F32),
            pltpu.VMEM((share, D), BF),
            pltpu.VMEM((8, D), F32),
            pltpu.VMEM((8, D), F32),
            pltpu.VMEM((SIDE, D), BF),
            pltpu.VMEM((SIDE, D), BF),
            pltpu.VMEM(flat.shape, F32),
            pltpu.VMEM(flat.shape, F32),
            dma((3,)),
            dma((2, 4)),
            dma((2, 2 * steps)),
            dma((2, 4)),
        ],
        compiler_params=pltpu.CompilerParams(
            collective_id=5, has_side_effects=True, vmem_limit_bytes=VMEM_BYTES
        ),
        name="conv_back",
    )(g0, h1, img, stats, split, vectors, flat, one, two)


def shards(
    latents,
    out_grad,
    text_states,
    time_embed,
    group_ids,
    group_weights,
    timesteps,
    step_weights,
    vectors,
    split_vectors,
    up_bias,
    conv_one,
    conv_two,
    time_proj,
    self_query,
    self_kv,
    self_out,
    cross_query,
    cross_kv,
    cross_out,
    ff_up,
    ff_down,
    query_left_state,
    query_right_state,
    up_left_state,
    up_right_state,
):
    devices_dp = lax.axis_size("dp")
    chips = devices_dp // 2
    index = lax.axis_index("dp")
    side = lax.axis_index("mp")
    core = lax.rem(index, 2)
    home = core == side
    core_pairs = [(i, i ^ 1) for i in range(devices_dp)]
    cross_pairs = [
        (i * 2 + j, (i ^ 1) * 2 + (j ^ 1))
        for i in range(devices_dp)
        for j in range(2)
        if i % 2 != j
    ]

    def core_swap(values):
        return lax.ppermute(values, "dp", core_pairs)

    def side_swap(values):
        return lax.ppermute(values, "mp", [(0, 1), (1, 0)])

    def cross_swap(values):
        return lax.ppermute(values, ("dp", "mp"), cross_pairs)

    def join_sides(values):
        other = side_swap(values)
        first = jnp.where(side == 0, values, other)
        second = jnp.where(side == 0, other, values)
        return jnp.concatenate([first, second], axis=-1)

    def pick(values):
        return jnp.where(home, values, core_swap(values))

    pieces = [
        conv_one,
        time_proj[None],
        conv_two.transpose(0, 2, 1),
        self_query[None],
        self_kv.transpose(1, 0, 2),
        self_out.T[None],
        cross_query[None],
        cross_kv.transpose(1, 0, 2),
        cross_out.T[None],
        jnp.concatenate([ff_up.transpose(1, 0, 2), ff_down.T[None]], axis=0),
    ]
    gathers = all(piece.shape[1] % 8 == 0 for piece in pieces)
    if not gathers:
        pieces = [lax.all_gather(join_sides(p), "dp", axis=1, tiled=True) for p in pieces]
    hidden_one, inner, img, stats, split_all, *full = conv_block(
        latents[0], time_embed, split_vectors, vectors, pieces, chips, gathers
    )
    if gathers:
        ff_block, *full = full
    else:
        ff_block, full = jnp.zeros((3, 8, LANES), BF), pieces[:-1]
    w_one, w_time, w_two_t, w_q, w_kv, w_so_t, w_cq, w_ckv, w_co_t = full
    w_q, w_so_t, w_cq, w_co_t = w_q[0], w_so_t[0], w_cq[0], w_co_t[0]

    bias_all = join_sides(up_bias)
    qr_all = join_sides(query_right_state[0])
    ur_all = join_sides(up_right_state[0])
    query_left = query_left_state[0]
    up_left = up_left_state[0]
    q_pair_left = pair_left(query_left).astype(BF)
    q_pair_right = pair_right(qr_all).astype(BF)
    u_pair_left = pair_left(up_left).astype(BF)
    u_pair_right = pair_right(ur_all).astype(BF).transpose(1, 0, 2)

    step_hot = timesteps[:, None] == jnp.arange(step_weights.shape[0], dtype=jnp.int32)[None, :]
    chosen = jnp.sum(jnp.where(step_hot, step_weights[None, :], 0.0), axis=1)
    group_hot = group_ids[:, None] == jnp.arange(2, dtype=jnp.int32)[None, :]
    picked = jnp.sum(jnp.where(group_hot, group_weights[None, :], 0.0), axis=1)
    scale = pick((chosen * picked)[:, None])[0, 0]
    context = pick(text_states)[0]
    image_grad = jnp.where(home, out_grad, cross_swap(out_grad))[0]

    text = jnp.pad(context, ((0, LANES - context.shape[0]), (0, 0)))
    hidden_two, hidden_three, q, kv, o, lse, cq, ckv, ff_full = attention(
        hidden_one,
        vectors,
        w_q,
        q_pair_left,
        q_pair_right,
        w_kv,
        w_so_t,
        w_cq,
        w_ckv,
        w_co_t,
        text,
        ff_block,
        chips,
        gathers,
    )
    if not gathers:
        ff_full = pieces[-1]
    image_out, cotangent, u_outer, u_inner = feed_forward(
        hidden_three,
        image_grad,
        scale[None, None],
        vectors,
        ff_full,
        bias_all,
        u_pair_left,
        u_pair_right,
    )
    block_out = jnp.where(home, image_out, cross_swap(image_out))[None]
    cotangent, q_outer, q_inner = attention_back(
        cotangent,
        hidden_one,
        hidden_two,
        vectors,
        w_q,
        q_pair_left,
        q_pair_right,
        w_kv,
        w_so_t,
        w_cq,
        w_co_t,
        q,
        kv,
        o,
        lse,
        cq,
        ckv,
    )

    grad_query_left = left_grads(q_inner, query_left)
    grad_query_right = right_grads(q_outer, qr_all)
    grad_up_left = left_grads(u_inner, up_left)
    grad_up_right = right_grads(u_outer.transpose(1, 0, 2), ur_all)
    parts = [grad_query_left, grad_up_left, grad_query_right, grad_up_right]
    flat = jnp.concatenate([v.reshape(-1, LANES) for v in parts], axis=0)
    unit = 8 * devices_dp * 2
    flat = jnp.pad(flat, ((0, -flat.shape[0] % unit), (0, 0)))
    latents_grad, total = conv_back(
        cotangent, inner, img, stats, split_all, vectors, flat, w_one, w_two_t, devices_dp * 2
    )
    latents_grad = latents_grad[None]
    grads, start = [], 0
    for v in parts:
        grads.append(total[start : start + v.size // LANES].reshape(v.shape))
        start += v.size // LANES
    grad_query_left, grad_up_left, grad_query_right, grad_up_right = grads

    def my_side(values):
        size = values.shape[-1] // 2
        return lax.dynamic_slice_in_dim(values, side * size, size, values.ndim - 1)

    grad_query_right = my_side(grad_query_right)
    grad_up_right = my_side(grad_up_right)
    left_weight, left_moment, left_second, left_average = adamw_parts(
        query_left_state, grad_query_left
    )
    right_weight, right_moment, right_second, right_average = adamw_parts(
        query_right_state, grad_query_right
    )
    query_left_new = jnp.stack([left_weight, left_average])
    query_left_copy = left_weight.astype(BF)
    query_right_new = jnp.stack([right_weight, right_average])
    query_right_copy = right_weight.astype(BF)
    left_pair = my_side(jnp.stack([left_moment, left_second]).transpose(0, 1, 3, 2))
    right_pair = jnp.stack([right_moment, right_second])
    query_moments = jnp.stack([left_pair, right_pair])
    up_left_new, up_left_copy = adamw(up_left_state, grad_up_left)
    up_right_new, up_right_copy = adamw(up_right_state, grad_up_right)
    return (
        block_out,
        latents_grad,
        query_left_new,
        query_left_copy,
        query_right_new,
        query_right_copy,
        up_left_new,
        up_left_copy,
        up_right_new,
        up_right_copy,
        query_moments,
    )


def solution(mesh):
    placed = (
        P("dp", None, None),
        P("dp", "mp", None),
        P("dp", None, None),
        P("dp", None),
        P("dp"),
        P(),
        P("dp"),
        P(),
        P(),
        P(None, "mp"),
        P(None, "mp"),
        P(None, "dp", "mp"),
        P(None, "mp", "dp"),
        P("dp", "mp"),
        P("dp", "mp"),
        P("dp", None, "mp"),
        P("mp", "dp"),
        P("dp", "mp"),
        P("dp", None, "mp"),
        P("mp", "dp"),
        P("dp", None, "mp"),
        P("mp", "dp"),
        P(),
        P(None, None, None, "mp"),
        P(),
        P(None, None, None, None, "mp"),
    )
    return jax.shard_map(
        shards,
        mesh=mesh,
        in_specs=placed,
        out_specs=(
            P("dp", "mp", None),
            P("dp", None, None),
            P(),
            P(),
            P(None, None, None, "mp"),
            P(None, None, "mp"),
            P(),
            P(),
            P(None, None, None, None, "mp"),
            P(None, None, None, "mp"),
            P(None, None, None, None, "mp"),
        ),
        check_vma=False,
    )
```

```python
import functools
import types

import jax
import jax.numpy as jnp
from jax import lax
from jax.experimental import pallas as pl
from jax.experimental.pallas import tpu as pltpu
from jax.sharding import PartitionSpec as P

D = 640
HEAD_DIM = 80
GROUPS = 32
SIDE = 32
ADAM_STEP = 10
LANES = 128

NORM_EPS = 1e-05
BETA_ONE = 0.9
BETA_TWO = 0.999
ADAM_EPS = 1e-08
DECAY_RATE = 0.01
LEARN_RATE = 0.06
EMA_KEEP = 0.995
INV_ROOT_TWO = 0.7071067811865476
INV_ROOT_TWOPI = 0.3989422804014327

MESH = pl.DeviceIdType.MESH
BF = jnp.bfloat16
F32 = jnp.float32


def adamw_parts(state, grads):
    weight, moment, second, average = (state[0], state[1], state[2], state[3])
    moment = BETA_ONE * moment + (1.0 - BETA_ONE) * grads
    second = BETA_TWO * second + (1.0 - BETA_TWO) * grads * grads
    moment_hat = moment / (1.0 - BETA_ONE**ADAM_STEP)
    second_hat = second / (1.0 - BETA_TWO**ADAM_STEP)
    weight = weight - LEARN_RATE * (
        moment_hat / (jnp.sqrt(second_hat) + ADAM_EPS) + DECAY_RATE * weight
    )
    average = EMA_KEEP * average + (1.0 - EMA_KEEP) * weight
    return (weight, moment, second, average)


def adamw(state, grads):
    weight, moment, second, average = adamw_parts(state, grads)
    return (jnp.stack([weight, moment, second, average]), weight.astype(BF))


def dot_nn(left, right):
    return jnp.dot(left, right, preferred_element_type=F32)


def dot_nt(left, right):
    return lax.dot_general(left, right, (((1,), (1,)), ((), ())), preferred_element_type=F32)


def dot_tn(left, right):
    return lax.dot_general(left, right, (((0,), (0,)), ((), ())), preferred_element_type=F32)


def silu_slope(values):
    sigma = jax.nn.sigmoid(values)
    return sigma * (1.0 + values * (1.0 - sigma))


def layer_norm(values, gain, bias):
    centred = values - jnp.mean(values, axis=1, keepdims=True)
    inv_std = lax.rsqrt(jnp.mean(centred * centred, axis=1, keepdims=True) + NORM_EPS)
    normal = centred * inv_std
    return (normal * gain + bias, normal, inv_std)


def layer_back(grads, normal, inv_std, gain):
    scaled = grads * gain
    return inv_std * (
        scaled
        - jnp.mean(scaled, axis=1, keepdims=True)
        - normal * jnp.mean(scaled * normal, axis=1, keepdims=True)
    )


def ring_chip(place, chips):
    place = lax.rem(place + 2 * chips, chips)
    return jnp.where(place < chips // 2, 2 * place, 2 * (chips - 1 - place) + 1)


def ring_place(chip, chips):
    column = chip // 2
    return jnp.where(lax.rem(chip, 2) == 0, column, chips - 1 - column)


WHOLE = pl.BlockSpec(memory_space=pltpu.VMEM)
VMEM_BYTES = 63 * 1024 * 1024
FACTOR = HEAD_DIM**-0.5
LOG_TWO_E = 1.4426950408889634
HEADS = D // HEAD_DIM
RANK_SQ = 64


def split_low(values):
    high = values.astype(BF)
    return high, (values - high.astype(F32)).astype(BF)


def to_heads(slots, values):
    blank = jnp.zeros((values.shape[0], LANES - HEAD_DIM), BF)
    for head in range(HEADS):
        part = values[:, HEAD_DIM * head : HEAD_DIM * (head + 1)]
        slots[head] = jnp.concatenate([part, blank], axis=1)


def from_heads(slots):
    return jnp.concatenate([slots[head][:, :HEAD_DIM] for head in range(HEADS)], axis=1)


def ff_kernel(
    h3_ref,
    cot_ref,
    scale_ref,
    vec_ref,
    weights_ref,
    bias_ref,
    left_ref,
    right_ref,
    rows_ref,
    cols_ref,
    out_ref,
    g2_ref,
    right_out,
    left_out,
    act,
    cot_low,
    wide,
    down_acc,
    back_acc,
):
    tile = pl.program_id(0)
    down_ref = weights_ref.at[2]
    cols = down_ref.shape[1]
    gain = 1.0 + vec_ref[7:8, :]

    @pl.when(tile == 0)
    def _():
        norm, _, _ = layer_norm(h3_ref[...], gain, vec_ref[8:9, :])
        low = norm.astype(BF)
        act[:, :D] = low
        act[:, D:] = dot_nn(low, left_ref[...]).astype(BF)
        cot_low[...] = (cot_ref[...].astype(F32) * scale_ref[0:1, 0:1]).astype(BF)

    for part in range(2):
        wide[:D, part * cols : (part + 1) * cols] = weights_ref[part]
        wide[D:, part * cols : (part + 1) * cols] = right_ref[part]
    mixed = dot_nn(act[...], wide[...])
    value = mixed[:, :cols] + bias_ref[0:1, :]
    gate = mixed[:, cols:] + bias_ref[1:2, :]
    cdf = 0.5 * (1.0 + lax.erf(gate * INV_ROOT_TWO))
    gelu = gate * cdf
    hidden = (value * gelu).astype(BF)
    down = dot_nt(hidden, down_ref[...])
    hidden_grad = dot_nn(cot_low[...], down_ref[...])
    slope = cdf + gate * jnp.exp(-0.5 * gate * gate) * INV_ROOT_TWOPI
    grads = jnp.concatenate(
        [(hidden_grad * gelu).astype(BF), (hidden_grad * value * slope).astype(BF)], axis=1
    )
    outer = dot_tn(act[:, D:], grads)
    for part in range(2):
        base = 16 * part
        one, two = factor_rows(
            outer[:, part * cols : (part + 1) * cols],
            rows_ref[base : base + 8, :],
            rows_ref[base + 8 : base + 16, :],
        )
        right_out[0, part] = one
        right_out[1, part] = two
    back = dot_nt(grads, wide[...])

    @pl.when(tile == 0)
    def _():
        down_acc[...] = down
        back_acc[...] = back

    @pl.when(tile > 0)
    def _():
        down_acc[...] += down
        back_acc[...] += back

    @pl.when(tile == pl.num_programs(0) - 1)
    def _():
        out_ref[...] = (h3_ref[...] + (down_acc[...] + vec_ref[11:12, :])).astype(BF)
        low_rank = back_acc[:, D:].astype(BF)
        one, two = factor_rows(
            dot_tn(low_rank, act[:, :D]), cols_ref[0:8, :], cols_ref[8:16, :]
        )
        left_out[0] = one
        left_out[1] = two
        normed_grad = back_acc[:, :D] + dot_nt(low_rank, left_ref[...])
        _, normal, inv = layer_norm(h3_ref[...], gain, vec_ref[8:9, :])
        cot = cot_ref[...].astype(F32) * scale_ref[0:1, 0:1]
        g2_ref[...] = cot + layer_back(normed_grad, normal, inv, gain)


def feed_forward(h3, cot, scale, vectors, weights, bias, left, right, rows, columns):
    share = h3.shape[0]
    hidden = weights.shape[2]
    cols = 256
    return pl.pallas_call(
        ff_kernel,
        grid=(hidden // cols,),
        out_shape=[
            jax.ShapeDtypeStruct((share, D), BF),
            jax.ShapeDtypeStruct((share, D), F32),
            jax.ShapeDtypeStruct((2, 2, 8, hidden), F32),
            jax.ShapeDtypeStruct((2, 8, D), F32),
        ],
        in_specs=[
            WHOLE,
            WHOLE,
            WHOLE,
            WHOLE,
            pl.BlockSpec((3, D, cols), lambda i: (0, 0, i)),
            pl.BlockSpec((2, cols), lambda i: (0, i)),
            WHOLE,
            pl.BlockSpec((2, RANK_SQ, cols), lambda i: (0, 0, i)),
            pl.BlockSpec((32, cols), lambda i: (0, i)),
            WHOLE,
        ],
        out_specs=[WHOLE, WHOLE, pl.BlockSpec((2, 2, 8, cols), lambda i: (0, 0, 0, i)), WHOLE],
        scratch_shapes=[
            pltpu.VMEM((share, D + RANK_SQ), BF),
            pltpu.VMEM((share, D), BF),
            pltpu.VMEM((D + RANK_SQ, 2 * cols), BF),
            pltpu.VMEM((share, D), F32),
            pltpu.VMEM((share, D + RANK_SQ), F32),
        ],
        compiler_params=pltpu.CompilerParams(vmem_limit_bytes=VMEM_BYTES),
        name="feed_forward",
    )(h3, cot, scale, vectors, weights, bias, left, right, rows, columns)


def partner_barrier():
    index = lax.axis_index("dp")
    where = (index + 1 - 2 * lax.rem(index, 2), lax.axis_index("mp"))
    barrier = pltpu.get_barrier_semaphore()
    pl.semaphore_signal(barrier, inc=1, device_id=where, device_id_type=MESH)
    return lax.rem(index, 2), where, barrier


def send_to(where, src, dst, sems, slot):
    return pltpu.make_async_remote_copy(
        src_ref=src,
        dst_ref=dst,
        send_sem=sems.at[0, slot],
        recv_sem=sems.at[1, slot],
        device_id=where,
        device_id_type=MESH,
    )


TEXT = 77


def cross_probs(query, keys):
    scores = dot_nt(query, keys)
    column = lax.broadcasted_iota(jnp.int32, scores.shape, 1)
    scores = jnp.where(column < TEXT, scores, -1e30)
    top = jnp.max(scores, axis=1, keepdims=True)
    expo = jnp.exp2((scores - top) * (FACTOR * LOG_TWO_E))
    return expo * (1.0 / jnp.sum(expo, axis=1, keepdims=True))


def attention_back_kernel(
    g2_ref,
    h_ref,
    h2_ref,
    vec_ref,
    wq_ref,
    left_ref,
    right_ref,
    wkv_ref,
    wso_ref,
    wcq_ref,
    wco_ref,
    q_ref,
    kv_ref,
    o_ref,
    lse_ref,
    cq_ref,
    ckv_ref,
    rows_ref,
    cols_ref,
    image_ref,
    g0_ref,
    right_out,
    left_out,
    block_ref,
    wide,
    dout,
    cot,
    delta,
    dq_acc,
    dkv_acc,
    give,
    take,
    sems,
):
    core, where, barrier = partner_barrier()
    side = where[1]
    share = h_ref.shape[0]
    diagonal = (where[0], 1 - side)
    pl.semaphore_signal(barrier, inc=1, device_id=diagonal, device_id_type=MESH)
    pl.semaphore_wait(barrier, 2)
    home = core == side
    out_copy = remote(image_ref, block_ref, diagonal, sems, 1)

    @pl.when(home)
    def _():
        block_ref[...] = image_ref[...]

    @pl.when(jnp.logical_not(home))
    def _():
        out_copy.start()

    dco = dot_nn(g2_ref[...].astype(BF), wco_ref[...]).astype(BF)
    to_heads(dout, dco)

    def cross_head(head, carry):
        probs = cross_probs(cq_ref[head], ckv_ref[0, head])
        dprobs = dot_nt(dout[head], ckv_ref[1, head])
        shift = jnp.sum(dprobs * probs, axis=1, keepdims=True)
        dscores = (probs * (dprobs - shift)).astype(BF)
        dout[head] = (dot_nn(dscores, ckv_ref[0, head]) * FACTOR).astype(BF)
        return carry

    lax.fori_loop(0, HEADS, cross_head, 0)
    gain = 1.0 + vec_ref[5:6, :]
    _, normal, inv = layer_norm(h2_ref[...], gain, vec_ref[6:7, :])
    cot[...] = g2_ref[...] + layer_back(
        dot_nt(from_heads(dout), wcq_ref[...]), normal, inv, gain
    )
    dso = dot_nn(cot[...].astype(BF), wso_ref[...]).astype(BF)
    to_heads(dout, dso)
    prod = dso.astype(F32) * o_ref[...].astype(F32)
    head_row = lax.broadcasted_iota(jnp.int32, (HEADS, D), 0)
    head_col = lax.broadcasted_iota(jnp.int32, (HEADS, D), 1)
    low_edge = head_row * HEAD_DIM
    mark = jnp.where((head_col >= low_edge) & (head_col < low_edge + HEAD_DIM), 1.0, 0.0).astype(BF)
    high, rest = split_low(prod)
    delta[...] = dot_nt(mark, high) + dot_nt(mark, rest)
    for turn in range(2):
        half = core if turn == 1 else 1 - core
        span = pl.ds(pl.multiple_of(half * share, share), share)

        def one_head(head, carry, turn=turn, span=span):
            keys = kv_ref[0, head, span, :]
            vals = kv_ref[1, head, span, :]
            query = q_ref[head]
            grad = dout[head]
            scores = dot_nt(keys, query)
            probs = jnp.exp2(scores * (FACTOR * LOG_TWO_E) - lse_ref[pl.ds(head, 1), :])
            dprobs = dot_nt(vals, grad)
            dscores = (probs * (dprobs - delta[pl.ds(head, 1), :])).astype(BF)
            dval = dot_nn(probs.astype(BF), grad)
            dkey = dot_nn(dscores, query) * FACTOR
            dquery = dot_tn(keys, dscores)
            if turn == 0:
                dq_acc[head] = dquery
                give[0, head] = dkey.astype(BF)
                give[1, head] = dval.astype(BF)
            else:
                dq_acc[head] += dquery
                dkv_acc[0, head] = dkey
                dkv_acc[1, head] = dval
            return carry

        lax.fori_loop(0, HEADS, one_head, 0)
        if turn == 0:
            copy = send_to(where, give, take, sems, 0)
            copy.start()
    for head in range(HEADS):
        dout[head] = (dq_acc[head].T * FACTOR).astype(BF)
    dq = from_heads(dout)
    gain = 1.0 + vec_ref[3:4, :]
    norm, normal, inv = layer_norm(h_ref[...], gain, vec_ref[4:5, :])
    low = norm.astype(BF)
    wide[:D, :] = wq_ref[...]
    wide[D:, :] = right_ref[...]
    back = dot_nt(dq, wide[...])
    low_rank = back[:, D:].astype(BF)
    outer = dot_tn(dot_nn(low, left_ref[...]).astype(BF), dq)
    one, two = factor_rows(outer, rows_ref[0:8, :], rows_ref[8:16, :])
    right_out[0] = one
    right_out[1] = two
    one, two = factor_rows(dot_tn(low_rank, low), cols_ref[0:8, :], cols_ref[8:16, :])
    left_out[0] = one
    left_out[1] = two
    total = back[:, :D] + dot_nt(low_rank, left_ref[...])
    copy.wait()
    for part in range(2):
        for head in range(HEADS):
            dout[head] = (dkv_acc[part, head] + take[part, head].astype(F32)).astype(BF)
        total += dot_nt(from_heads(dout), wkv_ref[part])
    g0_ref[...] = cot[...] + layer_back(total, normal, inv, gain)

    @pl.when(jnp.logical_not(home))
    def _():
        out_copy.wait()


def attention_back(*operands):
    share = operands[0].shape[0]
    return pl.pallas_call(
        attention_back_kernel,
        out_shape=[
            jax.ShapeDtypeStruct((share, D), F32),
            jax.ShapeDtypeStruct((2, 8, D), F32),
            jax.ShapeDtypeStruct((2, 8, D), F32),
            jax.ShapeDtypeStruct((share, D), BF),
        ],
        in_specs=[WHOLE] * 20,
        out_specs=[WHOLE] * 4,
        scratch_shapes=[
            pltpu.VMEM((D + RANK_SQ, D), BF),
            pltpu.VMEM((HEADS, share, LANES), BF),
            pltpu.VMEM((share, D), F32),
            pltpu.VMEM((HEADS, share), F32),
            pltpu.VMEM((HEADS, LANES, share), F32),
            pltpu.VMEM((2, HEADS, share, LANES), F32),
            pltpu.VMEM((2, HEADS, share, LANES), BF),
            pltpu.VMEM((2, HEADS, share, LANES), BF),
            pltpu.SemaphoreType.DMA((2, 2)),
        ],
        compiler_params=pltpu.CompilerParams(
            collective_id=4, has_side_effects=True, vmem_limit_bytes=VMEM_BYTES
        ),
        name="attention_back",
    )(*operands)


class Ring:
    def __init__(self, chips, ring_sems, core_sems, side_sems, own_sems):
        self.chips = chips
        self.half = chips // 2
        index = lax.axis_index("dp")
        self.plane = lax.axis_index("mp")
        self.core = lax.rem(index, 2)
        self.place = ring_place(index // 2, chips)
        self.right = ring_chip(self.place + 1, chips) * 2 + self.core
        self.left = ring_chip(self.place - 1, chips) * 2 + self.core
        self.index = index
        self.partner = index + 1 - 2 * self.core
        self.ring_sems, self.core_sems = ring_sems, core_sems
        self.side_sems, self.own_sems = side_sems, own_sems
        self.pieces = []

    def add(self, source, target, via=None, turn=0):
        self.pieces.append((source, target, via, turn))
        return len(self.pieces) - 1

    def last(self, which):
        turn = self.pieces[which][3]
        return (self.half - turn, self.half - 1 + turn)

    def spot(self, which, hop):
        return self.pieces[which][1](ring_chip(self.place - hop, self.chips) * 2 + self.core)

    def ring_copy(self, which, way, step):
        sign = 1 if way == 0 else -1
        spot = self.spot(which, sign * (step - 1))
        return pltpu.make_async_remote_copy(
            src_ref=self.pieces[which][0] if step == 1 else spot,
            dst_ref=spot,
            send_sem=self.ring_sems.at[0, way, which, step - 1],
            recv_sem=self.ring_sems.at[1, way, which, step - 1],
            device_id=(self.right if way == 0 else self.left, self.plane),
            device_id_type=MESH,
        )

    def core_copy(self, which, slot, hop):
        spot = self.spot(which, hop)
        return pltpu.make_async_remote_copy(
            src_ref=self.pieces[which][0] if slot == 0 else spot,
            dst_ref=spot,
            send_sem=self.core_sems.at[0, which, slot],
            recv_sem=self.core_sems.at[1, which, slot],
            device_id=(self.partner, self.plane),
            device_id_type=MESH,
        )

    def side_copy(self, which, slot, hop):
        spot = self.spot(which, hop)
        return pltpu.make_async_remote_copy(
            src_ref=spot,
            dst_ref=spot,
            send_sem=self.side_sems.at[0, which, slot],
            recv_sem=self.side_sems.at[1, which, slot],
            device_id=(self.index, 1 - self.plane),
            device_id_type=MESH,
        )

    def own_copy(self, which):
        return pltpu.make_async_copy(
            self.pieces[which][0], self.spot(which, 0), self.own_sems.at[which]
        )

    def on_ring(self, which, inside, outside=None):
        via = self.pieces[which][2]
        if via is None:
            inside()
            return
        pl.when(self.plane == via)(inside)
        if outside is not None:
            pl.when(self.plane != via)(outside)

    def begin(self, which):
        def inside():
            self.ring_copy(which, 0, 1).start()
            self.ring_copy(which, 1, 1).start()

        self.on_ring(which, inside)
        self.core_copy(which, 0, 0).start()
        self.own_copy(which).start()

    def event(self, which, way, step):
        slot = step if way == 0 else self.last(which)[0] + step
        hop = step if way == 0 else -step

        def inside():
            self.ring_copy(which, way, step).wait_recv()
            if step < self.last(which)[way]:
                self.ring_copy(which, way, step + 1).start()
            if self.pieces[which][2] is not None:
                self.side_copy(which, slot, hop).start()
            self.core_copy(which, slot, hop).start()

        self.on_ring(which, inside)

    def relay(self, which, way, step):
        slot = step if way == 0 else self.last(which)[0] + step
        hop = step if way == 0 else -step

        def outside():
            self.side_copy(which, slot, hop).wait_recv()
            self.core_copy(which, slot, hop).start()

        self.on_ring(which, lambda: None, outside)

    def plan(self, groups):
        rounds = []
        for number, group in enumerate(groups):
            for step in range(1, self.half + 1):
                rounds.append(
                    [
                        (number, which, way, step)
                        for which in group
                        for way in (0, 1)
                        if step <= self.last(which)[way]
                    ]
                )
        events, late = [], [[], []]
        for turn in rounds + [[], []]:
            events += [(False,) + e for e in turn] + [(True,) + e for e in late.pop(0)]
            late.append([e for e in turn if self.pieces[e[1]][2] is not None])
        return events

    def arrived(self, which):
        for slot in range(self.chips):
            self.core_copy(which, slot, 0).wait_recv()
        self.own_copy(which).wait()

    def drain(self, which):
        last = self.last(which)

        def inside():
            for way in (0, 1):
                for step in range(1, last[way] + 1):
                    self.ring_copy(which, way, step).wait_send()
            if self.pieces[which][2] is not None:
                for slot in range(1, self.chips):
                    self.side_copy(which, slot, 0).wait_send()

        self.on_ring(which, inside)
        for slot in range(self.chips):
            self.core_copy(which, slot, 0).wait_send()


def remote(src, dst, where, sems, slot):
    return pltpu.make_async_remote_copy(
        src_ref=src,
        dst_ref=dst,
        send_sem=sems.at[0, slot],
        recv_sem=sems.at[1, slot],
        device_id=where,
        device_id_type=MESH,
    )


MEMBERS = D // GROUPS


def group_mean(column):
    column = jnp.broadcast_to(column, (8, D))
    lane = lax.broadcasted_iota(jnp.int32, (8, D), 1)
    first = lane == 0
    for group in range(1, GROUPS):
        first = first | (lane == group * MEMBERS)

    def shift(values, count):
        return pltpu.roll(values, count % D, 1)

    two = column + shift(column, -1)
    four = two + shift(two, -2)
    eight = four + shift(four, -4)
    whole = eight + shift(eight, -8) + shift(four, -16)
    whole = jnp.where(first, whole, 0.0)
    two = whole + shift(whole, 1)
    four = two + shift(two, 2)
    eight = four + shift(four, 4)
    spread = eight + shift(eight, 8) + shift(four, 16)
    return spread[0:1, :] * (1.0 / MEMBERS)


def col_mean(values):
    return jnp.sum(values, axis=0, keepdims=True) * (1.0 / values.shape[0])


def side_by_side(wide, values, order):
    rows = values.shape[0]
    column = lax.broadcasted_iota(jnp.int32, (rows, D), 0) & (SIDE - 1)
    before = jnp.where(column == 0, 0.0, pltpu.roll(values, 1, 0)).astype(BF)
    after = jnp.where(column == SIDE - 1, 0.0, pltpu.roll(values, rows - 1, 0)).astype(BF)
    parts = (before, values.astype(BF), after)
    for spot, part in enumerate(order):
        wide[:, spot * D : (spot + 1) * D] = parts[part]


def swap_edges(act, edge_send, edge_got, core, partner, sems, slot):
    share = act.shape[0] - 2 * SIDE
    start = pl.multiple_of(share - (share - SIDE) * core, SIDE)
    edge_send[...] = act[pl.ds(start, SIDE), :].astype(BF)
    copy = remote(edge_send, edge_got, partner, sems, slot)
    copy.start()
    copy.wait()
    border = edge_got[...].astype(F32)
    top = (core == 1).astype(F32)
    act[:SIDE, :] = border * top
    act[SIDE + share :, :] = border * (1.0 - top)


SHARDS = ("one", "time", "two", "q", "kv", "so", "cq", "ckv", "co", "ff")


def call_named(body, name, ins, outs, scratch, collective):
    names = list(ins) + list(outs) + list(scratch)

    def kernel(*refs):
        body(types.SimpleNamespace(**dict(zip(names, refs))))

    results = pl.pallas_call(
        kernel,
        out_shape=[jax.ShapeDtypeStruct(o[0], o[1]) for o in outs.values()],
        in_specs=[i[1] for i in ins.values()],
        out_specs=[o[2] for o in outs.values()],
        scratch_shapes=list(scratch.values()),
        compiler_params=pltpu.CompilerParams(
            collective_id=collective, has_side_effects=True, vmem_limit_bytes=VMEM_BYTES
        ),
        name=name,
    )(*[i[0] for i in ins.values()])
    return types.SimpleNamespace(**dict(zip(outs, results)))


def expand_left(left, which):
    row = lax.broadcasted_iota(jnp.int32, (8, RANK_SQ), 0)
    col = lax.broadcasted_iota(jnp.int32, (8, RANK_SQ), 1)
    chosen = (col >> 3) if which == 0 else (col & 7)
    mark = jnp.where(row == chosen, 1.0, 0.0)
    return jnp.dot(left, mark, precision=lax.Precision.HIGHEST, preferred_element_type=F32)


def turned(left):
    row = lax.broadcasted_iota(jnp.int32, (8, 8), 0)
    col = lax.broadcasted_iota(jnp.int32, (8, 8), 1)
    mark = jnp.where(row == col, 1.0, 0.0)
    return lax.dot_general(
        mark,
        left,
        (((1,), (1,)), ((), ())),
        precision=lax.Precision.HIGHEST,
        preferred_element_type=F32,
    )


def factor_rows(outer, first, second):
    grad_first = [
        jnp.sum(outer[8 * r : 8 * r + 8] * second, axis=0, keepdims=True) for r in range(8)
    ]
    grad_second = sum(outer[8 * r : 8 * r + 8] * first[r : r + 1] for r in range(8))
    return jnp.concatenate(grad_first, axis=0), grad_second


def forward_body(chips, gathers, r):
    ring = Ring(chips, r.ring_sems, r.pair_sems, r.over_sems, r.own_sems)
    core, side = ring.core, ring.plane
    neighbour = (ring.index, 1 - side)
    partner = (ring.partner, side)
    diagonal = (ring.partner, 1 - side)
    home = core == side
    away = jnp.logical_not(home)
    barrier = pltpu.get_barrier_semaphore()
    others = [partner, neighbour, diagonal]
    if gathers:
        others += [(ring.right, side), (ring.left, side)]
    for where in others:
        pl.semaphore_signal(barrier, inc=1, device_id=where, device_id_type=MESH)
    pl.semaphore_wait(barrier, len(others))

    shard = {name: getattr(r, "in_" + name) for name in SHARDS} if gathers else {}
    got = {name: getattr(r, "got_" + name) for name in shard}
    joined = {name: getattr(r, "wide_" + name) for name in shard}
    full = {name: getattr(r, "full_" + name) for name in SHARDS}
    side_copies = {}
    for slot, name in enumerate(shard):
        if name != "one":
            side_copies[name] = remote(shard[name], got[name], neighbour, r.side_sems, slot)
    first_copies = []
    if gathers:
        for u in range(3):
            part = slice(3 * u, 3 * u + 3)
            copy = remote(
                shard["one"].at[part], got["one"].at[part], neighbour, r.first_sems, u
            )
            copy.start()
            first_copies.append(copy)
    core_copies = {}
    for slot, name in enumerate(("lat", "emb", "text", "scale")):
        core_copies[name] = remote(
            getattr(r, name), getattr(r, "got_" + name), partner, r.core_sems, slot
        )
    core_copies["lat"].start()
    core_copies["emb"].start()
    flat = ("split", "bias", "qr", "ur")
    for slot, name in enumerate(flat):
        side_copies["f_" + name] = remote(
            getattr(r, name),
            getattr(r, "got_" + name),
            neighbour,
            r.side_sems,
            len(SHARDS) + slot,
        )
    core_copies["text"].start()

    def send(*names):
        for name in names:
            side_copies[name].start()

    if gathers:
        send("time", "two")
    send("f_split", "f_qr")

    def join(name, first=0, count=None):
        if count is None:
            side_copies[name].wait_recv()
        mine, theirs, out = shard[name], got[name], joined[name]
        for lead in range(first, first + (count or mine.shape[0])):

            @pl.when(side == 0)
            def _():
                out[lead] = jnp.concatenate([mine[lead], theirs[lead]], axis=1)

            @pl.when(side == 1)
            def _():
                out[lead] = jnp.concatenate([theirs[lead], mine[lead]], axis=1)

    def piece(name, start, size, via=None, turn=0, first=0, count=None):
        rows = shard[name].shape[1]
        count = joined[name].shape[2] if count is None else count

        def target(owner):
            at = pl.multiple_of(owner * rows, 8)
            return full[name].at[start : start + size, pl.ds(at, rows), first : first + count]

        source = joined[name].at[start : start + size, :, first : first + count]
        return ring.add(source, target, via, turn)

    def taps(name):
        return [piece(name, 0, 3, 0, 0), piece(name, 3, 3, 1, 0), piece(name, 6, 3, None, 1)]

    groups = []
    if gathers:
        quarter = joined["ff"].shape[2] // 4
        groups = [
            [piece("one", 3 * u, 3, None, u % 2) for u in range(3)],
            [piece("time", 0, 1)] + taps("two"),
            [
                piece("q", 0, 1),
                piece("kv", 0, 1, 0, 0),
                piece("kv", 1, 1, 1, 0),
                piece("so", 0, 1, None, 1),
            ],
            [
                piece("cq", 0, 1),
                piece("ckv", 0, 1, 0, 0),
                piece("ckv", 1, 1, 1, 0),
                piece("co", 0, 1, None, 1),
            ],
            [
                piece("ff", 0, 3, 0, 0, 0, quarter),
                piece("ff", 0, 3, 1, 0, quarter, quarter),
                piece("ff", 0, 3, None, 1, 2 * quarter, quarter),
            ],
            [
                piece("ff", 0, 1, 0, 0, 3 * quarter, quarter),
                piece("ff", 1, 1, 1, 0, 3 * quarter, quarter),
                piece("ff", 2, 1, None, 1, 3 * quarter, quarter),
            ],
        ]
    events = ring.plan(groups)
    begun = {}

    def begin(number):
        if number < len(groups) and number not in begun:
            begun[number] = True
            for which in groups[number]:
                ring.begin(which)

    def poll(limit=4):
        while events and limit > 0:
            relayed, number, which, way, step = events.pop(0)
            if relayed:
                ring.relay(which, way, step)
                continue
            limit -= 1
            ring.event(which, way, step)
            if step == ring.half - 1 and (which, way) == (groups[number][-1], 1):
                begin(number + 2)

    def poll_group(number):
        while any(e[1] <= number for e in events):
            poll(1)

    def arrived(number, position):
        if gathers:
            ring.arrived(groups[number][position])

    def load(name, start, size, target, slot):
        copy = pltpu.make_async_copy(
            full[name].at[start : start + size] if size else full[name].at[start],
            target,
            r.load_sems.at[slot],
        )
        copy.start()
        return copy

    core_copies["lat"].wait_recv()

    @pl.when(home)
    def _():
        r.image[...] = r.lat[...]

    @pl.when(away)
    def _():
        r.image[...] = r.got_lat[...]

    if gathers:
        begun[0] = True
        for u in range(3):
            first_copies[u].wait_recv()
            join("one", 3 * u, 3)
            ring.begin(groups[0][u])
        send("q", "kv", "so", "cq", "ckv", "co")
    share = r.image.shape[0] // 2
    mine = pl.ds(pl.multiple_of(core * share, share), share)
    pixels = r.image[...].astype(F32)
    mean_one = group_mean(col_mean(pixels))
    centred = pixels - mean_one
    inv_one = lax.rsqrt(group_mean(col_mean(centred * centred)) + NORM_EPS)
    slope = inv_one * (1.0 + r.vec[0:1, :])

    def first_act(values):
        pre = (values.astype(F32) - mean_one) * slope + r.vec[1:2, :]
        return pre * jax.nn.sigmoid(pre)

    r.img[...] = r.image[mine, :]
    r.act[SIDE : SIDE + share, :] = first_act(r.image[mine, :])
    border = first_act(r.image[pl.ds(pl.multiple_of(share - SIDE * core, SIDE), SIDE), :])
    top = (core == 1).astype(F32)
    r.act[:SIDE, :] = border * top
    r.act[SIDE + share :, :] = border * (1.0 - top)
    side_by_side(r.wide, r.act[...], (0, 1, 2))
    if gathers:
        join("time")
        join("two")
        begin(1)
        send("ff")
    send("f_bias", "f_ur")
    poll(6)
    for name in SHARDS[3:-1] if gathers else ():
        join(name)
    poll(6)
    if gathers:
        join("ff")

    for name in flat:
        side_copies["f_" + name].wait_recv()
        own_part, got_part, whole = (
            getattr(r, name),
            getattr(r, "got_" + name),
            getattr(r, "all_" + name),
        )

        @pl.when(side == 0)
        def _():
            whole[...] = jnp.concatenate([own_part[...], got_part[...]], axis=1)

        @pl.when(side == 1)
        def _():
            whole[...] = jnp.concatenate([got_part[...], own_part[...]], axis=1)

    for row in range(8):
        rows = slice(8 * row, 8 * row + 8)
        r.zq[rows, :] = (r.all_qr[row : row + 1, :] * r.all_qr[8:16, :]).astype(BF)
        for part in range(2):
            base = 16 * part
            r.zu[part, rows, :] = (
                r.all_ur[base + row : base + row + 1, :] * r.all_ur[base + 8 : base + 16, :]
            ).astype(BF)
    poll()
    for left, pair, flipped in ((r.ql, r.yq, r.lq), (r.ul, r.yu, r.lu)):
        pair[...] = (expand_left(left[0], 0) * expand_left(left[1], 1)).astype(BF)
        flipped[0:8, :] = turned(left[0])
        flipped[8:16, :] = turned(left[1])

    poll()

    def chosen(table, spot):
        lane = lax.broadcasted_iota(jnp.int32, table.shape, 1)
        return jnp.sum(jnp.where(lane == spot[...], table[...], 0.0), axis=1, keepdims=True)

    scale = chosen(r.step_weights, r.step) * chosen(r.group_weights, r.group)
    r.scale[...] = jnp.broadcast_to(scale, r.scale.shape)
    core_copies["scale"].start()
    cot_copy = remote(r.cot, r.all_cot, diagonal, r.core_sems, 6)

    @pl.when(home)
    def _():
        r.all_cot[...] = r.cot[...]

    @pl.when(away)
    def _():
        cot_copy.start()

    core_copies["emb"].wait_recv()
    core_copies["text"].wait_recv()
    core_copies["scale"].wait_recv()
    own = home.astype(F32)
    r.scale_out[...] = r.scale[...] * own + r.got_scale[...] * (1.0 - own)
    count = r.text.shape[0]

    @pl.when(home)
    def _():
        r.text_all[:count, :] = r.text[...]

    @pl.when(away)
    def _():
        r.text_all[:count, :] = r.got_text[...]

    r.text_all[count:, :] = jnp.zeros((LANES - count, r.text.shape[1]), BF)
    poll_group(0)

    loads = []
    for u in range(3):
        arrived(0, u)
        loads.append(load("one", 3 * u, 3, r.kernels.at[3 * u : 3 * u + 3], u))
    for u in range(3):
        loads[u].wait()
        term = dot_nn(
            r.wide[u * SIDE : u * SIDE + share, :],
            r.kernels[3 * u : 3 * u + 3].reshape(3 * D, D),
        )
        if u == 0:
            r.h1[...] = term
        else:
            r.h1[...] += term
        poll()
    while any(e[2] == groups[1][0] for e in events):
        poll(1)
    arrived(1, 0)
    time_load = load("time", 0, 0, r.time_buf, 3)
    time_load.wait()
    embed = r.emb[...] * own + r.got_emb[...] * (1.0 - own)
    embed = (embed * jax.nn.sigmoid(embed)).astype(BF)
    shift = dot_nn(jnp.broadcast_to(embed, (8, embed.shape[1])), r.time_buf[...])[0:1, :]
    inner = r.h1[...] + (r.all_split[0:1, :] + (shift + r.all_split[1:2, :]))
    r.h1[...] = inner
    poll()
    local_mean = group_mean(col_mean(inner))
    local_dev = inner - local_mean
    local_var = group_mean(col_mean(local_dev * local_dev))
    r.stat_send[0:1, :] = local_mean
    r.stat_send[1:2, :] = local_var
    stat_copy = remote(r.stat_send, r.stat_got, partner, r.core_sems, 4)
    stat_copy.start()
    poll()
    stat_copy.wait()
    other_mean, other_var = r.stat_got[0:1, :], r.stat_got[1:2, :]
    mean_two = 0.5 * (local_mean + other_mean)
    gap = 0.5 * (local_mean - other_mean)
    inv_two = lax.rsqrt(0.5 * (local_var + other_var) + gap * gap + NORM_EPS)
    r.stats[0:1, :] = mean_one
    r.stats[1:2, :] = inv_one
    r.stats[2:3, :] = mean_two
    r.stats[3:4, :] = inv_two
    r.stats[4:8, :] = jnp.zeros((4, D), F32)
    pre = (r.h1[...] - mean_two) * (inv_two * (1.0 + r.all_split[2:3, :])) + r.all_split[3:4, :]
    r.act[SIDE : SIDE + share, :] = pre * jax.nn.sigmoid(pre)
    swap_edges(r.act, r.edge_send, r.edge_got, core, partner, r.core_sems, 5)
    side_by_side(r.wide, r.act[...], (0, 1, 2))
    poll_group(1)

    loads = []
    for u in range(3):
        arrived(1, 1 + u)
        loads.append(load("two", 3 * u, 3, r.kernels.at[3 * u : 3 * u + 3], u))
    for u in range(3):
        loads[u].wait()
        term = None
        for w in range(3):
            part = dot_nt(
                r.wide[u * SIDE : u * SIDE + share, w * D : (w + 1) * D], r.kernels[3 * u + w]
            )
            term = part if term is None else term + part
        if u == 0:
            r.h[...] = term
        else:
            r.h[...] += term
        poll()
    r.h[...] = r.img[...].astype(F32) + (r.h[...] + r.vec[2:3, :])

    poll_group(2)
    loads = []
    for slot, (name, spots, at, size) in enumerate(
        (("kv", (1, 2), 1, 2), ("q", (0,), 0, 1), ("so", (3,), 3, 1))
    ):
        for spot in spots:
            arrived(2, spot)
        loads.append(load(name, 0, size, r.kernels.at[at : at + size], slot))
    norm, _, _ = layer_norm(r.h[...], 1.0 + r.vec[3:4, :], r.vec[4:5, :])
    low = norm.astype(BF)
    loads[0].wait()
    for part in range(2):
        proj = dot_nn(low, r.kernels[1 + part]).astype(BF)
        blank = jnp.zeros((share, LANES - HEAD_DIM), BF)
        for head in range(HEADS):
            span = proj[:, HEAD_DIM * head : HEAD_DIM * (head + 1)]
            r.kv[part, head, mine, :] = jnp.concatenate([span, blank], axis=1)
    kv_copy = remote(r.kv.at[:, :, mine, :], r.kv.at[:, :, mine, :], partner, r.core_sems, 7)
    kv_copy.start()
    loads[1].wait()
    r.ext_act[:, :D] = low
    r.ext_act[:, D:] = dot_nn(low, r.yq[...]).astype(BF)
    r.ext_w[:D, :] = r.kernels[0]
    r.ext_w[D:, :] = r.zq[...]
    to_heads(r.q, dot_nn(r.ext_act[...], r.ext_w[...]).astype(BF))
    kv_copy.wait()
    poll()
    lane = lax.broadcasted_iota(jnp.int32, (share, LANES), 1)
    r.lse_cols[...] = jnp.zeros_like(r.lse_cols)

    def one_head(head, carry):
        scores = dot_nt(r.q[head], r.kv[0, head])
        peak = jnp.max(scores, axis=1, keepdims=True)
        expo = jnp.exp2((scores - peak) * (FACTOR * LOG_TWO_E))
        total = jnp.sum(expo, axis=1, keepdims=True)
        probs = (expo * (1.0 / total)).astype(BF)
        r.heads[head] = dot_nn(probs, r.kv[1, head]).astype(BF)
        row = peak * (FACTOR * LOG_TWO_E) + jnp.log2(total)
        r.lse_cols[...] = jnp.where(lane == head, row, r.lse_cols[...])
        return carry

    for first in range(0, HEADS, 2):
        lax.fori_loop(first, first + 2, one_head, 0)
        poll()
    r.lse[...] = r.lse_cols[...].T
    merged = from_heads(r.heads)
    r.o[...] = merged
    loads[2].wait()
    r.h2[...] = r.h[...] + (dot_nt(merged, r.kernels[3]) + r.vec[9:10, :])

    poll()
    poll_group(3)
    for position in range(4):
        arrived(3, position)
    loads = [
        load("cq", 0, 1, r.kernels.at[4:5], 0),
        load("ckv", 0, 2, r.text_kv, 1),
        load("co", 0, 1, r.kernels.at[5:6], 2),
    ]
    norm, _, _ = layer_norm(r.h2[...], 1.0 + r.vec[5:6, :], r.vec[6:7, :])
    loads[0].wait()
    to_heads(r.cq, dot_nn(norm.astype(BF), r.kernels[4]).astype(BF))
    loads[1].wait()
    for part in range(2):
        to_heads(r.ckv.at[part], dot_nn(r.text_all[...], r.text_kv[part]).astype(BF))

    poll()

    def cross_head(head, carry):
        probs = cross_probs(r.cq[head], r.ckv[0, head])
        r.heads[head] = dot_nn(probs.astype(BF), r.ckv[1, head]).astype(BF)
        return carry

    lax.fori_loop(0, HEADS, cross_head, 0)
    loads[2].wait()
    r.h3[...] = r.h2[...] + (dot_nt(from_heads(r.heads), r.kernels[5]) + r.vec[10:11, :])

    poll(len(events))
    for group in groups[4:]:
        for which in group:
            ring.arrived(which)
    for group in groups:
        for which in group:
            ring.drain(which)
    for copy in first_copies + list(side_copies.values()) + list(core_copies.values()):
        copy.wait_send()

    @pl.when(away)
    def _():
        cot_copy.wait()


def forward(arrays, shards, full, chips):
    gathers = full is None
    share = arrays["lat"].shape[0] // 2
    anywhere = pl.BlockSpec(memory_space=pl.ANY)
    dma = pltpu.SemaphoreType.DMA
    ins = {name: (value, WHOLE) for name, value in arrays.items()}
    text_rows, text_width = arrays["text"].shape
    time_width = arrays["emb"].shape[1]

    def double(name):
        rows, cols = arrays[name].shape
        return (rows, 2 * cols)

    outs = {
        "h": ((share, D), F32, WHOLE),
        "h1": ((share, D), F32, WHOLE),
        "img": ((share, D), BF, WHOLE),
        "stats": ((8, D), F32, WHOLE),
        "h2": ((share, D), F32, WHOLE),
        "h3": ((share, D), F32, WHOLE),
        "q": ((HEADS, share, LANES), BF, WHOLE),
        "kv": ((2, HEADS, 2 * share, LANES), BF, WHOLE),
        "o": ((share, D), BF, WHOLE),
        "lse": ((LANES, share), F32, WHOLE),
        "cq": ((HEADS, share, LANES), BF, WHOLE),
        "ckv": ((2, HEADS, LANES, LANES), BF, WHOLE),
        "all_split": (double("split"), F32, WHOLE),
        "all_bias": (double("bias"), F32, WHOLE),
        "all_qr": (double("qr"), F32, WHOLE),
        "all_ur": (double("ur"), F32, WHOLE),
        "yq": ((D, RANK_SQ), BF, WHOLE),
        "yu": ((D, RANK_SQ), BF, WHOLE),
        "lq": ((16, D), F32, WHOLE),
        "lu": ((16, D), F32, WHOLE),
        "zq": ((RANK_SQ, D), BF, WHOLE),
        "zu": ((2, RANK_SQ, double("ur")[1]), BF, WHOLE),
        "all_cot": ((share, D), BF, WHOLE),
        "scale_out": ((8, LANES), F32, WHOLE),
    }
    scratch = {}
    if gathers:
        for name, value in zip(SHARDS, shards):
            lead, rows, cols = value.shape
            ins["in_" + name] = (value, WHOLE)
            outs["full_" + name] = ((lead, rows * chips * 2, 2 * cols), BF, anywhere)
            scratch["got_" + name] = pltpu.VMEM(value.shape, BF)
            scratch["wide_" + name] = pltpu.VMEM((lead, rows, 2 * cols), BF)
    else:
        for name, value in zip(SHARDS, full):
            ins["full_" + name] = (value, anywhere)
    for name in ("lat", "emb", "text", "split", "bias", "qr", "ur"):
        value = arrays[name]
        scratch["got_" + name] = pltpu.VMEM(value.shape, value.dtype)
    pieces = 22 if gathers else 1
    scratch.update(
        image=pltpu.VMEM(arrays["lat"].shape, BF),
        kernels=pltpu.VMEM((9, D, D), BF),
        time_buf=pltpu.VMEM((time_width, D), BF),
        text_kv=pltpu.VMEM((2, text_width, D), BF),
        text_all=pltpu.VMEM((LANES, text_width), BF),
        wide=pltpu.VMEM((share + 2 * SIDE, 3 * D), BF),
        act=pltpu.VMEM((share + 2 * SIDE, D), F32),
        scale=pltpu.VMEM((8, LANES), F32),
        got_scale=pltpu.VMEM((8, LANES), F32),
        stat_send=pltpu.VMEM((8, D), F32),
        stat_got=pltpu.VMEM((8, D), F32),
        edge_send=pltpu.VMEM((SIDE, D), BF),
        edge_got=pltpu.VMEM((SIDE, D), BF),
        ext_act=pltpu.VMEM((share, D + RANK_SQ), BF),
        ext_w=pltpu.VMEM((D + RANK_SQ, D), BF),
        heads=pltpu.VMEM((HEADS, share, LANES), BF),
        lse_cols=pltpu.VMEM((share, LANES), F32),
        first_sems=dma((2, 3)),
        side_sems=dma((2, len(SHARDS) + 4)),
        core_sems=dma((2, 8)),
        load_sems=dma((4,)),
        ring_sems=dma((2, 2, pieces, chips // 2)),
        pair_sems=dma((2, pieces, chips)),
        over_sems=dma((2, pieces, chips)),
        own_sems=dma((pieces,)),
    )
    return call_named(
        functools.partial(forward_body, chips, gathers), "forward", ins, outs, scratch, 1
    )


class Halving:
    HALVINGS = 3

    def __init__(self, steps, acc, got, out, sems):
        self.acc, self.got, self.out, self.sems, self.steps = acc, got, out, sems, steps
        index = lax.axis_index("dp")
        plane = lax.axis_index("mp")
        core = lax.rem(index, 2)
        chip = index // 2
        self.partners = [((index + 1 - 2 * core, plane), core), ((index, 1 - plane), plane)]
        span = 1
        for _ in range(steps - 2):
            bit = lax.rem(chip // span, 2)
            self.partners.append((((chip + span - 2 * span * bit) * 2 + core, plane), bit))
            span *= 2
        self.offset, self.size, self.base = 0, acc.shape[0], 0
        self.trail = []
        self.flight = None
        self.done = 0

    @classmethod
    def room(cls, rows, steps):
        small = rows >> cls.HALVINGS
        return rows - small + small * (steps - cls.HALVINGS)

    def begin(self):
        self._down(0)

    def _down(self, step):
        where, bit = self.partners[step]
        if step < self.HALVINGS:
            size = self.size // 2
            mine = pl.multiple_of(self.offset + bit * size, 8)
            theirs = pl.multiple_of(self.offset + (1 - bit) * size, 8)
        else:
            size, mine, theirs = self.size, self.offset, self.offset
        copy = remote(
            self.acc.at[pl.ds(theirs, size), :],
            self.got.at[pl.ds(self.base, size), :],
            where,
            self.sems,
            step,
        )
        copy.start()
        self.flight = (copy, mine, size)

    def _up(self, step):
        mine, size, where = self.trail[step]
        part = self.out.at[pl.ds(mine, size), :]
        copy = remote(part, part, where, self.sems, self.steps + step)
        copy.start()
        self.flight = (copy, mine, size)

    def step(self):
        steps, total = self.steps, self.steps + self.HALVINGS
        if self.done >= total:
            return
        copy, mine, size = self.flight
        copy.wait()
        if self.done < steps:
            self.acc[pl.ds(mine, size), :] += self.got[pl.ds(self.base, size), :]
            self.trail.append((mine, size, self.partners[self.done][0]))
            self.offset, self.size = mine, size
            self.base += size
            if self.done + 1 < steps:
                self._down(self.done + 1)
            else:
                self.out[pl.ds(mine, size), :] = self.acc[pl.ds(mine, size), :]
                self._up(self.HALVINGS - 1)
        elif self.done + 1 < total:
            self._up(total - 2 - self.done)
        self.done += 1


def conv_back_kernel(
    steps,
    g0_ref,
    h1_ref,
    img_ref,
    stat_ref,
    split_ref,
    vec_ref,
    up_right_ref,
    up_left_ref,
    query_right_ref,
    query_left_ref,
    one_ref,
    two_ref,
    grad_ref,
    sum_ref,
    one_buf,
    two_buf,
    wide,
    act,
    half_back,
    stat_send,
    stat_got,
    edge_send,
    edge_got,
    acc,
    got,
    load_sems,
    core_sems,
    sum_sems,
    back_sems,
):
    index = lax.axis_index("dp")
    side = lax.axis_index("mp")
    core = lax.rem(index, 2)
    partner = (index + 1 - 2 * core, side)
    neighbour = (index, 1 - side)
    diagonal = (index + 1 - 2 * core, 1 - side)
    share = g0_ref.shape[0]
    loads = []
    for slot, (src, dst) in enumerate(((two_ref, two_buf), (one_ref, one_buf))):
        load = pltpu.make_async_copy(src, dst, load_sems.at[slot])
        load.start()
        loads.append(load)
    total = Halving(steps, acc, got, sum_ref, sum_sems)
    barrier = pltpu.get_barrier_semaphore()
    for where, _ in total.partners:
        pl.semaphore_signal(barrier, inc=1, device_id=where, device_id_type=MESH)
    pl.semaphore_signal(barrier, inc=1, device_id=diagonal, device_id_type=MESH)
    parts = []
    for member in range(2):
        for part in range(2):
            for block in range(up_right_ref.shape[3] // D):
                parts.append(up_right_ref[member, part, :, block * D : (block + 1) * D])
    for ref in (query_right_ref, up_left_ref, query_left_ref):
        parts += [ref[0], ref[1]]
    for spot, part in enumerate(parts):
        acc[8 * spot : 8 * spot + 8, :] = part
    acc[8 * len(parts) :, :] = jnp.zeros((acc.shape[0] - 8 * len(parts), D), F32)
    act[SIDE : SIDE + share, :] = g0_ref[...]
    pl.semaphore_wait(barrier, steps + 1)
    total.begin()
    swap_edges(act, edge_send, edge_got, core, partner, core_sems, 0)
    side_by_side(wide, act[...], (2, 1, 0))
    total.step()
    inner = act.at[SIDE : SIDE + share, :]
    loads[0].wait()
    for u in range(3):
        term = dot_nn(
            wide[u * SIDE : u * SIDE + share, :],
            two_buf[3 * (2 - u) : 3 * (2 - u) + 3].reshape(3 * D, D),
        )
        if u == 0:
            inner[...] = term
        else:
            inner[...] += term
        total.step()
    mean_two, inv_two = stat_ref[2:3, :], stat_ref[3:4, :]
    gain_two = 1.0 + split_ref[2:3, :]
    normal = (h1_ref[...] - mean_two) * inv_two
    scaled = inner[...] * silu_slope(normal * gain_two + split_ref[3:4, :]) * gain_two
    means = pair_means(scaled, normal, stat_send, stat_got, partner, core_sems, 1)
    inner[...] = inv_two * (scaled - means[0] - normal * means[1])
    swap_edges(act, edge_send, edge_got, core, partner, core_sems, 2)
    side_by_side(wide, act[...], (2, 1, 0))
    total.step()
    loads[1].wait()
    for u in range(3):
        term = None
        for spot in range(3):
            part = dot_nt(
                wide[u * SIDE : u * SIDE + share, spot * D : (spot + 1) * D],
                one_buf[3 * (2 - u) + spot],
            )
            term = part if term is None else term + part
        if u == 0:
            inner[...] = term
        else:
            inner[...] += term
        total.step()
    mean_one, inv_one = stat_ref[0:1, :], stat_ref[1:2, :]
    gain_one = 1.0 + vec_ref[0:1, :]
    normal = (img_ref[...].astype(F32) - mean_one) * inv_one
    scaled = inner[...] * silu_slope(normal * gain_one + vec_ref[1:2, :]) * gain_one
    means = pair_means(scaled, normal, stat_send, stat_got, partner, core_sems, 3)
    half_back[...] = (
        g0_ref[...] + inv_one * (scaled - means[0] - normal * means[1])
    ).astype(BF)
    mine = grad_ref.at[pl.ds(pl.multiple_of(core * share, share), share), :]
    home = core == side

    @pl.when(home)
    def _():
        remote(half_back, mine, neighbour, back_sems, core).start()
        pltpu.make_async_copy(half_back, mine, load_sems.at[2]).start()

    @pl.when(jnp.logical_not(home))
    def _():
        remote(half_back, mine, diagonal, back_sems, core).start()
        remote(half_back, mine, partner, back_sems, 2 + core).start()

    for _ in range(2 * steps):
        total.step()

    def part(which):
        return grad_ref.at[pl.ds(pl.multiple_of(which * share, share), share), :]

    @pl.when(home)
    def _():
        remote(half_back, mine, neighbour, back_sems, core).wait_send()
        pltpu.make_async_copy(half_back, mine, load_sems.at[2]).wait()
        remote(half_back, part(1 - core), partner, back_sems, 3 - core).wait_recv()

    @pl.when(jnp.logical_not(home))
    def _():
        remote(half_back, mine, diagonal, back_sems, core).wait_send()
        remote(half_back, mine, partner, back_sems, 2 + core).wait_send()
        remote(half_back, part(core), neighbour, back_sems, core).wait_recv()
        remote(half_back, part(1 - core), diagonal, back_sems, 1 - core).wait_recv()


def pair_means(scaled, normal, stat_send, stat_got, partner, sems, slot):
    stat_send[0:1, :] = group_mean(col_mean(scaled))
    stat_send[1:2, :] = group_mean(col_mean(scaled * normal))
    copy = remote(stat_send, stat_got, partner, sems, slot)
    copy.start()
    copy.wait()
    both = 0.5 * (stat_send[...] + stat_got[...])
    return both[0:1, :], both[1:2, :]


def conv_back(g0, h1, img, stats, split, vectors, grads, one, two, devices):
    share = g0.shape[0]
    steps = devices.bit_length() - 1
    dma = pltpu.SemaphoreType.DMA
    unit = 8 << Halving.HALVINGS
    rows = -(-sum(g.size // D for g in grads) // unit) * unit
    return pl.pallas_call(
        functools.partial(conv_back_kernel, steps),
        out_shape=[
            jax.ShapeDtypeStruct((2 * share, D), BF),
            jax.ShapeDtypeStruct((rows, D), F32),
        ],
        in_specs=[WHOLE] * 10 + [pl.BlockSpec(memory_space=pl.ANY)] * 2,
        out_specs=[WHOLE] * 2,
        scratch_shapes=[
            pltpu.VMEM((9, D, D), BF),
            pltpu.VMEM((9, D, D), BF),
            pltpu.VMEM((share + 2 * SIDE, 3 * D), BF),
            pltpu.VMEM((share + 2 * SIDE, D), F32),
            pltpu.VMEM((share, D), BF),
            pltpu.VMEM((8, D), F32),
            pltpu.VMEM((8, D), F32),
            pltpu.VMEM((SIDE, D), BF),
            pltpu.VMEM((SIDE, D), BF),
            pltpu.VMEM((rows, D), F32),
            pltpu.VMEM((Halving.room(rows, steps), D), F32),
            dma((3,)),
            dma((2, 4)),
            dma((2, steps + Halving.HALVINGS)),
            dma((2, 4)),
        ],
        compiler_params=pltpu.CompilerParams(
            collective_id=5, has_side_effects=True, vmem_limit_bytes=VMEM_BYTES
        ),
        name="conv_back",
    )(g0, h1, img, stats, split, vectors, *grads, one, two)


def shards(
    latents,
    out_grad,
    text_states,
    time_embed,
    group_ids,
    group_weights,
    timesteps,
    step_weights,
    vectors,
    split_vectors,
    up_bias,
    conv_one,
    conv_two,
    time_proj,
    self_query,
    self_kv,
    self_out,
    cross_query,
    cross_kv,
    cross_out,
    ff_up,
    ff_down,
    query_left_state,
    query_right_state,
    up_left_state,
    up_right_state,
):
    devices_dp = lax.axis_size("dp")
    chips = devices_dp // 2
    side = lax.axis_index("mp")

    def join_sides(values):
        other = lax.ppermute(values, "mp", [(0, 1), (1, 0)])
        first = jnp.where(side == 0, values, other)
        second = jnp.where(side == 0, other, values)
        return jnp.concatenate([first, second], axis=-1)

    pieces = [
        conv_one,
        time_proj[None],
        conv_two.transpose(0, 2, 1),
        self_query[None],
        self_kv.transpose(1, 0, 2),
        self_out.T[None],
        cross_query[None],
        cross_kv.transpose(1, 0, 2),
        cross_out.T[None],
        jnp.concatenate([ff_up.transpose(1, 0, 2), ff_down.T[None]], axis=0),
    ]
    gathers = all(piece.shape[1] % 8 == 0 for piece in pieces)
    full = None
    if not gathers:
        full = [lax.all_gather(join_sides(p), "dp", axis=1, tiled=True) for p in pieces]
    up_rows = up_right_state[0].transpose(2, 0, 1, 3)
    arrays = {
        "lat": latents[0],
        "emb": time_embed,
        "text": text_states[0],
        "split": split_vectors,
        "bias": up_bias,
        "qr": query_right_state[0].reshape(-1, query_right_state.shape[-1]),
        "ur": up_rows.reshape(-1, up_rows.shape[-1]),
        "ql": query_left_state[0],
        "ul": up_left_state[0],
        "vec": vectors,
        "cot": out_grad[0],
        "step": timesteps[:, None],
        "group": group_ids[:, None],
        "step_weights": step_weights[None],
        "group_weights": group_weights[None],
    }
    fwd = forward(arrays, pieces, full, chips)
    if not gathers:
        w_one, _, w_two_t, w_q, w_kv, w_so_t, w_cq, _, w_co_t, w_ff = full
    else:
        w_one, w_two_t, w_q, w_kv = fwd.full_one, fwd.full_two, fwd.full_q, fwd.full_kv
        w_so_t, w_cq, w_co_t, w_ff = fwd.full_so, fwd.full_cq, fwd.full_co, fwd.full_ff
    image_out, cotangent, grad_up_right, grad_up_left = feed_forward(
        fwd.h3,
        fwd.all_cot,
        fwd.scale_out,
        vectors,
        w_ff,
        fwd.all_bias,
        fwd.yu,
        fwd.zu,
        fwd.all_ur,
        fwd.lu,
    )
    cotangent, grad_query_right, grad_query_left, block_out = attention_back(
        cotangent,
        fwd.h,
        fwd.h2,
        vectors,
        w_q[0],
        fwd.yq,
        fwd.zq,
        w_kv,
        w_so_t[0],
        w_cq[0],
        w_co_t[0],
        fwd.q,
        fwd.kv,
        fwd.o,
        fwd.lse,
        fwd.cq,
        fwd.ckv,
        fwd.all_qr,
        fwd.lq,
        image_out,
    )
    block_out = block_out[None]
    latents_grad, total = conv_back(
        cotangent,
        fwd.h1,
        fwd.img,
        fwd.stats,
        fwd.all_split,
        vectors,
        [grad_up_right, grad_up_left, grad_query_right, grad_query_left],
        w_one,
        w_two_t,
        devices_dp * 2,
    )
    latents_grad = latents_grad[None]
    blocks = grad_up_right.shape[3] // D
    rows = 4 * blocks * 8
    grad_up_right = total[:rows].reshape(2, 2, blocks, 8, D).transpose(0, 3, 1, 2, 4)
    grad_up_right = grad_up_right.reshape(2, 8, 2, blocks * D)
    grad_query_right = total[rows : rows + 16].reshape(2, 8, D)
    grad_up_left = total[rows + 16 : rows + 32].reshape(2, 8, D).transpose(0, 2, 1)
    grad_query_left = total[rows + 32 : rows + 48].reshape(2, 8, D).transpose(0, 2, 1)

    def my_side(values):
        size = values.shape[-1] // 2
        return lax.dynamic_slice_in_dim(values, side * size, size, values.ndim - 1)

    grad_query_right = my_side(grad_query_right)
    grad_up_right = my_side(grad_up_right)
    left_weight, left_moment, left_second, left_average = adamw_parts(
        query_left_state, grad_query_left
    )
    right_weight, right_moment, right_second, right_average = adamw_parts(
        query_right_state, grad_query_right
    )
    query_left_new = jnp.stack([left_weight, left_average])
    query_left_copy = left_weight.astype(BF)
    query_right_new = jnp.stack([right_weight, right_average])
    query_right_copy = right_weight.astype(BF)
    left_pair = my_side(jnp.stack([left_moment, left_second]).transpose(0, 1, 3, 2))
    right_pair = jnp.stack([right_moment, right_second])
    query_moments = jnp.stack([left_pair, right_pair])
    up_left_new, up_left_copy = adamw(up_left_state, grad_up_left)
    up_right_new, up_right_copy = adamw(up_right_state, grad_up_right)
    return (
        block_out,
        latents_grad,
        query_left_new,
        query_left_copy,
        query_right_new,
        query_right_copy,
        up_left_new,
        up_left_copy,
        up_right_new,
        up_right_copy,
        query_moments,
    )


def solution(mesh):
    placed = (
        P("dp", None, None),
        P("dp", "mp", None),
        P("dp", None, None),
        P("dp", None),
        P("dp"),
        P(),
        P("dp"),
        P(),
        P(),
        P(None, "mp"),
        P(None, "mp"),
        P(None, "dp", "mp"),
        P(None, "mp", "dp"),
        P("dp", "mp"),
        P("dp", "mp"),
        P("dp", None, "mp"),
        P("mp", "dp"),
        P("dp", "mp"),
        P("dp", None, "mp"),
        P("mp", "dp"),
        P("dp", None, "mp"),
        P("mp", "dp"),
        P(),
        P(None, None, None, "mp"),
        P(),
        P(None, None, None, None, "mp"),
    )
    return jax.shard_map(
        shards,
        mesh=mesh,
        in_specs=placed,
        out_specs=(
            P("dp", "mp", None),
            P("dp", None, None),
            P(),
            P(),
            P(None, None, None, "mp"),
            P(None, None, "mp"),
            P(),
            P(),
            P(None, None, None, None, "mp"),
            P(None, None, None, "mp"),
            P(None, None, None, None, "mp"),
        ),
        check_vma=False,
    )
```

```python
import functools
import types

import jax
import jax.numpy as jnp
from jax import lax
from jax.experimental import pallas as pl
from jax.experimental.pallas import tpu as pltpu
from jax.sharding import PartitionSpec as P

D = 640
HEAD_DIM = 80
GROUPS = 32
SIDE = 32
ADAM_STEP = 10
LANES = 128

NORM_EPS = 1e-05
BETA_ONE = 0.9
BETA_TWO = 0.999
ADAM_EPS = 1e-08
DECAY_RATE = 0.01
LEARN_RATE = 0.06
EMA_KEEP = 0.995
INV_ROOT_TWO = 0.7071067811865476
INV_ROOT_TWOPI = 0.3989422804014327

MESH = pl.DeviceIdType.MESH
BF = jnp.bfloat16
F32 = jnp.float32


def adamw_parts(state, grads):
    weight, moment, second, average = (state[0], state[1], state[2], state[3])
    moment = BETA_ONE * moment + (1.0 - BETA_ONE) * grads
    second = BETA_TWO * second + (1.0 - BETA_TWO) * grads * grads
    moment_hat = moment / (1.0 - BETA_ONE**ADAM_STEP)
    second_hat = second / (1.0 - BETA_TWO**ADAM_STEP)
    weight = weight - LEARN_RATE * (
        moment_hat / (jnp.sqrt(second_hat) + ADAM_EPS) + DECAY_RATE * weight
    )
    average = EMA_KEEP * average + (1.0 - EMA_KEEP) * weight
    return (weight, moment, second, average)


def dot_nn(left, right):
    return jnp.dot(left, right, preferred_element_type=F32)


def dot_nt(left, right):
    return lax.dot_general(left, right, (((1,), (1,)), ((), ())), preferred_element_type=F32)


def dot_tn(left, right):
    return lax.dot_general(left, right, (((0,), (0,)), ((), ())), preferred_element_type=F32)


def silu_slope(values):
    sigma = jax.nn.sigmoid(values)
    return sigma * (1.0 + values * (1.0 - sigma))


def layer_norm(values, gain, bias):
    centred = values - jnp.mean(values, axis=1, keepdims=True)
    inv_std = lax.rsqrt(jnp.mean(centred * centred, axis=1, keepdims=True) + NORM_EPS)
    normal = centred * inv_std
    return (normal * gain + bias, normal, inv_std)


def layer_back(grads, normal, inv_std, gain):
    scaled = grads * gain
    return inv_std * (
        scaled
        - jnp.mean(scaled, axis=1, keepdims=True)
        - normal * jnp.mean(scaled * normal, axis=1, keepdims=True)
    )


def ring_chip(place, chips):
    place = lax.rem(place + 2 * chips, chips)
    return jnp.where(place < chips // 2, 2 * place, 2 * (chips - 1 - place) + 1)


def ring_place(chip, chips):
    column = chip // 2
    return jnp.where(lax.rem(chip, 2) == 0, column, chips - 1 - column)


WHOLE = pl.BlockSpec(memory_space=pltpu.VMEM)
VMEM_BYTES = 63 * 1024 * 1024
FACTOR = HEAD_DIM**-0.5
LOG_TWO_E = 1.4426950408889634
HEADS = D // HEAD_DIM
RANK_SQ = 64


def split_low(values):
    high = values.astype(BF)
    return high, (values - high.astype(F32)).astype(BF)


def to_heads(slots, values):
    blank = jnp.zeros((values.shape[0], LANES - HEAD_DIM), BF)
    for head in range(HEADS):
        part = values[:, HEAD_DIM * head : HEAD_DIM * (head + 1)]
        slots[head] = jnp.concatenate([part, blank], axis=1)


def from_heads(slots):
    return jnp.concatenate([slots[head][:, :HEAD_DIM] for head in range(HEADS)], axis=1)


def partner_barrier():
    index = lax.axis_index("dp")
    where = (index + 1 - 2 * lax.rem(index, 2), lax.axis_index("mp"))
    barrier = pltpu.get_barrier_semaphore()
    pl.semaphore_signal(barrier, inc=1, device_id=where, device_id_type=MESH)
    return lax.rem(index, 2), where, barrier


def send_to(where, src, dst, sems, slot):
    return pltpu.make_async_remote_copy(
        src_ref=src,
        dst_ref=dst,
        send_sem=sems.at[0, slot],
        recv_sem=sems.at[1, slot],
        device_id=where,
        device_id_type=MESH,
    )


TEXT = 77


def cross_probs(query, keys):
    scores = dot_nt(query, keys)
    column = lax.broadcasted_iota(jnp.int32, scores.shape, 1)
    scores = jnp.where(column < TEXT, scores, -1e30)
    top = jnp.max(scores, axis=1, keepdims=True)
    expo = jnp.exp2((scores - top) * (FACTOR * LOG_TWO_E))
    return expo * (1.0 / jnp.sum(expo, axis=1, keepdims=True))


def attention_back_kernel(
    g2_ref,
    h_ref,
    h2_ref,
    vec_ref,
    wq_ref,
    left_ref,
    right_ref,
    wkv_ref,
    wso_ref,
    wcq_ref,
    wco_ref,
    q_ref,
    kv_ref,
    o_ref,
    lse_ref,
    cq_ref,
    ckv_ref,
    rows_ref,
    cols_ref,
    image_ref,
    g0_ref,
    right_out,
    left_out,
    block_ref,
    wide,
    dout,
    cot,
    delta,
    dq_acc,
    dkv_acc,
    give,
    take,
    sems,
):
    core, where, barrier = partner_barrier()
    side = where[1]
    share = h_ref.shape[0]
    diagonal = (where[0], 1 - side)
    pl.semaphore_signal(barrier, inc=1, device_id=diagonal, device_id_type=MESH)
    pl.semaphore_wait(barrier, 2)
    home = core == side
    out_copy = remote(image_ref, block_ref, diagonal, sems, 1)

    @pl.when(home)
    def _():
        block_ref[...] = image_ref[...]

    @pl.when(jnp.logical_not(home))
    def _():
        out_copy.start()

    dco = dot_nn(g2_ref[...].astype(BF), wco_ref[...]).astype(BF)
    to_heads(dout, dco)

    def cross_head(head, carry):
        probs = cross_probs(cq_ref[head], ckv_ref[0, head])
        dprobs = dot_nt(dout[head], ckv_ref[1, head])
        shift = jnp.sum(dprobs * probs, axis=1, keepdims=True)
        dscores = (probs * (dprobs - shift)).astype(BF)
        dout[head] = (dot_nn(dscores, ckv_ref[0, head]) * FACTOR).astype(BF)
        return carry

    lax.fori_loop(0, HEADS, cross_head, 0)
    gain = 1.0 + vec_ref[5:6, :]
    _, normal, inv = layer_norm(h2_ref[...], gain, vec_ref[6:7, :])
    cot[...] = g2_ref[...] + layer_back(
        dot_nt(from_heads(dout), wcq_ref[...]), normal, inv, gain
    )
    dso = dot_nn(cot[...].astype(BF), wso_ref[...]).astype(BF)
    to_heads(dout, dso)
    prod = dso.astype(F32) * o_ref[...].astype(F32)
    head_row = lax.broadcasted_iota(jnp.int32, (HEADS, D), 0)
    head_col = lax.broadcasted_iota(jnp.int32, (HEADS, D), 1)
    low_edge = head_row * HEAD_DIM
    mark = jnp.where((head_col >= low_edge) & (head_col < low_edge + HEAD_DIM), 1.0, 0.0).astype(BF)
    high, rest = split_low(prod)
    delta[...] = dot_nt(mark, high) + dot_nt(mark, rest)
    for turn in range(2):
        half = core if turn == 1 else 1 - core
        span = pl.ds(pl.multiple_of(half * share, share), share)

        def one_head(head, carry, turn=turn, span=span):
            keys = kv_ref[0, head, span, :]
            vals = kv_ref[1, head, span, :]
            query = q_ref[head]
            grad = dout[head]
            scores = dot_nt(keys, query)
            probs = jnp.exp2(scores * (FACTOR * LOG_TWO_E) - lse_ref[pl.ds(head, 1), :])
            dprobs = dot_nt(vals, grad)
            dscores = (probs * (dprobs - delta[pl.ds(head, 1), :])).astype(BF)
            dval = dot_nn(probs.astype(BF), grad)
            dkey = dot_nn(dscores, query) * FACTOR
            dquery = dot_tn(keys, dscores)
            if turn == 0:
                dq_acc[head] = dquery
                give[0, head] = dkey.astype(BF)
                give[1, head] = dval.astype(BF)
            else:
                dq_acc[head] += dquery
                dkv_acc[0, head] = dkey
                dkv_acc[1, head] = dval
            return carry

        lax.fori_loop(0, HEADS, one_head, 0)
        if turn == 0:
            copy = send_to(where, give, take, sems, 0)
            copy.start()
    for head in range(HEADS):
        dout[head] = (dq_acc[head].T * FACTOR).astype(BF)
    dq = from_heads(dout)
    gain = 1.0 + vec_ref[3:4, :]
    norm, normal, inv = layer_norm(h_ref[...], gain, vec_ref[4:5, :])
    low = norm.astype(BF)
    wide[:D, :] = wq_ref[...]
    wide[D:, :] = right_ref[...]
    back = dot_nt(dq, wide[...])
    low_rank = back[:, D:].astype(BF)
    outer = dot_tn(dot_nn(low, left_ref[...]).astype(BF), dq)
    one, two = factor_rows(outer, rows_ref[0:8, :], rows_ref[8:16, :])
    right_out[0] = one
    right_out[1] = two
    one, two = factor_rows(dot_tn(low_rank, low), cols_ref[0], cols_ref[1])
    left_out[0] = one
    left_out[1] = two
    total = back[:, :D] + dot_nt(low_rank, left_ref[...])
    copy.wait()
    for part in range(2):
        for head in range(HEADS):
            dout[head] = (dkv_acc[part, head] + take[part, head].astype(F32)).astype(BF)
        total += dot_nt(from_heads(dout), wkv_ref[part])
    g0_ref[...] = cot[...] + layer_back(total, normal, inv, gain)

    @pl.when(jnp.logical_not(home))
    def _():
        out_copy.wait()


def attention_back(*operands):
    share = operands[0].shape[0]
    return pl.pallas_call(
        attention_back_kernel,
        out_shape=[
            jax.ShapeDtypeStruct((share, D), F32),
            jax.ShapeDtypeStruct((2, 8, D), F32),
            jax.ShapeDtypeStruct((2, 8, D), F32),
            jax.ShapeDtypeStruct((share, D), BF),
        ],
        in_specs=[WHOLE] * 20,
        out_specs=[WHOLE] * 4,
        scratch_shapes=[
            pltpu.VMEM((D + RANK_SQ, D), BF),
            pltpu.VMEM((HEADS, share, LANES), BF),
            pltpu.VMEM((share, D), F32),
            pltpu.VMEM((HEADS, share), F32),
            pltpu.VMEM((HEADS, LANES, share), F32),
            pltpu.VMEM((2, HEADS, share, LANES), F32),
            pltpu.VMEM((2, HEADS, share, LANES), BF),
            pltpu.VMEM((2, HEADS, share, LANES), BF),
            pltpu.SemaphoreType.DMA((2, 2)),
        ],
        compiler_params=pltpu.CompilerParams(
            collective_id=4, has_side_effects=True, vmem_limit_bytes=VMEM_BYTES
        ),
        name="attention_back",
    )(*operands)


class Ring:
    def __init__(self, chips, ring_sems, core_sems, side_sems, own_sems):
        self.chips = chips
        self.half = chips // 2
        index = lax.axis_index("dp")
        self.plane = lax.axis_index("mp")
        self.core = lax.rem(index, 2)
        self.place = ring_place(index // 2, chips)
        self.right = ring_chip(self.place + 1, chips) * 2 + self.core
        self.left = ring_chip(self.place - 1, chips) * 2 + self.core
        self.index = index
        self.partner = index + 1 - 2 * self.core
        self.ring_sems, self.core_sems = ring_sems, core_sems
        self.side_sems, self.own_sems = side_sems, own_sems
        self.pieces = []

    def add(self, source, target, via=None, turn=0):
        self.pieces.append((source, target, via, turn))
        return len(self.pieces) - 1

    def last(self, which):
        turn = self.pieces[which][3]
        return (self.half - turn, self.half - 1 + turn)

    def spot(self, which, hop):
        return self.pieces[which][1](ring_chip(self.place - hop, self.chips) * 2 + self.core)

    def ring_copy(self, which, way, step):
        sign = 1 if way == 0 else -1
        spot = self.spot(which, sign * (step - 1))
        return pltpu.make_async_remote_copy(
            src_ref=self.pieces[which][0] if step == 1 else spot,
            dst_ref=spot,
            send_sem=self.ring_sems.at[0, way, which, step - 1],
            recv_sem=self.ring_sems.at[1, way, which, step - 1],
            device_id=(self.right if way == 0 else self.left, self.plane),
            device_id_type=MESH,
        )

    def core_copy(self, which, slot, hop):
        spot = self.spot(which, hop)
        return pltpu.make_async_remote_copy(
            src_ref=self.pieces[which][0] if slot == 0 else spot,
            dst_ref=spot,
            send_sem=self.core_sems.at[0, which, slot],
            recv_sem=self.core_sems.at[1, which, slot],
            device_id=(self.partner, self.plane),
            device_id_type=MESH,
        )

    def side_copy(self, which, slot, hop):
        spot = self.spot(which, hop)
        return pltpu.make_async_remote_copy(
            src_ref=spot,
            dst_ref=spot,
            send_sem=self.side_sems.at[0, which, slot],
            recv_sem=self.side_sems.at[1, which, slot],
            device_id=(self.index, 1 - self.plane),
            device_id_type=MESH,
        )

    def own_copy(self, which):
        return pltpu.make_async_copy(
            self.pieces[which][0], self.spot(which, 0), self.own_sems.at[which]
        )

    def on_ring(self, which, inside, outside=None):
        via = self.pieces[which][2]
        if via is None:
            inside()
            return
        pl.when(self.plane == via)(inside)
        if outside is not None:
            pl.when(self.plane != via)(outside)

    def begin(self, which):
        def inside():
            self.ring_copy(which, 0, 1).start()
            self.ring_copy(which, 1, 1).start()

        self.on_ring(which, inside)
        self.core_copy(which, 0, 0).start()
        self.own_copy(which).start()

    def event(self, which, way, step):
        slot = step if way == 0 else self.last(which)[0] + step
        hop = step if way == 0 else -step

        def inside():
            self.ring_copy(which, way, step).wait_recv()
            if step < self.last(which)[way]:
                self.ring_copy(which, way, step + 1).start()
            if self.pieces[which][2] is not None:
                self.side_copy(which, slot, hop).start()
            self.core_copy(which, slot, hop).start()

        self.on_ring(which, inside)

    def relay(self, which, way, step):
        slot = step if way == 0 else self.last(which)[0] + step
        hop = step if way == 0 else -step

        def outside():
            self.side_copy(which, slot, hop).wait_recv()
            self.core_copy(which, slot, hop).start()

        self.on_ring(which, lambda: None, outside)

    def plan(self, groups):
        rounds = []
        for number, group in enumerate(groups):
            for step in range(1, self.half + 1):
                rounds.append(
                    [
                        (number, which, way, step)
                        for which in group
                        for way in (0, 1)
                        if step <= self.last(which)[way]
                    ]
                )
        events, late = [], [[], []]
        for turn in rounds + [[], []]:
            events += [(False,) + e for e in turn] + [(True,) + e for e in late.pop(0)]
            late.append([e for e in turn if self.pieces[e[1]][2] is not None])
        return events

    def arrived(self, which):
        for slot in range(self.chips):
            self.core_copy(which, slot, 0).wait_recv()
        self.own_copy(which).wait()

    def drain(self, which):
        last = self.last(which)

        def inside():
            for way in (0, 1):
                for step in range(1, last[way] + 1):
                    self.ring_copy(which, way, step).wait_send()
            if self.pieces[which][2] is not None:
                for slot in range(1, self.chips):
                    self.side_copy(which, slot, 0).wait_send()

        self.on_ring(which, inside)
        for slot in range(self.chips):
            self.core_copy(which, slot, 0).wait_send()


def remote(src, dst, where, sems, slot):
    return pltpu.make_async_remote_copy(
        src_ref=src,
        dst_ref=dst,
        send_sem=sems.at[0, slot],
        recv_sem=sems.at[1, slot],
        device_id=where,
        device_id_type=MESH,
    )


MEMBERS = D // GROUPS


def group_mean(column):
    column = jnp.broadcast_to(column, (8, D))
    lane = lax.broadcasted_iota(jnp.int32, (8, D), 1)
    first = lane == 0
    for group in range(1, GROUPS):
        first = first | (lane == group * MEMBERS)

    def shift(values, count):
        return pltpu.roll(values, count % D, 1)

    two = column + shift(column, -1)
    four = two + shift(two, -2)
    eight = four + shift(four, -4)
    whole = eight + shift(eight, -8) + shift(four, -16)
    whole = jnp.where(first, whole, 0.0)
    two = whole + shift(whole, 1)
    four = two + shift(two, 2)
    eight = four + shift(four, 4)
    spread = eight + shift(eight, 8) + shift(four, 16)
    return spread[0:1, :] * (1.0 / MEMBERS)


def col_mean(values):
    return jnp.sum(values, axis=0, keepdims=True) * (1.0 / values.shape[0])


def side_by_side(wide, values, order):
    rows = values.shape[0]
    column = lax.broadcasted_iota(jnp.int32, (rows, D), 0) & (SIDE - 1)
    before = jnp.where(column == 0, 0.0, pltpu.roll(values, 1, 0)).astype(BF)
    after = jnp.where(column == SIDE - 1, 0.0, pltpu.roll(values, rows - 1, 0)).astype(BF)
    parts = (before, values.astype(BF), after)
    for spot, part in enumerate(order):
        wide[:, spot * D : (spot + 1) * D] = parts[part]


def swap_edges(act, edge_send, edge_got, core, partner, sems, slot):
    share = act.shape[0] - 2 * SIDE
    start = pl.multiple_of(share - (share - SIDE) * core, SIDE)
    edge_send[...] = act[pl.ds(start, SIDE), :].astype(BF)
    copy = remote(edge_send, edge_got, partner, sems, slot)
    copy.start()
    copy.wait()
    border = edge_got[...].astype(F32)
    top = (core == 1).astype(F32)
    act[:SIDE, :] = border * top
    act[SIDE + share :, :] = border * (1.0 - top)


SHARDS = ("one", "time", "two", "q", "kv", "so", "cq", "ckv", "co", "ff")


def call_named(body, name, ins, outs, scratch, collective):
    anywhere = pl.BlockSpec(memory_space=pl.ANY)
    fetched = [n for n, i in ins.items() if i[1] is None]
    flushed = [n for n, o in outs.items() if o[2] is None]
    scratch = dict(scratch)
    for n in fetched:
        scratch[n] = pltpu.VMEM(ins[n][0].shape, ins[n][0].dtype)
    for n in flushed:
        scratch[n] = pltpu.VMEM(outs[n][0], outs[n][1])
    scratch["fetch_sems"] = pltpu.SemaphoreType.DMA((max(len(fetched), 1),))
    scratch["flush_sems"] = pltpu.SemaphoreType.DMA((max(len(flushed), 1),))
    held = lambda n, spec: "hbm_" + n if spec is None else n
    names = [held(n, i[1]) for n, i in ins.items()] + [held(n, o[2]) for n, o in outs.items()]
    names += list(scratch)

    def kernel(*refs):
        r = types.SimpleNamespace(**dict(zip(names, refs)))
        loads, stores = {}, []
        for slot, n in enumerate(fetched):
            copy = pltpu.make_async_copy(
                getattr(r, "hbm_" + n), getattr(r, n), r.fetch_sems.at[slot]
            )
            copy.start()
            loads[n] = copy

        def need(*wanted):
            for n in wanted:
                if n in loads:
                    loads.pop(n).wait()

        def flush(*done):
            for n in done:
                copy = pltpu.make_async_copy(
                    getattr(r, n), getattr(r, "hbm_" + n), r.flush_sems.at[flushed.index(n)]
                )
                copy.start()
                stores.append(copy)

        r.need, r.flush = need, flush
        body(r)
        need(*fetched)
        for copy in stores:
            copy.wait()

    results = pl.pallas_call(
        kernel,
        out_shape=[jax.ShapeDtypeStruct(o[0], o[1]) for o in outs.values()],
        in_specs=[i[1] or anywhere for i in ins.values()],
        out_specs=[o[2] or anywhere for o in outs.values()],
        scratch_shapes=list(scratch.values()),
        compiler_params=pltpu.CompilerParams(
            collective_id=collective, has_side_effects=True, vmem_limit_bytes=VMEM_BYTES
        ),
        name=name,
    )(*[i[0] for i in ins.values()])
    return types.SimpleNamespace(**dict(zip(outs, results)))


def expand_left(left, which):
    row = lax.broadcasted_iota(jnp.int32, (8, RANK_SQ), 0)
    col = lax.broadcasted_iota(jnp.int32, (8, RANK_SQ), 1)
    chosen = (col >> 3) if which == 0 else (col & 7)
    mark = jnp.where(row == chosen, 1.0, 0.0)
    return lax.dot_general(
        left,
        mark,
        (((0,), (0,)), ((), ())),
        precision=lax.Precision.HIGHEST,
        preferred_element_type=F32,
    )


def factor_rows(outer, first, second):
    grad_first = [
        jnp.sum(outer[8 * r : 8 * r + 8] * second, axis=0, keepdims=True) for r in range(8)
    ]
    grad_second = sum(outer[8 * r : 8 * r + 8] * first[r : r + 1] for r in range(8))
    return jnp.concatenate(grad_first, axis=0), grad_second


def forward_body(chips, gathers, r):
    ring = Ring(chips, r.ring_sems, r.pair_sems, r.over_sems, r.own_sems)
    core, side = ring.core, ring.plane
    neighbour = (ring.index, 1 - side)
    partner = (ring.partner, side)
    diagonal = (ring.partner, 1 - side)
    home = core == side
    away = jnp.logical_not(home)
    barrier = pltpu.get_barrier_semaphore()
    others = [partner, neighbour, diagonal]
    if gathers:
        others += [(ring.right, side), (ring.left, side)]
    for where in others:
        pl.semaphore_signal(barrier, inc=1, device_id=where, device_id_type=MESH)
    pl.semaphore_wait(barrier, len(others))

    shard = {name: getattr(r, "in_" + name) for name in SHARDS} if gathers else {}
    got = {name: getattr(r, "got_" + name) for name in shard}
    joined = {name: getattr(r, "wide_" + name) for name in shard}
    full = {name: getattr(r, "full_" + name) for name in SHARDS}
    side_copies = {}
    for slot, name in enumerate(shard):
        if name != "one":
            side_copies[name] = remote(
                getattr(r, "hbm_in_" + name), got[name], neighbour, r.side_sems, slot
            )
    first_copies = []
    if gathers:
        for u in range(3):
            part = slice(3 * u, 3 * u + 3)
            copy = remote(
                r.hbm_in_one.at[part], got["one"].at[part], neighbour, r.first_sems, u
            )
            copy.start()
            first_copies.append(copy)
    core_copies = {}
    for slot, name in enumerate(("lat", "emb", "text", "scale")):
        source = r.scale if name == "scale" else getattr(r, "hbm_" + name)
        core_copies[name] = remote(source, getattr(r, "got_" + name), partner, r.core_sems, slot)
    core_copies["lat"].start()
    core_copies["emb"].start()
    flat = ("split", "bias", "qr", "ur")
    for slot, name in enumerate(flat):
        side_copies["f_" + name] = remote(
            getattr(r, "hbm_" + name),
            getattr(r, "got_" + name),
            neighbour,
            r.side_sems,
            len(SHARDS) + slot,
        )
    core_copies["text"].start()

    def send(*names):
        for name in names:
            side_copies[name].start()

    if gathers:
        send("time", "two")
    send("f_split", "f_qr")

    def join(name, first=0, count=None):
        r.need("in_" + name)
        if count is None:
            side_copies[name].wait_recv()
        mine, theirs, out = shard[name], got[name], joined[name]
        for lead in range(first, first + (count or mine.shape[0])):

            @pl.when(side == 0)
            def _():
                out[lead] = jnp.concatenate([mine[lead], theirs[lead]], axis=1)

            @pl.when(side == 1)
            def _():
                out[lead] = jnp.concatenate([theirs[lead], mine[lead]], axis=1)

    def piece(name, start, size, via=None, turn=0, first=0, count=None):
        rows = shard[name].shape[1]
        count = joined[name].shape[2] if count is None else count

        def target(owner):
            at = pl.multiple_of(owner * rows, 8)
            return full[name].at[start : start + size, pl.ds(at, rows), first : first + count]

        source = joined[name].at[start : start + size, :, first : first + count]
        return ring.add(source, target, via, turn)

    def taps(name):
        return [piece(name, 0, 3, 0, 0), piece(name, 3, 3, 1, 0), piece(name, 6, 3, None, 1)]

    groups = []
    if gathers:
        quarter = joined["ff"].shape[2] // 4
        groups = [
            [piece("one", 3 * u, 3, None, u % 2) for u in range(3)],
            [piece("time", 0, 1)] + taps("two"),
            [
                piece("q", 0, 1),
                piece("kv", 0, 1, 0, 0),
                piece("kv", 1, 1, 1, 0),
                piece("so", 0, 1, None, 1),
            ],
            [
                piece("cq", 0, 1),
                piece("ckv", 0, 1, 0, 0),
                piece("ckv", 1, 1, 1, 0),
                piece("co", 0, 1, None, 1),
            ],
        ]
        for part in range(4):
            first = part * quarter
            groups.append(
                [
                    piece("ff", 0, 1, 0, 0, first, quarter),
                    piece("ff", 1, 1, 1, 0, first, quarter),
                    piece("ff", 2, 1, None, 1, first, quarter),
                ]
            )
    events = ring.plan(groups)
    begun = {}

    def begin(number):
        if number < len(groups) and number not in begun:
            begun[number] = True
            for which in groups[number]:
                ring.begin(which)

    def poll(limit=4):
        while events and limit > 0:
            relayed, number, which, way, step = events.pop(0)
            if relayed:
                ring.relay(which, way, step)
                continue
            limit -= 1
            ring.event(which, way, step)
            if step == ring.half - 1 and (which, way) == (groups[number][-1], 1):
                begin(number + 2)

    def poll_group(number):
        while any(e[1] <= number for e in events):
            poll(1)

    def arrived(number, position):
        if gathers:
            ring.arrived(groups[number][position])

    def load(name, start, size, target, slot):
        copy = pltpu.make_async_copy(
            full[name].at[start : start + size] if size else full[name].at[start],
            target,
            r.load_sems.at[slot],
        )
        copy.start()
        return copy

    r.need("lat")
    core_copies["lat"].wait_recv()

    @pl.when(home)
    def _():
        r.image[...] = r.lat[...]

    @pl.when(away)
    def _():
        r.image[...] = r.got_lat[...]

    if gathers:
        begun[0] = True
        for u in range(3):
            first_copies[u].wait_recv()
            join("one", 3 * u, 3)
            ring.begin(groups[0][u])
        send("q", "kv", "so", "cq", "ckv", "co")
    share = r.image.shape[0] // 2
    mine = pl.ds(pl.multiple_of(core * share, share), share)
    r.need("vec")
    pixels = r.image[...].astype(F32)
    mean_one = group_mean(col_mean(pixels))
    centred = pixels - mean_one
    inv_one = lax.rsqrt(group_mean(col_mean(centred * centred)) + NORM_EPS)
    slope = inv_one * (1.0 + r.vec[0:1, :])

    def first_act(values):
        pre = (values.astype(F32) - mean_one) * slope + r.vec[1:2, :]
        return pre * jax.nn.sigmoid(pre)

    r.img[...] = r.image[mine, :]
    r.flush("img")
    r.act[SIDE : SIDE + share, :] = first_act(r.image[mine, :])
    border = first_act(r.image[pl.ds(pl.multiple_of(share - SIDE * core, SIDE), SIDE), :])
    top = (core == 1).astype(F32)
    r.act[:SIDE, :] = border * top
    r.act[SIDE + share :, :] = border * (1.0 - top)
    side_by_side(r.wide, r.act[...], (0, 1, 2))
    if gathers:
        join("time")
        join("two")
        begin(1)
        send("ff")
    send("f_bias", "f_ur")
    poll(6)
    for name in SHARDS[3:-1] if gathers else ():
        join(name)
    poll(6)
    if gathers:
        join("ff")

    r.need(*flat, "ql", "ul", "step", "group", "step_weights", "group_weights", "cot", "emb", "text")
    for name in flat:
        side_copies["f_" + name].wait_recv()
        own_part, got_part, whole = (
            getattr(r, name),
            getattr(r, "got_" + name),
            getattr(r, "all_" + name),
        )

        @pl.when(side == 0)
        def _():
            whole[...] = jnp.concatenate([own_part[...], got_part[...]], axis=1)

        @pl.when(side == 1)
        def _():
            whole[...] = jnp.concatenate([got_part[...], own_part[...]], axis=1)

    for row in range(8):
        rows = slice(8 * row, 8 * row + 8)
        r.zq[rows, :] = (r.all_qr[row : row + 1, :] * r.all_qr[8:16, :]).astype(BF)
        for part in range(2):
            base = 16 * part
            r.zu[part, rows, :] = (
                r.all_ur[base + row : base + row + 1, :] * r.all_ur[base + 8 : base + 16, :]
            ).astype(BF)
    poll()
    for left, pair in ((r.ql, r.yq), (r.ul, r.yu)):
        pair[...] = (expand_left(left[0], 0) * expand_left(left[1], 1)).astype(BF)

    poll()

    def chosen(table, spot):
        lane = lax.broadcasted_iota(jnp.int32, table.shape, 1)
        return jnp.sum(jnp.where(lane == spot[...], table[...], 0.0), axis=1, keepdims=True)

    scale = chosen(r.step_weights, r.step) * chosen(r.group_weights, r.group)
    r.scale[...] = jnp.broadcast_to(scale, r.scale.shape)
    core_copies["scale"].start()
    cot_copy = remote(r.hbm_cot, r.all_cot, diagonal, r.core_sems, 6)

    @pl.when(home)
    def _():
        r.all_cot[...] = r.cot[...]

    @pl.when(away)
    def _():
        cot_copy.start()

    core_copies["emb"].wait_recv()
    core_copies["text"].wait_recv()
    core_copies["scale"].wait_recv()
    own = home.astype(F32)
    r.scale_out[...] = r.scale[...] * own + r.got_scale[...] * (1.0 - own)
    count = r.text.shape[0]

    @pl.when(home)
    def _():
        r.text_all[:count, :] = r.text[...]

    @pl.when(away)
    def _():
        r.text_all[:count, :] = r.got_text[...]

    r.text_all[count:, :] = jnp.zeros((LANES - count, r.text.shape[1]), BF)
    poll_group(0)

    loads = []
    for u in range(3):
        arrived(0, u)
        loads.append(load("one", 3 * u, 3, r.kernels.at[3 * u : 3 * u + 3], u))
    for u in range(3):
        loads[u].wait()
        term = dot_nn(
            r.wide[u * SIDE : u * SIDE + share, :],
            r.kernels[3 * u : 3 * u + 3].reshape(3 * D, D),
        )
        if u == 0:
            r.h1[...] = term
        else:
            r.h1[...] += term
        poll()
    while any(e[2] == groups[1][0] for e in events):
        poll(1)
    arrived(1, 0)
    time_load = load("time", 0, 0, r.time_buf, 3)
    time_load.wait()
    embed = r.emb[...] * own + r.got_emb[...] * (1.0 - own)
    embed = (embed * jax.nn.sigmoid(embed)).astype(BF)
    shift = dot_nn(jnp.broadcast_to(embed, (8, embed.shape[1])), r.time_buf[...])[0:1, :]
    inner = r.h1[...] + (r.all_split[0:1, :] + (shift + r.all_split[1:2, :]))
    r.h1[...] = inner
    r.flush("h1")
    poll()
    local_mean = group_mean(col_mean(inner))
    local_dev = inner - local_mean
    local_var = group_mean(col_mean(local_dev * local_dev))
    r.stat_send[0:1, :] = local_mean
    r.stat_send[1:2, :] = local_var
    stat_copy = remote(r.stat_send, r.stat_got, partner, r.core_sems, 4)
    stat_copy.start()
    poll()
    stat_copy.wait()
    other_mean, other_var = r.stat_got[0:1, :], r.stat_got[1:2, :]
    mean_two = 0.5 * (local_mean + other_mean)
    gap = 0.5 * (local_mean - other_mean)
    inv_two = lax.rsqrt(0.5 * (local_var + other_var) + gap * gap + NORM_EPS)
    r.stats[0:1, :] = mean_one
    r.stats[1:2, :] = inv_one
    r.stats[2:3, :] = mean_two
    r.stats[3:4, :] = inv_two
    r.stats[4:8, :] = jnp.zeros((4, D), F32)
    pre = (r.h1[...] - mean_two) * (inv_two * (1.0 + r.all_split[2:3, :])) + r.all_split[3:4, :]
    r.act[SIDE : SIDE + share, :] = pre * jax.nn.sigmoid(pre)
    swap_edges(r.act, r.edge_send, r.edge_got, core, partner, r.core_sems, 5)
    side_by_side(r.wide, r.act[...], (0, 1, 2))
    poll_group(1)

    loads = []
    for u in range(3):
        arrived(1, 1 + u)
        loads.append(load("two", 3 * u, 3, r.kernels.at[3 * u : 3 * u + 3], u))
    for u in range(3):
        loads[u].wait()
        term = None
        for w in range(3):
            part = dot_nt(
                r.wide[u * SIDE : u * SIDE + share, w * D : (w + 1) * D], r.kernels[3 * u + w]
            )
            term = part if term is None else term + part
        if u == 0:
            r.h[...] = term
        else:
            r.h[...] += term
        poll()
    r.h[...] = r.img[...].astype(F32) + (r.h[...] + r.vec[2:3, :])
    r.flush("h")

    poll_group(2)
    loads = []
    for slot, (name, spots, at, size) in enumerate(
        (("kv", (1, 2), 1, 2), ("q", (0,), 0, 1), ("so", (3,), 3, 1))
    ):
        for spot in spots:
            arrived(2, spot)
        loads.append(load(name, 0, size, r.kernels.at[at : at + size], slot))
    norm, _, _ = layer_norm(r.h[...], 1.0 + r.vec[3:4, :], r.vec[4:5, :])
    low = norm.astype(BF)
    loads[0].wait()
    for part in range(2):
        proj = dot_nn(low, r.kernels[1 + part]).astype(BF)
        blank = jnp.zeros((share, LANES - HEAD_DIM), BF)
        for head in range(HEADS):
            span = proj[:, HEAD_DIM * head : HEAD_DIM * (head + 1)]
            r.kv[part, head, mine, :] = jnp.concatenate([span, blank], axis=1)
    kv_copy = remote(r.kv.at[:, :, mine, :], r.kv.at[:, :, mine, :], partner, r.core_sems, 7)
    kv_copy.start()
    loads[1].wait()
    r.ext_act[:, :D] = low
    r.ext_act[:, D:] = dot_nn(low, r.yq[...]).astype(BF)
    r.ext_w[:D, :] = r.kernels[0]
    r.ext_w[D:, :] = r.zq[...]
    to_heads(r.q, dot_nn(r.ext_act[...], r.ext_w[...]).astype(BF))
    kv_copy.wait()
    r.flush("kv", "q")
    poll()
    lane = lax.broadcasted_iota(jnp.int32, (share, LANES), 1)
    r.lse_cols[...] = jnp.zeros_like(r.lse_cols)

    def one_head(head, carry):
        scores = dot_nt(r.q[head], r.kv[0, head])
        peak = jnp.max(scores, axis=1, keepdims=True)
        expo = jnp.exp2((scores - peak) * (FACTOR * LOG_TWO_E))
        total = jnp.sum(expo, axis=1, keepdims=True)
        probs = (expo * (1.0 / total)).astype(BF)
        r.heads[head] = dot_nn(probs, r.kv[1, head]).astype(BF)
        row = peak * (FACTOR * LOG_TWO_E) + jnp.log2(total)
        r.lse_cols[...] = jnp.where(lane == head, row, r.lse_cols[...])
        return carry

    for first in range(0, HEADS, 2):
        lax.fori_loop(first, first + 2, one_head, 0)
        poll()
    r.lse[...] = r.lse_cols[...].T
    merged = from_heads(r.heads)
    r.o[...] = merged
    r.flush("lse", "o")
    loads[2].wait()
    r.h2[...] = r.h[...] + (dot_nt(merged, r.kernels[3]) + r.vec[9:10, :])
    r.flush("h2")

    poll()
    poll_group(3)
    for position in range(4):
        arrived(3, position)
    loads = [
        load("cq", 0, 1, r.kernels.at[4:5], 0),
        load("ckv", 0, 2, r.text_kv, 1),
        load("co", 0, 1, r.kernels.at[5:6], 2),
    ]
    norm, _, _ = layer_norm(r.h2[...], 1.0 + r.vec[5:6, :], r.vec[6:7, :])
    loads[0].wait()
    to_heads(r.cq, dot_nn(norm.astype(BF), r.kernels[4]).astype(BF))
    loads[1].wait()
    for part in range(2):
        to_heads(r.ckv.at[part], dot_nn(r.text_all[...], r.text_kv[part]).astype(BF))

    poll()

    def cross_head(head, carry):
        probs = cross_probs(r.cq[head], r.ckv[0, head])
        r.heads[head] = dot_nn(probs.astype(BF), r.ckv[1, head]).astype(BF)
        return carry

    lax.fori_loop(0, HEADS, cross_head, 0)
    loads[2].wait()
    r.h3[...] = r.h2[...] + (dot_nt(from_heads(r.heads), r.kernels[5]) + r.vec[10:11, :])

    r.flush("cq", "ckv")
    poll()

    gain = 1.0 + r.vec[7:8, :]
    norm, _, _ = layer_norm(r.h3[...], gain, r.vec[8:9, :])
    low = norm.astype(BF)
    r.ext_act[:, :D] = low
    r.ext_act[:, D:] = dot_nn(low, r.yu[...]).astype(BF)

    @pl.when(away)
    def _():
        cot_copy.wait()

    r.cot_low[...] = (r.all_cot[...].astype(F32) * r.scale_out[0:1, 0:1]).astype(BF)
    down_acc = r.act.at[:share, :]
    quarter = full["ff"].shape[2] // 4
    for part in range(4):
        poll_group(4 + part)
        for position in range(3):
            arrived(4 + part, position)
        first = part * quarter
        span = slice(first, first + quarter)
        slots = r.kernels.at[3 * (part % 2) : 3 * (part % 2) + 3]
        copy = pltpu.make_async_copy(full["ff"].at[:, :, span], slots, r.load_sems.at[part])
        copy.start()
        copy.wait()
        for half in range(2):
            cols = slice(half * quarter, (half + 1) * quarter)
            r.ff_wide[:D, cols] = slots[half]
            r.ff_wide[D:, cols] = r.zu[half, :, span]
        mixed = dot_nn(r.ext_act[...], r.ff_wide[...])
        value = mixed[:, :quarter] + r.all_bias[0:1, span]
        gate = mixed[:, quarter:] + r.all_bias[1:2, span]
        cdf = 0.5 * (1.0 + lax.erf(gate * INV_ROOT_TWO))
        gelu = gate * cdf
        slope = cdf + gate * jnp.exp(-0.5 * gate * gate) * INV_ROOT_TWOPI
        poll(3)
        hidden_grad = dot_nn(r.cot_low[...], slots[2])
        r.ff_grads[:, :quarter] = (hidden_grad * gelu).astype(BF)
        r.ff_grads[:, quarter:] = (hidden_grad * value * slope).astype(BF)
        down = dot_nt((value * gelu).astype(BF), slots[2])
        poll(3)
        outer = dot_tn(r.ext_act[:, D:], r.ff_grads[...])
        for half in range(2):
            base = 16 * half
            one, two = factor_rows(
                outer[:, half * quarter : (half + 1) * quarter],
                r.all_ur[base : base + 8, span],
                r.all_ur[base + 8 : base + 16, span],
            )
            r.up_right[0, half, :, span] = one
            r.up_right[1, half, :, span] = two
        back = dot_nt(r.ff_grads[...], r.ff_wide[...])
        if part == 0:
            down_acc[...] = down
            r.back_acc[...] = back
        else:
            down_acc[...] += down
            r.back_acc[...] += back
        poll(3)
    r.flush("up_right")
    r.out_img[...] = (r.h3[...] + (down_acc[...] + r.vec[11:12, :])).astype(BF)
    r.flush("out_img")
    low_rank = r.back_acc[:, D:].astype(BF)
    one, two = factor_rows(dot_tn(low_rank, r.ext_act[:, :D]), r.ul[0], r.ul[1])
    r.up_left[0] = one
    r.up_left[1] = two
    normed_grad = r.back_acc[:, :D] + dot_nt(low_rank, r.yu[...])
    _, normal, inv = layer_norm(r.h3[...], gain, r.vec[8:9, :])
    cot = r.all_cot[...].astype(F32) * r.scale_out[0:1, 0:1]
    r.g2[...] = cot + layer_back(normed_grad, normal, inv, gain)
    r.flush("g2")
    poll(len(events))
    for group in groups:
        for which in group:
            ring.drain(which)
    for copy in first_copies + list(side_copies.values()) + list(core_copies.values()):
        copy.wait_send()


def forward(arrays, shards, full, chips):
    gathers = full is None
    share = arrays["lat"].shape[0] // 2
    anywhere = pl.BlockSpec(memory_space=pl.ANY)
    dma = pltpu.SemaphoreType.DMA
    ins = {name: (arrays[name], None) for name in ("lat", "vec")}
    if gathers:
        ins["in_one"] = (shards[0], None)
    ins.update({name: (value, None) for name, value in arrays.items()})
    text_rows, text_width = arrays["text"].shape
    time_width = arrays["emb"].shape[1]

    def double(name):
        rows, cols = arrays[name].shape
        return (rows, 2 * cols)

    outs = {
        "h": ((share, D), F32, None),
        "h1": ((share, D), F32, None),
        "img": ((share, D), BF, None),
        "stats": ((8, D), F32, WHOLE),
        "h2": ((share, D), F32, None),
        "q": ((HEADS, share, LANES), BF, None),
        "kv": ((2, HEADS, 2 * share, LANES), BF, None),
        "o": ((share, D), BF, None),
        "lse": ((LANES, share), F32, None),
        "cq": ((HEADS, share, LANES), BF, None),
        "ckv": ((2, HEADS, LANES, LANES), BF, None),
        "all_split": (double("split"), F32, WHOLE),
        "all_qr": (double("qr"), F32, WHOLE),
        "yq": ((D, RANK_SQ), BF, WHOLE),
        "zq": ((RANK_SQ, D), BF, WHOLE),
        "out_img": ((share, D), BF, None),
        "g2": ((share, D), F32, None),
        "up_right": ((2, 2, 8, double("ur")[1]), F32, None),
        "up_left": ((2, 8, D), F32, WHOLE),
    }
    scratch = {}
    if gathers:
        for name, value in zip(SHARDS, shards):
            lead, rows, cols = value.shape
            ins["in_" + name] = (value, None)
            outs["full_" + name] = ((lead, rows * chips * 2, 2 * cols), BF, anywhere)
            scratch["got_" + name] = pltpu.VMEM(value.shape, BF)
            scratch["wide_" + name] = pltpu.VMEM((lead, rows, 2 * cols), BF)
    else:
        for name, value in zip(SHARDS, full):
            ins["full_" + name] = (value, anywhere)
    for name in ("lat", "emb", "text", "split", "bias", "qr", "ur"):
        value = arrays[name]
        scratch["got_" + name] = pltpu.VMEM(value.shape, value.dtype)
    pieces = 27 if gathers else 1
    hidden = double("ur")[1]
    scratch.update(
        image=pltpu.VMEM(arrays["lat"].shape, BF),
        kernels=pltpu.VMEM((9, D, D), BF),
        time_buf=pltpu.VMEM((time_width, D), BF),
        text_kv=pltpu.VMEM((2, text_width, D), BF),
        text_all=pltpu.VMEM((LANES, text_width), BF),
        wide=pltpu.VMEM((share + 2 * SIDE, 3 * D), BF),
        act=pltpu.VMEM((share + 2 * SIDE, D), F32),
        scale=pltpu.VMEM((8, LANES), F32),
        got_scale=pltpu.VMEM((8, LANES), F32),
        stat_send=pltpu.VMEM((8, D), F32),
        stat_got=pltpu.VMEM((8, D), F32),
        edge_send=pltpu.VMEM((SIDE, D), BF),
        edge_got=pltpu.VMEM((SIDE, D), BF),
        ext_act=pltpu.VMEM((share, D + RANK_SQ), BF),
        ext_w=pltpu.VMEM((D + RANK_SQ, D), BF),
        heads=pltpu.VMEM((HEADS, share, LANES), BF),
        lse_cols=pltpu.VMEM((share, LANES), F32),
        h3=pltpu.VMEM((share, D), F32),
        all_bias=pltpu.VMEM(double("bias"), F32),
        all_ur=pltpu.VMEM(double("ur"), F32),
        yu=pltpu.VMEM((D, RANK_SQ), BF),
        zu=pltpu.VMEM((2, RANK_SQ, hidden), BF),
        all_cot=pltpu.VMEM((share, D), BF),
        scale_out=pltpu.VMEM((8, LANES), F32),
        cot_low=pltpu.VMEM((share, D), BF),
        ff_wide=pltpu.VMEM((D + RANK_SQ, hidden // 2), BF),
        ff_grads=pltpu.VMEM((share, hidden // 2), BF),
        back_acc=pltpu.VMEM((share, D + RANK_SQ), F32),
        first_sems=dma((2, 3)),
        side_sems=dma((2, len(SHARDS) + 4)),
        core_sems=dma((2, 8)),
        load_sems=dma((4,)),
        ring_sems=dma((2, 2, pieces, chips // 2)),
        pair_sems=dma((2, pieces, chips)),
        over_sems=dma((2, pieces, chips)),
        own_sems=dma((pieces,)),
    )
    return call_named(
        functools.partial(forward_body, chips, gathers), "forward", ins, outs, scratch, 1
    )


class Halving:
    HALVINGS = 3

    def __init__(self, steps, acc, got, out, sems):
        self.acc, self.got, self.out, self.sems, self.steps = acc, got, out, sems, steps
        index = lax.axis_index("dp")
        plane = lax.axis_index("mp")
        core = lax.rem(index, 2)
        chip = index // 2
        self.partners = [((index + 1 - 2 * core, plane), core), ((index, 1 - plane), plane)]
        span = 1
        for _ in range(steps - 2):
            bit = lax.rem(chip // span, 2)
            self.partners.append((((chip + span - 2 * span * bit) * 2 + core, plane), bit))
            span *= 2
        self.offset, self.size, self.base = 0, acc.shape[0], 0
        self.trail = []
        self.flight = None
        self.done = 0

    @classmethod
    def room(cls, rows, steps):
        small = rows >> cls.HALVINGS
        return rows - small + small * (steps - cls.HALVINGS)

    def begin(self):
        self._down(0)

    def _down(self, step):
        where, bit = self.partners[step]
        if step < self.HALVINGS:
            size = self.size // 2
            mine = pl.multiple_of(self.offset + bit * size, 8)
            theirs = pl.multiple_of(self.offset + (1 - bit) * size, 8)
        else:
            size, mine, theirs = self.size, self.offset, self.offset
        copy = remote(
            self.acc.at[pl.ds(theirs, size), :],
            self.got.at[pl.ds(self.base, size), :],
            where,
            self.sems,
            step,
        )
        copy.start()
        self.flight = (copy, mine, size)

    def _up(self, step):
        mine, size, where = self.trail[step]
        part = self.out.at[pl.ds(mine, size), :]
        copy = remote(part, part, where, self.sems, self.steps + step)
        copy.start()
        self.flight = (copy, mine, size)

    def step(self):
        steps, total = self.steps, self.steps + self.HALVINGS
        if self.done >= total:
            return
        copy, mine, size = self.flight
        copy.wait()
        if self.done < steps:
            self.acc[pl.ds(mine, size), :] += self.got[pl.ds(self.base, size), :]
            self.trail.append((mine, size, self.partners[self.done][0]))
            self.offset, self.size = mine, size
            self.base += size
            if self.done + 1 < steps:
                self._down(self.done + 1)
            else:
                self.out[pl.ds(mine, size), :] = self.acc[pl.ds(mine, size), :]
                self._up(self.HALVINGS - 1)
        elif self.done + 1 < total:
            self._up(total - 2 - self.done)
        self.done += 1


def conv_back_kernel(
    steps,
    g0_ref,
    h1_ref,
    img_ref,
    stat_ref,
    split_ref,
    vec_ref,
    up_right_ref,
    up_left_ref,
    query_right_ref,
    query_left_ref,
    ql_state,
    qr_state,
    ul_state,
    ur_state,
    one_ref,
    two_ref,
    grad_ref,
    ql_new,
    ql_copy,
    qr_new,
    qr_copy,
    ul_new,
    ul_copy,
    ur_new,
    ur_copy,
    moments,
    sum_ref,
    one_buf,
    two_buf,
    wide,
    act,
    half_back,
    stat_send,
    stat_got,
    edge_send,
    edge_got,
    acc,
    got,
    half_row,
    load_sems,
    core_sems,
    sum_sems,
    back_sems,
):
    index = lax.axis_index("dp")
    side = lax.axis_index("mp")
    core = lax.rem(index, 2)
    partner = (index + 1 - 2 * core, side)
    neighbour = (index, 1 - side)
    diagonal = (index + 1 - 2 * core, 1 - side)
    share = g0_ref.shape[0]
    loads = []
    for slot, (src, dst) in enumerate(((two_ref, two_buf), (one_ref, one_buf))):
        load = pltpu.make_async_copy(src, dst, load_sems.at[slot])
        load.start()
        loads.append(load)
    total = Halving(steps, acc, got, sum_ref, sum_sems)
    barrier = pltpu.get_barrier_semaphore()
    for where, _ in total.partners:
        pl.semaphore_signal(barrier, inc=1, device_id=where, device_id_type=MESH)
    pl.semaphore_signal(barrier, inc=1, device_id=diagonal, device_id_type=MESH)
    parts = []
    for member in range(2):
        for part in range(2):
            for block in range(up_right_ref.shape[3] // D):
                parts.append(up_right_ref[member, part, :, block * D : (block + 1) * D])
    for ref in (query_right_ref, up_left_ref, query_left_ref):
        parts += [ref[0], ref[1]]
    for spot, part in enumerate(parts):
        acc[8 * spot : 8 * spot + 8, :] = part
    acc[8 * len(parts) :, :] = jnp.zeros((acc.shape[0] - 8 * len(parts), D), F32)
    act[SIDE : SIDE + share, :] = g0_ref[...]
    pl.semaphore_wait(barrier, steps + 1)
    total.begin()
    swap_edges(act, edge_send, edge_got, core, partner, core_sems, 0)
    side_by_side(wide, act[...], (2, 1, 0))
    total.step()
    inner = act.at[SIDE : SIDE + share, :]
    loads[0].wait()
    for u in range(3):
        term = dot_nn(
            wide[u * SIDE : u * SIDE + share, :],
            two_buf[3 * (2 - u) : 3 * (2 - u) + 3].reshape(3 * D, D),
        )
        if u == 0:
            inner[...] = term
        else:
            inner[...] += term
        total.step()
    mean_two, inv_two = stat_ref[2:3, :], stat_ref[3:4, :]
    gain_two = 1.0 + split_ref[2:3, :]
    normal = (h1_ref[...] - mean_two) * inv_two
    scaled = inner[...] * silu_slope(normal * gain_two + split_ref[3:4, :]) * gain_two
    means = pair_means(scaled, normal, stat_send, stat_got, partner, core_sems, 1)
    inner[...] = inv_two * (scaled - means[0] - normal * means[1])
    swap_edges(act, edge_send, edge_got, core, partner, core_sems, 2)
    side_by_side(wide, act[...], (2, 1, 0))
    total.step()
    loads[1].wait()
    for u in range(3):
        term = None
        for spot in range(3):
            part = dot_nt(
                wide[u * SIDE : u * SIDE + share, spot * D : (spot + 1) * D],
                one_buf[3 * (2 - u) + spot],
            )
            term = part if term is None else term + part
        if u == 0:
            inner[...] = term
        else:
            inner[...] += term
        total.step()
    mean_one, inv_one = stat_ref[0:1, :], stat_ref[1:2, :]
    gain_one = 1.0 + vec_ref[0:1, :]
    normal = (img_ref[...].astype(F32) - mean_one) * inv_one
    scaled = inner[...] * silu_slope(normal * gain_one + vec_ref[1:2, :]) * gain_one
    means = pair_means(scaled, normal, stat_send, stat_got, partner, core_sems, 3)
    half_back[...] = (
        g0_ref[...] + inv_one * (scaled - means[0] - normal * means[1])
    ).astype(BF)
    mine = grad_ref.at[pl.ds(pl.multiple_of(core * share, share), share), :]
    home = core == side

    @pl.when(home)
    def _():
        remote(half_back, mine, neighbour, back_sems, core).start()
        pltpu.make_async_copy(half_back, mine, load_sems.at[2]).start()

    @pl.when(jnp.logical_not(home))
    def _():
        remote(half_back, mine, diagonal, back_sems, core).start()
        remote(half_back, mine, partner, back_sems, 2 + core).start()

    for _ in range(2 * steps):
        total.step()

    blocks = up_right_ref.shape[3] // D
    base = 4 * blocks * 8

    def update(state, at, grads):
        return adamw_parts([state[(entry,) + at] for entry in range(4)], grads)

    def sided(values):
        size = values.shape[1] // 2

        @pl.when(side == 0)
        def _():
            half_row[...] = values[:, :size]

        @pl.when(side == 1)
        def _():
            half_row[...] = values[:, size:]

        return half_row[...]

    for member in range(2):
        at = pl.ds(base + 8 * member, 8)
        weight, moment, second, average = update(qr_state, (member,), sided(sum_ref[at, :]))
        qr_new[0, member] = weight
        qr_new[1, member] = average
        qr_copy[member] = weight.astype(BF)
        moments[1, 0, member] = moment
        moments[1, 1, member] = second
        at = pl.ds(base + 16 + 8 * member, 8)
        parts = update(ul_state, (member,), sum_ref[at, :])
        for entry in range(4):
            ul_new[entry, member] = parts[entry]
        ul_copy[member] = parts[0].astype(BF)
        at = pl.ds(base + 32 + 8 * member, 8)
        weight, moment, second, average = update(ql_state, (member,), sum_ref[at, :])
        ql_new[0, member] = weight
        ql_new[1, member] = average
        ql_copy[member] = weight.astype(BF)
        moments[0, 0, member] = sided(moment)
        moments[0, 1, member] = sided(second)
        for part_number in range(2):
            for block in range(blocks // 2):
                row = ((member * 2 + part_number) * blocks + side * (blocks // 2) + block) * 8
                grads = sum_ref[pl.ds(pl.multiple_of(row, 8), 8), :]
                cols = slice(block * D, (block + 1) * D)
                parts = adamw_parts(
                    [ur_state[entry, member, part_number, :, cols] for entry in range(4)], grads
                )
                for entry in range(4):
                    ur_new[entry, member, part_number, :, cols] = parts[entry]
                ur_copy[member, part_number, :, cols] = parts[0].astype(BF)

    def part(which):
        return grad_ref.at[pl.ds(pl.multiple_of(which * share, share), share), :]

    @pl.when(home)
    def _():
        remote(half_back, mine, neighbour, back_sems, core).wait_send()
        pltpu.make_async_copy(half_back, mine, load_sems.at[2]).wait()
        remote(half_back, part(1 - core), partner, back_sems, 3 - core).wait_recv()

    @pl.when(jnp.logical_not(home))
    def _():
        remote(half_back, mine, diagonal, back_sems, core).wait_send()
        remote(half_back, mine, partner, back_sems, 2 + core).wait_send()
        remote(half_back, part(core), neighbour, back_sems, core).wait_recv()
        remote(half_back, part(1 - core), diagonal, back_sems, 1 - core).wait_recv()


def pair_means(scaled, normal, stat_send, stat_got, partner, sems, slot):
    stat_send[0:1, :] = group_mean(col_mean(scaled))
    stat_send[1:2, :] = group_mean(col_mean(scaled * normal))
    copy = remote(stat_send, stat_got, partner, sems, slot)
    copy.start()
    copy.wait()
    both = 0.5 * (stat_send[...] + stat_got[...])
    return both[0:1, :], both[1:2, :]


def conv_back(g0, h1, img, stats, split, vectors, grads, states, one, two, devices):
    share = g0.shape[0]
    steps = devices.bit_length() - 1
    dma = pltpu.SemaphoreType.DMA
    unit = 8 << Halving.HALVINGS
    rows = -(-sum(g.size // D for g in grads) // unit) * unit
    ql, qr, ul, ur = states
    return pl.pallas_call(
        functools.partial(conv_back_kernel, steps),
        out_shape=[
            jax.ShapeDtypeStruct((2 * share, D), BF),
            jax.ShapeDtypeStruct((2,) + ql.shape[1:], F32),
            jax.ShapeDtypeStruct(ql.shape[1:], BF),
            jax.ShapeDtypeStruct((2,) + qr.shape[1:], F32),
            jax.ShapeDtypeStruct(qr.shape[1:], BF),
            jax.ShapeDtypeStruct(ul.shape, F32),
            jax.ShapeDtypeStruct(ul.shape[1:], BF),
            jax.ShapeDtypeStruct(ur.shape, F32),
            jax.ShapeDtypeStruct(ur.shape[1:], BF),
            jax.ShapeDtypeStruct((2, 2) + qr.shape[1:], F32),
        ],
        in_specs=[WHOLE] * 14 + [pl.BlockSpec(memory_space=pl.ANY)] * 2,
        out_specs=[WHOLE] * 10,
        scratch_shapes=[
            pltpu.VMEM((rows, D), F32),
            pltpu.VMEM((9, D, D), BF),
            pltpu.VMEM((9, D, D), BF),
            pltpu.VMEM((share + 2 * SIDE, 3 * D), BF),
            pltpu.VMEM((share + 2 * SIDE, D), F32),
            pltpu.VMEM((share, D), BF),
            pltpu.VMEM((8, D), F32),
            pltpu.VMEM((8, D), F32),
            pltpu.VMEM((SIDE, D), BF),
            pltpu.VMEM((SIDE, D), BF),
            pltpu.VMEM((rows, D), F32),
            pltpu.VMEM((Halving.room(rows, steps), D), F32),
            pltpu.VMEM(qr.shape[2:], F32),
            dma((3,)),
            dma((2, 4)),
            dma((2, steps + Halving.HALVINGS)),
            dma((2, 4)),
        ],
        compiler_params=pltpu.CompilerParams(
            collective_id=5, has_side_effects=True, vmem_limit_bytes=VMEM_BYTES
        ),
        name="conv_back",
    )(g0, h1, img, stats, split, vectors, *grads, *states, one, two)


def shards(
    latents,
    out_grad,
    text_states,
    time_embed,
    group_ids,
    group_weights,
    timesteps,
    step_weights,
    vectors,
    split_vectors,
    up_bias,
    conv_one,
    conv_two,
    time_proj,
    self_query,
    self_kv,
    self_out,
    cross_query,
    cross_kv,
    cross_out,
    ff_up,
    ff_down,
    query_left_state,
    query_right_state,
    up_left_state,
    up_right_state,
):
    devices_dp = lax.axis_size("dp")
    chips = devices_dp // 2
    side = lax.axis_index("mp")

    def join_sides(values):
        other = lax.ppermute(values, "mp", [(0, 1), (1, 0)])
        first = jnp.where(side == 0, values, other)
        second = jnp.where(side == 0, other, values)
        return jnp.concatenate([first, second], axis=-1)

    pieces = [
        conv_one,
        time_proj[None],
        conv_two.transpose(0, 2, 1),
        self_query[None],
        self_kv.transpose(1, 0, 2),
        self_out.T[None],
        cross_query[None],
        cross_kv.transpose(1, 0, 2),
        cross_out.T[None],
        jnp.concatenate([ff_up.transpose(1, 0, 2), ff_down.T[None]], axis=0),
    ]
    gathers = all(piece.shape[1] % 8 == 0 for piece in pieces)
    full = None
    if not gathers:
        full = [lax.all_gather(join_sides(p), "dp", axis=1, tiled=True) for p in pieces]
    query_left_turned = query_left_state.transpose(0, 1, 3, 2)
    up_left_turned = up_left_state.transpose(0, 1, 3, 2)
    up_rows = up_right_state[0].transpose(2, 0, 1, 3)
    arrays = {
        "lat": latents[0],
        "emb": time_embed,
        "text": text_states[0],
        "split": split_vectors,
        "bias": up_bias,
        "qr": query_right_state[0].reshape(-1, query_right_state.shape[-1]),
        "ur": up_rows.reshape(-1, up_rows.shape[-1]),
        "ql": query_left_turned[0],
        "ul": up_left_turned[0],
        "vec": vectors,
        "cot": out_grad[0],
        "step": timesteps[:, None],
        "group": group_ids[:, None],
        "step_weights": step_weights[None],
        "group_weights": group_weights[None],
    }
    fwd = forward(arrays, pieces, full, chips)
    if not gathers:
        w_one, _, w_two_t, w_q, w_kv, w_so_t, w_cq, _, w_co_t, w_ff = full
    else:
        w_one, w_two_t, w_q, w_kv = fwd.full_one, fwd.full_two, fwd.full_q, fwd.full_kv
        w_so_t, w_cq, w_co_t, w_ff = fwd.full_so, fwd.full_cq, fwd.full_co, fwd.full_ff
    grad_up_right, grad_up_left = fwd.up_right, fwd.up_left
    cotangent, grad_query_right, grad_query_left, block_out = attention_back(
        fwd.g2,
        fwd.h,
        fwd.h2,
        vectors,
        w_q[0],
        fwd.yq,
        fwd.zq,
        w_kv,
        w_so_t[0],
        w_cq[0],
        w_co_t[0],
        fwd.q,
        fwd.kv,
        fwd.o,
        fwd.lse,
        fwd.cq,
        fwd.ckv,
        fwd.all_qr,
        query_left_turned[0],
        fwd.out_img,
    )
    block_out = block_out[None]
    (
        latents_grad,
        query_left_new,
        query_left_copy,
        query_right_new,
        query_right_copy,
        up_left_new,
        up_left_copy,
        up_right_new,
        up_right_copy,
        query_moments,
    ) = conv_back(
        cotangent,
        fwd.h1,
        fwd.img,
        fwd.stats,
        fwd.all_split,
        vectors,
        [grad_up_right, grad_up_left, grad_query_right, grad_query_left],
        [
            query_left_turned,
            query_right_state,
            up_left_turned,
            up_right_state.transpose(0, 1, 3, 2, 4),
        ],
        w_one,
        w_two_t,
        devices_dp * 2,
    )
    return (
        block_out,
        latents_grad[None],
        query_left_new.transpose(0, 1, 3, 2),
        query_left_copy.transpose(0, 2, 1),
        query_right_new,
        query_right_copy,
        up_left_new.transpose(0, 1, 3, 2),
        up_left_copy.transpose(0, 2, 1),
        up_right_new.transpose(0, 1, 3, 2, 4),
        up_right_copy.transpose(0, 2, 1, 3),
        query_moments,
    )


def solution(mesh):
    placed = (
        P("dp", None, None),
        P("dp", "mp", None),
        P("dp", None, None),
        P("dp", None),
        P("dp"),
        P(),
        P("dp"),
        P(),
        P(),
        P(None, "mp"),
        P(None, "mp"),
        P(None, "dp", "mp"),
        P(None, "mp", "dp"),
        P("dp", "mp"),
        P("dp", "mp"),
        P("dp", None, "mp"),
        P("mp", "dp"),
        P("dp", "mp"),
        P("dp", None, "mp"),
        P("mp", "dp"),
        P("dp", None, "mp"),
        P("mp", "dp"),
        P(),
        P(None, None, None, "mp"),
        P(),
        P(None, None, None, None, "mp"),
    )
    return jax.shard_map(
        shards,
        mesh=mesh,
        in_specs=placed,
        out_specs=(
            P("dp", "mp", None),
            P("dp", None, None),
            P(),
            P(),
            P(None, None, None, "mp"),
            P(None, None, "mp"),
            P(),
            P(),
            P(None, None, None, None, "mp"),
            P(None, None, None, "mp"),
            P(None, None, None, None, "mp"),
        ),
        check_vma=False,
    )
```

```python
import functools
import types

import jax
import jax.numpy as jnp
from jax import lax
from jax.experimental import pallas as pl
from jax.experimental.pallas import tpu as pltpu
from jax.sharding import PartitionSpec as P

D = 640
HEAD_DIM = 80
GROUPS = 32
SIDE = 32
ADAM_STEP = 10
LANES = 128

NORM_EPS = 1e-05
BETA_ONE = 0.9
BETA_TWO = 0.999
ADAM_EPS = 1e-08
DECAY_RATE = 0.01
LEARN_RATE = 0.06
EMA_KEEP = 0.995
INV_ROOT_TWO = 0.7071067811865476
INV_ROOT_TWOPI = 0.3989422804014327

MESH = pl.DeviceIdType.MESH
BF = jnp.bfloat16
F32 = jnp.float32


def adamw_parts(state, grads):
    weight, moment, second, average = (state[0], state[1], state[2], state[3])
    moment = BETA_ONE * moment + (1.0 - BETA_ONE) * grads
    second = BETA_TWO * second + (1.0 - BETA_TWO) * grads * grads
    moment_hat = moment / (1.0 - BETA_ONE**ADAM_STEP)
    second_hat = second / (1.0 - BETA_TWO**ADAM_STEP)
    weight = weight - LEARN_RATE * (
        moment_hat / (jnp.sqrt(second_hat) + ADAM_EPS) + DECAY_RATE * weight
    )
    average = EMA_KEEP * average + (1.0 - EMA_KEEP) * weight
    return (weight, moment, second, average)


def dot_nn(left, right):
    return jnp.dot(left, right, preferred_element_type=F32)


def dot_nt(left, right):
    return lax.dot_general(left, right, (((1,), (1,)), ((), ())), preferred_element_type=F32)


def dot_tn(left, right):
    return lax.dot_general(left, right, (((0,), (0,)), ((), ())), preferred_element_type=F32)


def silu_slope(values):
    sigma = jax.nn.sigmoid(values)
    return sigma * (1.0 + values * (1.0 - sigma))


def layer_norm(values, gain, bias):
    centred = values - jnp.mean(values, axis=1, keepdims=True)
    inv_std = lax.rsqrt(jnp.mean(centred * centred, axis=1, keepdims=True) + NORM_EPS)
    normal = centred * inv_std
    return (normal * gain + bias, normal, inv_std)


def layer_back(grads, normal, inv_std, gain):
    scaled = grads * gain
    return inv_std * (
        scaled
        - jnp.mean(scaled, axis=1, keepdims=True)
        - normal * jnp.mean(scaled * normal, axis=1, keepdims=True)
    )


def ring_chip(place, chips):
    place = lax.rem(place + 2 * chips, chips)
    return jnp.where(place < chips // 2, 2 * place, 2 * (chips - 1 - place) + 1)


def ring_place(chip, chips):
    column = chip // 2
    return jnp.where(lax.rem(chip, 2) == 0, column, chips - 1 - column)


WHOLE = pl.BlockSpec(memory_space=pltpu.VMEM)
VMEM_BYTES = 63 * 1024 * 1024
FACTOR = HEAD_DIM**-0.5
LOG_TWO_E = 1.4426950408889634
HEADS = D // HEAD_DIM
RANK_SQ = 64


def split_low(values):
    high = values.astype(BF)
    return high, (values - high.astype(F32)).astype(BF)


def to_heads(slots, values):
    blank = jnp.zeros((values.shape[0], LANES - HEAD_DIM), BF)
    for head in range(HEADS):
        part = values[:, HEAD_DIM * head : HEAD_DIM * (head + 1)]
        slots[head] = jnp.concatenate([part, blank], axis=1)


def from_heads(slots):
    return jnp.concatenate([slots[head][:, :HEAD_DIM] for head in range(HEADS)], axis=1)


def partner_barrier():
    index = lax.axis_index("dp")
    where = (index + 1 - 2 * lax.rem(index, 2), lax.axis_index("mp"))
    barrier = pltpu.get_barrier_semaphore()
    pl.semaphore_signal(barrier, inc=1, device_id=where, device_id_type=MESH)
    return lax.rem(index, 2), where, barrier


def send_to(where, src, dst, sems, slot):
    return pltpu.make_async_remote_copy(
        src_ref=src,
        dst_ref=dst,
        send_sem=sems.at[0, slot],
        recv_sem=sems.at[1, slot],
        device_id=where,
        device_id_type=MESH,
    )


TEXT = 77


def cross_probs(query, keys):
    scores = dot_nt(query, keys)
    column = lax.broadcasted_iota(jnp.int32, scores.shape, 1)
    scores = jnp.where(column < TEXT, scores, -1e30)
    top = jnp.max(scores, axis=1, keepdims=True)
    expo = jnp.exp2((scores - top) * (FACTOR * LOG_TWO_E))
    return expo * (1.0 / jnp.sum(expo, axis=1, keepdims=True))


def attention_back_kernel(
    need,
    g2_ref,
    h_ref,
    h2_ref,
    vec_ref,
    wq_ref,
    left_ref,
    right_ref,
    wkv_ref,
    wso_ref,
    wcq_ref,
    wco_ref,
    q_ref,
    kv_ref,
    o_ref,
    lse_ref,
    cq_ref,
    ckv_ref,
    rows_ref,
    cols_ref,
    image_ref,
    g0_ref,
    right_out,
    left_out,
    block_ref,
    wide,
    dout,
    cot,
    delta,
    dq_acc,
    dkv_acc,
    give,
    take,
    sems,
):
    core, where, barrier = partner_barrier()
    side = where[1]
    share = h_ref.shape[0]
    diagonal = (where[0], 1 - side)
    pl.semaphore_signal(barrier, inc=1, device_id=diagonal, device_id_type=MESH)
    pl.semaphore_wait(barrier, 2)
    home = core == side
    out_copy = remote(image_ref, block_ref, diagonal, sems, 1)
    need("g2", "wco", "cq", "ckv", "wcq", "h2", "vec")
    dco = dot_nn(g2_ref[...].astype(BF), wco_ref[...]).astype(BF)
    to_heads(dout, dco)

    def cross_head(head, carry):
        probs = cross_probs(cq_ref[head], ckv_ref[0, head])
        dprobs = dot_nt(dout[head], ckv_ref[1, head])
        shift = jnp.sum(dprobs * probs, axis=1, keepdims=True)
        dscores = (probs * (dprobs - shift)).astype(BF)
        dout[head] = (dot_nn(dscores, ckv_ref[0, head]) * FACTOR).astype(BF)
        return carry

    lax.fori_loop(0, HEADS, cross_head, 0)
    gain = 1.0 + vec_ref[5:6, :]
    _, normal, inv = layer_norm(h2_ref[...], gain, vec_ref[6:7, :])
    cot[...] = g2_ref[...] + layer_back(
        dot_nt(from_heads(dout), wcq_ref[...]), normal, inv, gain
    )
    need("image")

    @pl.when(home)
    def _():
        block_ref[...] = image_ref[...]

    @pl.when(jnp.logical_not(home))
    def _():
        out_copy.start()

    need("wso", "o")
    dso = dot_nn(cot[...].astype(BF), wso_ref[...]).astype(BF)
    to_heads(dout, dso)
    prod = dso.astype(F32) * o_ref[...].astype(F32)
    head_row = lax.broadcasted_iota(jnp.int32, (HEADS, D), 0)
    head_col = lax.broadcasted_iota(jnp.int32, (HEADS, D), 1)
    low_edge = head_row * HEAD_DIM
    mark = jnp.where((head_col >= low_edge) & (head_col < low_edge + HEAD_DIM), 1.0, 0.0).astype(BF)
    high, rest = split_low(prod)
    delta[...] = dot_nt(mark, high) + dot_nt(mark, rest)
    need("q", "kv", "lse")
    for turn in range(2):
        half = core if turn == 1 else 1 - core
        span = pl.ds(pl.multiple_of(half * share, share), share)

        def one_head(head, carry, turn=turn, span=span):
            keys = kv_ref[0, head, span, :]
            vals = kv_ref[1, head, span, :]
            query = q_ref[head]
            grad = dout[head]
            scores = dot_nt(keys, query)
            probs = jnp.exp2(scores * (FACTOR * LOG_TWO_E) - lse_ref[pl.ds(head, 1), :])
            dprobs = dot_nt(vals, grad)
            dscores = (probs * (dprobs - delta[pl.ds(head, 1), :])).astype(BF)
            dval = dot_nn(probs.astype(BF), grad)
            dkey = dot_nn(dscores, query) * FACTOR
            dquery = dot_tn(keys, dscores)
            if turn == 0:
                dq_acc[head] = dquery
                give[0, head] = dkey.astype(BF)
                give[1, head] = dval.astype(BF)
            else:
                dq_acc[head] += dquery
                dkv_acc[0, head] = dkey
                dkv_acc[1, head] = dval
            return carry

        lax.fori_loop(0, HEADS, one_head, 0)
        if turn == 0:
            copy = send_to(where, give, take, sems, 0)
            copy.start()
    need("h", "wq", "left", "right", "wkv", "rows", "cols")
    for head in range(HEADS):
        dout[head] = (dq_acc[head].T * FACTOR).astype(BF)
    dq = from_heads(dout)
    gain = 1.0 + vec_ref[3:4, :]
    norm, normal, inv = layer_norm(h_ref[...], gain, vec_ref[4:5, :])
    low = norm.astype(BF)
    wide[:D, :] = wq_ref[...]
    wide[D:, :] = right_ref[...]
    back = dot_nt(dq, wide[...])
    low_rank = back[:, D:].astype(BF)
    outer = dot_tn(dot_nn(low, left_ref[...]).astype(BF), dq)
    one, two = factor_rows(outer, rows_ref[0:8, :], rows_ref[8:16, :])
    right_out[0] = one
    right_out[1] = two
    one, two = factor_rows(dot_tn(low_rank, low), cols_ref[0], cols_ref[1])
    left_out[0] = one
    left_out[1] = two
    total = back[:, :D] + dot_nt(low_rank, left_ref[...])
    copy.wait()
    for part in range(2):
        for head in range(HEADS):
            dout[head] = (dkv_acc[part, head] + take[part, head].astype(F32)).astype(BF)
        total += dot_nt(from_heads(dout), wkv_ref[part])
    g0_ref[...] = cot[...] + layer_back(total, normal, inv, gain)

    @pl.when(jnp.logical_not(home))
    def _():
        out_copy.wait()


BACK_OPERANDS = (
    ("g2", "h", "h2", "vec", "wq", "left", "right", "wkv", "wso", "wcq", "wco")
    + ("q", "kv", "o", "lse", "cq", "ckv", "rows", "cols", "image")
)
BACK_FETCHES = (
    ("g2", "wco", "cq", "ckv", "wcq", "h2", "vec", "image", "wso", "o", "q", "kv", "lse")
    + ("h", "wq", "left", "right", "wkv", "rows", "cols")
)


def attention_back(*operands):
    share = operands[0].shape[0]
    given = dict(zip(BACK_OPERANDS, operands))
    outs = {
        "g0": ((share, D), F32, WHOLE),
        "right_grad": ((2, 8, D), F32, WHOLE),
        "left_grad": ((2, 8, D), F32, WHOLE),
        "block": ((share, D), BF, WHOLE),
    }
    scratch = {
        "wide": pltpu.VMEM((D + RANK_SQ, D), BF),
        "dout": pltpu.VMEM((HEADS, share, LANES), BF),
        "cot": pltpu.VMEM((share, D), F32),
        "delta": pltpu.VMEM((HEADS, share), F32),
        "dq_acc": pltpu.VMEM((HEADS, LANES, share), F32),
        "dkv_acc": pltpu.VMEM((2, HEADS, share, LANES), F32),
        "give": pltpu.VMEM((2, HEADS, share, LANES), BF),
        "take": pltpu.VMEM((2, HEADS, share, LANES), BF),
        "sems": pltpu.SemaphoreType.DMA((2, 2)),
    }

    def body(r):
        refs = [getattr(r, n) for n in BACK_OPERANDS + tuple(outs) + tuple(scratch)]
        attention_back_kernel(r.need, *refs)

    ins = {n: (given[n], None) for n in BACK_FETCHES}
    r = call_named(body, "attention_back", ins, outs, scratch, 4)
    return r.g0, r.right_grad, r.left_grad, r.block


class Ring:
    def __init__(self, chips, ring_sems, core_sems, side_sems, own_sems):
        self.chips = chips
        self.half = chips // 2
        index = lax.axis_index("dp")
        self.plane = lax.axis_index("mp")
        self.core = lax.rem(index, 2)
        self.place = ring_place(index // 2, chips)
        self.right = ring_chip(self.place + 1, chips) * 2 + self.core
        self.left = ring_chip(self.place - 1, chips) * 2 + self.core
        self.index = index
        self.partner = index + 1 - 2 * self.core
        self.ring_sems, self.core_sems = ring_sems, core_sems
        self.side_sems, self.own_sems = side_sems, own_sems
        self.pieces = []

    def add(self, source, target, via=None, turn=0):
        self.pieces.append((source, target, via, turn))
        return len(self.pieces) - 1

    def last(self, which):
        turn = self.pieces[which][3]
        return (self.half - turn, self.half - 1 + turn)

    def spot(self, which, hop):
        return self.pieces[which][1](ring_chip(self.place - hop, self.chips) * 2 + self.core)

    def ring_copy(self, which, way, step):
        sign = 1 if way == 0 else -1
        spot = self.spot(which, sign * (step - 1))
        return pltpu.make_async_remote_copy(
            src_ref=self.pieces[which][0] if step == 1 else spot,
            dst_ref=spot,
            send_sem=self.ring_sems.at[0, way, which, step - 1],
            recv_sem=self.ring_sems.at[1, way, which, step - 1],
            device_id=(self.right if way == 0 else self.left, self.plane),
            device_id_type=MESH,
        )

    def core_copy(self, which, slot, hop):
        spot = self.spot(which, hop)
        return pltpu.make_async_remote_copy(
            src_ref=self.pieces[which][0] if slot == 0 else spot,
            dst_ref=spot,
            send_sem=self.core_sems.at[0, which, slot],
            recv_sem=self.core_sems.at[1, which, slot],
            device_id=(self.partner, self.plane),
            device_id_type=MESH,
        )

    def side_copy(self, which, slot, hop):
        spot = self.spot(which, hop)
        return pltpu.make_async_remote_copy(
            src_ref=spot,
            dst_ref=spot,
            send_sem=self.side_sems.at[0, which, slot],
            recv_sem=self.side_sems.at[1, which, slot],
            device_id=(self.index, 1 - self.plane),
            device_id_type=MESH,
        )

    def own_copy(self, which):
        return pltpu.make_async_copy(
            self.pieces[which][0], self.spot(which, 0), self.own_sems.at[which]
        )

    def on_ring(self, which, inside, outside=None):
        via = self.pieces[which][2]
        if via is None:
            inside()
            return
        pl.when(self.plane == via)(inside)
        if outside is not None:
            pl.when(self.plane != via)(outside)

    def begin(self, which):
        def inside():
            self.ring_copy(which, 0, 1).start()
            self.ring_copy(which, 1, 1).start()

        self.on_ring(which, inside)
        self.core_copy(which, 0, 0).start()
        self.own_copy(which).start()

    def event(self, which, way, step):
        slot = step if way == 0 else self.last(which)[0] + step
        hop = step if way == 0 else -step

        def inside():
            self.ring_copy(which, way, step).wait_recv()
            if step < self.last(which)[way]:
                self.ring_copy(which, way, step + 1).start()
            if self.pieces[which][2] is not None:
                self.side_copy(which, slot, hop).start()
            self.core_copy(which, slot, hop).start()

        self.on_ring(which, inside)

    def relay(self, which, way, step):
        slot = step if way == 0 else self.last(which)[0] + step
        hop = step if way == 0 else -step

        def outside():
            self.side_copy(which, slot, hop).wait_recv()
            self.core_copy(which, slot, hop).start()

        self.on_ring(which, lambda: None, outside)

    def plan(self, groups, starts):
        turns = [[] for _ in range(max(starts, default=0) + self.half + 3)]
        for number, group in enumerate(groups):
            for step in range(1, self.half + 1):
                turns[starts[number] + step] += [
                    (number, which, way, step)
                    for which in group
                    for way in (0, 1)
                    if step <= self.last(which)[way]
                ]
        events, late = [], [[], []]
        for at, turn in enumerate(turns):
            events += [(None, g) for g in range(len(groups)) if starts[g] == at and at > 0]
            events += [(False,) + e for e in turn] + [(True,) + e for e in late.pop(0)]
            late.append([e for e in turn if self.pieces[e[1]][2] is not None])
        return events

    def arrived(self, which):
        for slot in range(self.chips):
            self.core_copy(which, slot, 0).wait_recv()
        self.own_copy(which).wait()

    def drain(self, which):
        last = self.last(which)

        def inside():
            for way in (0, 1):
                for step in range(1, last[way] + 1):
                    self.ring_copy(which, way, step).wait_send()
            if self.pieces[which][2] is not None:
                for slot in range(1, self.chips):
                    self.side_copy(which, slot, 0).wait_send()

        self.on_ring(which, inside)
        for slot in range(self.chips):
            self.core_copy(which, slot, 0).wait_send()


def remote(src, dst, where, sems, slot):
    return pltpu.make_async_remote_copy(
        src_ref=src,
        dst_ref=dst,
        send_sem=sems.at[0, slot],
        recv_sem=sems.at[1, slot],
        device_id=where,
        device_id_type=MESH,
    )


MEMBERS = D // GROUPS


def group_mean(column):
    column = jnp.broadcast_to(column, (8, D))
    lane = lax.broadcasted_iota(jnp.int32, (8, D), 1)
    first = lane == 0
    for group in range(1, GROUPS):
        first = first | (lane == group * MEMBERS)

    def shift(values, count):
        return pltpu.roll(values, count % D, 1)

    two = column + shift(column, -1)
    four = two + shift(two, -2)
    eight = four + shift(four, -4)
    whole = eight + shift(eight, -8) + shift(four, -16)
    whole = jnp.where(first, whole, 0.0)
    two = whole + shift(whole, 1)
    four = two + shift(two, 2)
    eight = four + shift(four, 4)
    spread = eight + shift(eight, 8) + shift(four, 16)
    return spread[0:1, :] * (1.0 / MEMBERS)


def col_mean(values):
    return jnp.sum(values, axis=0, keepdims=True) * (1.0 / values.shape[0])


def side_by_side(wide, values, order):
    rows = values.shape[0]
    column = lax.broadcasted_iota(jnp.int32, (rows, D), 0) & (SIDE - 1)
    before = jnp.where(column == 0, 0.0, pltpu.roll(values, 1, 0)).astype(BF)
    after = jnp.where(column == SIDE - 1, 0.0, pltpu.roll(values, rows - 1, 0)).astype(BF)
    parts = (before, values.astype(BF), after)
    for spot, part in enumerate(order):
        wide[:, spot * D : (spot + 1) * D] = parts[part]


def swap_edges(act, edge_send, edge_got, core, partner, sems, slot):
    share = act.shape[0] - 2 * SIDE
    start = pl.multiple_of(share - (share - SIDE) * core, SIDE)
    edge_send[...] = act[pl.ds(start, SIDE), :].astype(BF)
    copy = remote(edge_send, edge_got, partner, sems, slot)
    copy.start()
    copy.wait()
    border = edge_got[...].astype(F32)
    top = (core == 1).astype(F32)
    act[:SIDE, :] = border * top
    act[SIDE + share :, :] = border * (1.0 - top)


SHARDS = ("one", "time", "two", "q", "kv", "so", "cq", "ckv", "co", "ff")


def call_named(body, name, ins, outs, scratch, collective):
    anywhere = pl.BlockSpec(memory_space=pl.ANY)
    fetched = [n for n, i in ins.items() if i[1] is None]
    flushed = [n for n, o in outs.items() if o[2] is None]
    scratch = dict(scratch)
    for n in fetched:
        scratch[n] = pltpu.VMEM(ins[n][0].shape, ins[n][0].dtype)
    for n in flushed:
        scratch[n] = pltpu.VMEM(outs[n][0], outs[n][1])
    scratch["fetch_sems"] = pltpu.SemaphoreType.DMA((max(len(fetched), 1),))
    scratch["flush_sems"] = pltpu.SemaphoreType.DMA((max(len(flushed), 1),))
    held = lambda n, spec: "hbm_" + n if spec is None else n
    names = [held(n, i[1]) for n, i in ins.items()] + [held(n, o[2]) for n, o in outs.items()]
    names += list(scratch)

    def kernel(*refs):
        r = types.SimpleNamespace(**dict(zip(names, refs)))
        loads, stores = {}, []
        for slot, n in enumerate(fetched):
            copy = pltpu.make_async_copy(
                getattr(r, "hbm_" + n), getattr(r, n), r.fetch_sems.at[slot]
            )
            copy.start()
            loads[n] = copy

        def need(*wanted):
            for n in wanted:
                if n in loads:
                    loads.pop(n).wait()

        def flush(*done):
            for n in done:
                copy = pltpu.make_async_copy(
                    getattr(r, n), getattr(r, "hbm_" + n), r.flush_sems.at[flushed.index(n)]
                )
                copy.start()
                stores.append(copy)

        r.need, r.flush = need, flush
        body(r)
        need(*fetched)
        for copy in stores:
            copy.wait()

    results = pl.pallas_call(
        kernel,
        out_shape=[jax.ShapeDtypeStruct(o[0], o[1]) for o in outs.values()],
        in_specs=[i[1] or anywhere for i in ins.values()],
        out_specs=[o[2] or anywhere for o in outs.values()],
        scratch_shapes=list(scratch.values()),
        compiler_params=pltpu.CompilerParams(
            collective_id=collective, has_side_effects=True, vmem_limit_bytes=VMEM_BYTES
        ),
        name=name,
    )(*[i[0] for i in ins.values()])
    return types.SimpleNamespace(**dict(zip(outs, results)))


def expand_left(left, which):
    row = lax.broadcasted_iota(jnp.int32, (8, RANK_SQ), 0)
    col = lax.broadcasted_iota(jnp.int32, (8, RANK_SQ), 1)
    chosen = (col >> 3) if which == 0 else (col & 7)
    mark = jnp.where(row == chosen, 1.0, 0.0)
    return lax.dot_general(
        left,
        mark,
        (((0,), (0,)), ((), ())),
        precision=lax.Precision.HIGHEST,
        preferred_element_type=F32,
    )


def factor_rows(outer, first, second):
    grad_first = [
        jnp.sum(outer[8 * r : 8 * r + 8] * second, axis=0, keepdims=True) for r in range(8)
    ]
    grad_second = sum(outer[8 * r : 8 * r + 8] * first[r : r + 1] for r in range(8))
    return jnp.concatenate(grad_first, axis=0), grad_second


STARTS = (0, 2, 4, 5, 6, 7, 8, 9)


def forward_body(chips, gathers, r):
    ring = Ring(chips, r.ring_sems, r.pair_sems, r.over_sems, r.own_sems)
    core, side = ring.core, ring.plane
    neighbour = (ring.index, 1 - side)
    partner = (ring.partner, side)
    diagonal = (ring.partner, 1 - side)
    home = core == side
    away = jnp.logical_not(home)
    barrier = pltpu.get_barrier_semaphore()
    others = [partner, neighbour, diagonal]
    if gathers:
        others += [(ring.right, side), (ring.left, side)]
    for where in others:
        pl.semaphore_signal(barrier, inc=1, device_id=where, device_id_type=MESH)
    pl.semaphore_wait(barrier, len(others))

    shard = {name: getattr(r, "in_" + name) for name in SHARDS} if gathers else {}
    got = {name: getattr(r, "got_" + name) for name in shard}
    joined = {name: getattr(r, "wide_" + name) for name in shard}
    full = {name: getattr(r, "full_" + name) for name in SHARDS}
    side_copies = {}
    for slot, name in enumerate(shard):
        if name != "one":
            side_copies[name] = remote(
                getattr(r, "hbm_in_" + name), got[name], neighbour, r.side_sems, slot
            )
    first_copies = []
    if gathers:
        for u in range(3):
            part = slice(3 * u, 3 * u + 3)
            copy = remote(
                r.hbm_in_one.at[part], got["one"].at[part], neighbour, r.first_sems, u
            )
            copy.start()
            first_copies.append(copy)
    core_copies = {}
    for slot, name in enumerate(("lat", "emb", "text", "scale")):
        source = r.scale if name == "scale" else getattr(r, "hbm_" + name)
        core_copies[name] = remote(source, getattr(r, "got_" + name), partner, r.core_sems, slot)
    core_copies["lat"].start()
    core_copies["emb"].start()
    flat = ("split", "bias", "qr", "ur")
    for slot, name in enumerate(flat):
        side_copies["f_" + name] = remote(
            getattr(r, "hbm_" + name),
            getattr(r, "got_" + name),
            neighbour,
            r.side_sems,
            len(SHARDS) + slot,
        )
    core_copies["text"].start()

    def send(*names):
        for name in names:
            side_copies[name].start()

    if gathers:
        send("time", "two")
    send("f_split", "f_qr")

    def join(name, first=0, count=None):
        r.need("in_" + name)
        if count is None:
            side_copies[name].wait_recv()
        mine, theirs, out = shard[name], got[name], joined[name]
        for lead in range(first, first + (count or mine.shape[0])):

            @pl.when(side == 0)
            def _():
                out[lead] = jnp.concatenate([mine[lead], theirs[lead]], axis=1)

            @pl.when(side == 1)
            def _():
                out[lead] = jnp.concatenate([theirs[lead], mine[lead]], axis=1)

    def piece(name, start, size, via=None, turn=0, first=0, count=None):
        rows = shard[name].shape[1]
        count = joined[name].shape[2] if count is None else count

        def target(owner):
            at = pl.multiple_of(owner * rows, 8)
            return full[name].at[start : start + size, pl.ds(at, rows), first : first + count]

        source = joined[name].at[start : start + size, :, first : first + count]
        return ring.add(source, target, via, turn)

    def taps(name):
        return [piece(name, 0, 3, 0, 0), piece(name, 3, 3, 1, 0), piece(name, 6, 3, None, 1)]

    groups = []
    if gathers:
        quarter = joined["ff"].shape[2] // 4
        groups = [
            [piece("one", 3 * u, 3, None, u % 2) for u in range(3)],
            [piece("time", 0, 1)] + taps("two"),
            [
                piece("q", 0, 1),
                piece("kv", 0, 1, 0, 0),
                piece("kv", 1, 1, 1, 0),
                piece("so", 0, 1, None, 1),
            ],
            [
                piece("cq", 0, 1),
                piece("ckv", 0, 1, 0, 0),
                piece("ckv", 1, 1, 1, 0),
                piece("co", 0, 1, None, 1),
            ],
        ]
        for part in range(4):
            first = part * quarter
            groups.append(
                [
                    piece("ff", 0, 1, 0, 0, first, quarter),
                    piece("ff", 1, 1, 1, 0, first, quarter),
                    piece("ff", 2, 1, None, 1, first, quarter),
                ]
            )
    events = ring.plan(groups, STARTS[: len(groups)])

    def poll(limit=5):
        while events and limit > 0:
            kind, number, *rest = events.pop(0)
            if kind is None:
                for which in groups[number]:
                    ring.begin(which)
            elif kind:
                ring.relay(*rest)
            else:
                limit -= 1
                ring.event(*rest)

    def poll_group(number):
        while any(e[1] <= number for e in events):
            poll(1)

    def arrived(number, position):
        if gathers:
            ring.arrived(groups[number][position])

    def load(name, start, size, target, slot):
        copy = pltpu.make_async_copy(
            full[name].at[start : start + size] if size else full[name].at[start],
            target,
            r.load_sems.at[slot],
        )
        copy.start()
        return copy

    r.need("lat")
    core_copies["lat"].wait_recv()

    @pl.when(home)
    def _():
        r.image[...] = r.lat[...]

    @pl.when(away)
    def _():
        r.image[...] = r.got_lat[...]

    if gathers:
        for u in range(3):
            first_copies[u].wait_recv()
            join("one", 3 * u, 3)
            ring.begin(groups[0][u])
        send("q", "kv", "so", "cq", "ckv", "co")
    share = r.image.shape[0] // 2
    mine = pl.ds(pl.multiple_of(core * share, share), share)
    r.need("vec")
    pixels = r.image[...].astype(F32)
    mean_one = group_mean(col_mean(pixels))
    centred = pixels - mean_one
    inv_one = lax.rsqrt(group_mean(col_mean(centred * centred)) + NORM_EPS)
    slope = inv_one * (1.0 + r.vec[0:1, :])

    def first_act(values):
        pre = (values.astype(F32) - mean_one) * slope + r.vec[1:2, :]
        return pre * jax.nn.sigmoid(pre)

    r.img[...] = r.image[mine, :]
    r.flush("img")
    r.act[SIDE : SIDE + share, :] = first_act(r.image[mine, :])
    border = first_act(r.image[pl.ds(pl.multiple_of(share - SIDE * core, SIDE), SIDE), :])
    top = (core == 1).astype(F32)
    r.act[:SIDE, :] = border * top
    r.act[SIDE + share :, :] = border * (1.0 - top)
    side_by_side(r.wide, r.act[...], (0, 1, 2))
    if gathers:
        join("time")
        join("two")
        send("ff")
    send("f_bias", "f_ur")
    poll(6)
    for name in SHARDS[3:-1] if gathers else ():
        join(name)
    poll(6)
    if gathers:
        join("ff")

    r.need(*flat, "ql", "ul", "step", "group", "step_weights", "group_weights", "cot", "emb", "text")
    for name in flat:
        side_copies["f_" + name].wait_recv()
        own_part, got_part, whole = (
            getattr(r, name),
            getattr(r, "got_" + name),
            getattr(r, "all_" + name),
        )

        @pl.when(side == 0)
        def _():
            whole[...] = jnp.concatenate([own_part[...], got_part[...]], axis=1)

        @pl.when(side == 1)
        def _():
            whole[...] = jnp.concatenate([got_part[...], own_part[...]], axis=1)

    for row in range(8):
        rows = slice(8 * row, 8 * row + 8)
        r.zq[rows, :] = (r.all_qr[row : row + 1, :] * r.all_qr[8:16, :]).astype(BF)
        for part in range(2):
            base = 16 * part
            r.zu[part, rows, :] = (
                r.all_ur[base + row : base + row + 1, :] * r.all_ur[base + 8 : base + 16, :]
            ).astype(BF)
    poll()
    for left, pair in ((r.ql, r.yq), (r.ul, r.yu)):
        pair[...] = (expand_left(left[0], 0) * expand_left(left[1], 1)).astype(BF)

    poll()

    def chosen(table, spot):
        lane = lax.broadcasted_iota(jnp.int32, table.shape, 1)
        return jnp.sum(jnp.where(lane == spot[...], table[...], 0.0), axis=1, keepdims=True)

    scale = chosen(r.step_weights, r.step) * chosen(r.group_weights, r.group)
    r.scale[...] = jnp.broadcast_to(scale, r.scale.shape)
    core_copies["scale"].start()
    cot_copy = remote(r.hbm_cot, r.all_cot, diagonal, r.core_sems, 6)

    @pl.when(home)
    def _():
        r.all_cot[...] = r.cot[...]

    @pl.when(away)
    def _():
        cot_copy.start()

    core_copies["emb"].wait_recv()
    core_copies["text"].wait_recv()
    core_copies["scale"].wait_recv()
    own = home.astype(F32)
    r.scale_out[...] = r.scale[...] * own + r.got_scale[...] * (1.0 - own)
    count = r.text.shape[0]

    @pl.when(home)
    def _():
        r.text_all[:count, :] = r.text[...]

    @pl.when(away)
    def _():
        r.text_all[:count, :] = r.got_text[...]

    r.text_all[count:, :] = jnp.zeros((LANES - count, r.text.shape[1]), BF)
    poll_group(0)

    loads = []
    for u in range(3):
        arrived(0, u)
        loads.append(load("one", 3 * u, 3, r.kernels.at[3 * u : 3 * u + 3], u))
    for u in range(3):
        loads[u].wait()
        term = dot_nn(
            r.wide[u * SIDE : u * SIDE + share, :],
            r.kernels[3 * u : 3 * u + 3].reshape(3 * D, D),
        )
        if u == 0:
            r.h1[...] = term
        else:
            r.h1[...] += term
        poll()
    while any(len(e) > 2 and e[2] == groups[1][0] for e in events):
        poll(1)
    arrived(1, 0)
    time_load = load("time", 0, 0, r.time_buf, 3)
    time_load.wait()
    embed = r.emb[...] * own + r.got_emb[...] * (1.0 - own)
    embed = (embed * jax.nn.sigmoid(embed)).astype(BF)
    shift = dot_nn(jnp.broadcast_to(embed, (8, embed.shape[1])), r.time_buf[...])[0:1, :]
    inner = r.h1[...] + (r.all_split[0:1, :] + (shift + r.all_split[1:2, :]))
    r.h1[...] = inner
    r.flush("h1")
    poll()
    local_mean = group_mean(col_mean(inner))
    local_dev = inner - local_mean
    local_var = group_mean(col_mean(local_dev * local_dev))
    r.stat_send[0:1, :] = local_mean
    r.stat_send[1:2, :] = local_var
    stat_copy = remote(r.stat_send, r.stat_got, partner, r.core_sems, 4)
    stat_copy.start()
    poll()
    stat_copy.wait()
    other_mean, other_var = r.stat_got[0:1, :], r.stat_got[1:2, :]
    mean_two = 0.5 * (local_mean + other_mean)
    gap = 0.5 * (local_mean - other_mean)
    inv_two = lax.rsqrt(0.5 * (local_var + other_var) + gap * gap + NORM_EPS)
    r.stats[0:1, :] = mean_one
    r.stats[1:2, :] = inv_one
    r.stats[2:3, :] = mean_two
    r.stats[3:4, :] = inv_two
    r.stats[4:8, :] = jnp.zeros((4, D), F32)
    pre = (r.h1[...] - mean_two) * (inv_two * (1.0 + r.all_split[2:3, :])) + r.all_split[3:4, :]
    r.act[SIDE : SIDE + share, :] = pre * jax.nn.sigmoid(pre)
    swap_edges(r.act, r.edge_send, r.edge_got, core, partner, r.core_sems, 5)
    side_by_side(r.wide, r.act[...], (0, 1, 2))
    poll_group(1)

    loads = []
    for u in range(3):
        arrived(1, 1 + u)
        loads.append(load("two", 3 * u, 3, r.kernels.at[3 * u : 3 * u + 3], u))
    for u in range(3):
        loads[u].wait()
        term = None
        for w in range(3):
            part = dot_nt(
                r.wide[u * SIDE : u * SIDE + share, w * D : (w + 1) * D], r.kernels[3 * u + w]
            )
            term = part if term is None else term + part
        if u == 0:
            r.h[...] = term
        else:
            r.h[...] += term
        poll()
    r.h[...] = r.img[...].astype(F32) + (r.h[...] + r.vec[2:3, :])
    r.flush("h")

    poll_group(2)
    loads = []
    for slot, (name, spots, at, size) in enumerate(
        (("kv", (1, 2), 1, 2), ("q", (0,), 0, 1), ("so", (3,), 3, 1))
    ):
        for spot in spots:
            arrived(2, spot)
        loads.append(load(name, 0, size, r.kernels.at[at : at + size], slot))
    norm, _, _ = layer_norm(r.h[...], 1.0 + r.vec[3:4, :], r.vec[4:5, :])
    low = norm.astype(BF)
    loads[0].wait()
    for part in range(2):
        proj = dot_nn(low, r.kernels[1 + part]).astype(BF)
        blank = jnp.zeros((share, LANES - HEAD_DIM), BF)
        for head in range(HEADS):
            span = proj[:, HEAD_DIM * head : HEAD_DIM * (head + 1)]
            r.kv[part, head, mine, :] = jnp.concatenate([span, blank], axis=1)
    kv_copy = remote(r.kv.at[:, :, mine, :], r.kv.at[:, :, mine, :], partner, r.core_sems, 7)
    kv_copy.start()
    poll()
    loads[1].wait()
    r.ext_act[:, :D] = low
    r.ext_act[:, D:] = dot_nn(low, r.yq[...]).astype(BF)
    r.ext_w[:D, :] = r.kernels[0]
    r.ext_w[D:, :] = r.zq[...]
    to_heads(r.q, dot_nn(r.ext_act[...], r.ext_w[...]).astype(BF))
    poll()
    kv_copy.wait()
    r.flush("kv", "q")
    lane = lax.broadcasted_iota(jnp.int32, (share, LANES), 1)
    r.lse_cols[...] = jnp.zeros_like(r.lse_cols)

    def one_head(head, carry):
        scores = dot_nt(r.q[head], r.kv[0, head])
        peak = jnp.max(scores, axis=1, keepdims=True)
        expo = jnp.exp2((scores - peak) * (FACTOR * LOG_TWO_E))
        total = jnp.sum(expo, axis=1, keepdims=True)
        probs = (expo * (1.0 / total)).astype(BF)
        r.heads[head] = dot_nn(probs, r.kv[1, head]).astype(BF)
        row = peak * (FACTOR * LOG_TWO_E) + jnp.log2(total)
        r.lse_cols[...] = jnp.where(lane == head, row, r.lse_cols[...])
        return carry

    for first in range(0, HEADS, 2):
        lax.fori_loop(first, first + 2, one_head, 0)
        poll()
    r.lse[...] = r.lse_cols[...].T
    merged = from_heads(r.heads)
    r.o[...] = merged
    r.flush("lse", "o")
    loads[2].wait()
    r.h2[...] = r.h[...] + (dot_nt(merged, r.kernels[3]) + r.vec[9:10, :])
    r.flush("h2")

    poll()
    poll_group(3)
    for position in range(4):
        arrived(3, position)
    loads = [
        load("cq", 0, 1, r.kernels.at[4:5], 0),
        load("ckv", 0, 2, r.text_kv, 1),
        load("co", 0, 1, r.kernels.at[5:6], 2),
    ]
    norm, _, _ = layer_norm(r.h2[...], 1.0 + r.vec[5:6, :], r.vec[6:7, :])
    poll()
    loads[0].wait()
    to_heads(r.cq, dot_nn(norm.astype(BF), r.kernels[4]).astype(BF))
    loads[1].wait()
    for part in range(2):
        to_heads(r.ckv.at[part], dot_nn(r.text_all[...], r.text_kv[part]).astype(BF))

    poll()

    def cross_head(head, carry):
        probs = cross_probs(r.cq[head], r.ckv[0, head])
        r.heads[head] = dot_nn(probs.astype(BF), r.ckv[1, head]).astype(BF)
        return carry

    lax.fori_loop(0, HEADS, cross_head, 0)
    loads[2].wait()
    r.h3[...] = r.h2[...] + (dot_nt(from_heads(r.heads), r.kernels[5]) + r.vec[10:11, :])

    r.flush("cq", "ckv")
    poll()

    gain = 1.0 + r.vec[7:8, :]
    norm, _, _ = layer_norm(r.h3[...], gain, r.vec[8:9, :])
    low = norm.astype(BF)
    r.ext_act[:, :D] = low
    r.ext_act[:, D:] = dot_nn(low, r.yu[...]).astype(BF)

    @pl.when(away)
    def _():
        cot_copy.wait()

    r.cot_low[...] = (r.all_cot[...].astype(F32) * r.scale_out[0:1, 0:1]).astype(BF)
    down_acc = r.act.at[:share, :]
    quarter = full["ff"].shape[2] // 4
    for part in range(4):
        poll_group(4 + part)
        for position in range(3):
            arrived(4 + part, position)
        first = part * quarter
        span = slice(first, first + quarter)
        slots = r.kernels.at[3 * (part % 2) : 3 * (part % 2) + 3]
        copy = pltpu.make_async_copy(full["ff"].at[:, :, span], slots, r.load_sems.at[part])
        copy.start()
        copy.wait()
        for half in range(2):
            cols = slice(half * quarter, (half + 1) * quarter)
            r.ff_wide[:D, cols] = slots[half]
            r.ff_wide[D:, cols] = r.zu[half, :, span]
        poll(4)
        mixed = dot_nn(r.ext_act[...], r.ff_wide[...])
        value = mixed[:, :quarter] + r.all_bias[0:1, span]
        gate = mixed[:, quarter:] + r.all_bias[1:2, span]
        cdf = 0.5 * (1.0 + lax.erf(gate * INV_ROOT_TWO))
        gelu = gate * cdf
        slope = cdf + gate * jnp.exp(-0.5 * gate * gate) * INV_ROOT_TWOPI
        poll(4)
        hidden_grad = dot_nn(r.cot_low[...], slots[2])
        r.ff_grads[:, :quarter] = (hidden_grad * gelu).astype(BF)
        r.ff_grads[:, quarter:] = (hidden_grad * value * slope).astype(BF)
        down = dot_nt((value * gelu).astype(BF), slots[2])
        poll(4)
        outer = dot_tn(r.ext_act[:, D:], r.ff_grads[...])
        for half in range(2):
            base = 16 * half
            one, two = factor_rows(
                outer[:, half * quarter : (half + 1) * quarter],
                r.all_ur[base : base + 8, span],
                r.all_ur[base + 8 : base + 16, span],
            )
            r.up_right[0, half, :, span] = one
            r.up_right[1, half, :, span] = two
        back = dot_nt(r.ff_grads[...], r.ff_wide[...])
        if part == 0:
            down_acc[...] = down
            r.back_acc[...] = back
        else:
            down_acc[...] += down
            r.back_acc[...] += back
        poll(4)
    r.flush("up_right")
    r.out_img[...] = (r.h3[...] + (down_acc[...] + r.vec[11:12, :])).astype(BF)
    r.flush("out_img")
    low_rank = r.back_acc[:, D:].astype(BF)
    one, two = factor_rows(dot_tn(low_rank, r.ext_act[:, :D]), r.ul[0], r.ul[1])
    r.up_left[0] = one
    r.up_left[1] = two
    normed_grad = r.back_acc[:, :D] + dot_nt(low_rank, r.yu[...])
    _, normal, inv = layer_norm(r.h3[...], gain, r.vec[8:9, :])
    cot = r.all_cot[...].astype(F32) * r.scale_out[0:1, 0:1]
    r.g2[...] = cot + layer_back(normed_grad, normal, inv, gain)
    r.flush("g2")
    poll(len(events))
    for group in groups:
        for which in group:
            ring.drain(which)
    for copy in first_copies + list(side_copies.values()) + list(core_copies.values()):
        copy.wait_send()


def forward(arrays, shards, full, chips):
    gathers = full is None
    share = arrays["lat"].shape[0] // 2
    anywhere = pl.BlockSpec(memory_space=pl.ANY)
    dma = pltpu.SemaphoreType.DMA
    ins = {name: (arrays[name], None) for name in ("lat", "vec")}
    if gathers:
        ins["in_one"] = (shards[0], None)
    ins.update({name: (value, None) for name, value in arrays.items()})
    text_rows, text_width = arrays["text"].shape
    time_width = arrays["emb"].shape[1]

    def double(name):
        rows, cols = arrays[name].shape
        return (rows, 2 * cols)

    outs = {
        "h": ((share, D), F32, None),
        "h1": ((share, D), F32, None),
        "img": ((share, D), BF, None),
        "stats": ((8, D), F32, WHOLE),
        "h2": ((share, D), F32, None),
        "q": ((HEADS, share, LANES), BF, None),
        "kv": ((2, HEADS, 2 * share, LANES), BF, None),
        "o": ((share, D), BF, None),
        "lse": ((LANES, share), F32, None),
        "cq": ((HEADS, share, LANES), BF, None),
        "ckv": ((2, HEADS, LANES, LANES), BF, None),
        "all_split": (double("split"), F32, WHOLE),
        "all_qr": (double("qr"), F32, WHOLE),
        "yq": ((D, RANK_SQ), BF, WHOLE),
        "zq": ((RANK_SQ, D), BF, WHOLE),
        "out_img": ((share, D), BF, None),
        "g2": ((share, D), F32, None),
        "up_right": ((2, 2, 8, double("ur")[1]), F32, None),
        "up_left": ((2, 8, D), F32, WHOLE),
    }
    scratch = {}
    if gathers:
        for name, value in zip(SHARDS, shards):
            lead, rows, cols = value.shape
            ins["in_" + name] = (value, None)
            outs["full_" + name] = ((lead, rows * chips * 2, 2 * cols), BF, anywhere)
            scratch["got_" + name] = pltpu.VMEM(value.shape, BF)
            scratch["wide_" + name] = pltpu.VMEM((lead, rows, 2 * cols), BF)
    else:
        for name, value in zip(SHARDS, full):
            ins["full_" + name] = (value, anywhere)
    for name in ("lat", "emb", "text", "split", "bias", "qr", "ur"):
        value = arrays[name]
        scratch["got_" + name] = pltpu.VMEM(value.shape, value.dtype)
    pieces = 27 if gathers else 1
    hidden = double("ur")[1]
    scratch.update(
        image=pltpu.VMEM(arrays["lat"].shape, BF),
        kernels=pltpu.VMEM((9, D, D), BF),
        time_buf=pltpu.VMEM((time_width, D), BF),
        text_kv=pltpu.VMEM((2, text_width, D), BF),
        text_all=pltpu.VMEM((LANES, text_width), BF),
        wide=pltpu.VMEM((share + 2 * SIDE, 3 * D), BF),
        act=pltpu.VMEM((share + 2 * SIDE, D), F32),
        scale=pltpu.VMEM((8, LANES), F32),
        got_scale=pltpu.VMEM((8, LANES), F32),
        stat_send=pltpu.VMEM((8, D), F32),
        stat_got=pltpu.VMEM((8, D), F32),
        edge_send=pltpu.VMEM((SIDE, D), BF),
        edge_got=pltpu.VMEM((SIDE, D), BF),
        ext_act=pltpu.VMEM((share, D + RANK_SQ), BF),
        ext_w=pltpu.VMEM((D + RANK_SQ, D), BF),
        heads=pltpu.VMEM((HEADS, share, LANES), BF),
        lse_cols=pltpu.VMEM((share, LANES), F32),
        h3=pltpu.VMEM((share, D), F32),
        all_bias=pltpu.VMEM(double("bias"), F32),
        all_ur=pltpu.VMEM(double("ur"), F32),
        yu=pltpu.VMEM((D, RANK_SQ), BF),
        zu=pltpu.VMEM((2, RANK_SQ, hidden), BF),
        all_cot=pltpu.VMEM((share, D), BF),
        scale_out=pltpu.VMEM((8, LANES), F32),
        cot_low=pltpu.VMEM((share, D), BF),
        ff_wide=pltpu.VMEM((D + RANK_SQ, hidden // 2), BF),
        ff_grads=pltpu.VMEM((share, hidden // 2), BF),
        back_acc=pltpu.VMEM((share, D + RANK_SQ), F32),
        first_sems=dma((2, 3)),
        side_sems=dma((2, len(SHARDS) + 4)),
        core_sems=dma((2, 8)),
        load_sems=dma((4,)),
        ring_sems=dma((2, 2, pieces, chips // 2)),
        pair_sems=dma((2, pieces, chips)),
        over_sems=dma((2, pieces, chips)),
        own_sems=dma((pieces,)),
    )
    return call_named(
        functools.partial(forward_body, chips, gathers), "forward", ins, outs, scratch, 1
    )


class Halving:
    HALVINGS = 3

    def __init__(self, steps, acc, got, out, sems):
        self.acc, self.got, self.out, self.sems, self.steps = acc, got, out, sems, steps
        index = lax.axis_index("dp")
        plane = lax.axis_index("mp")
        core = lax.rem(index, 2)
        chip = index // 2
        self.partners = [((index + 1 - 2 * core, plane), core), ((index, 1 - plane), plane)]
        span = 1
        for _ in range(steps - 2):
            bit = lax.rem(chip // span, 2)
            self.partners.append((((chip + span - 2 * span * bit) * 2 + core, plane), bit))
            span *= 2
        self.offset, self.size, self.base = 0, acc.shape[0], 0
        self.trail = []
        self.flight = None
        self.done = 0

    @classmethod
    def room(cls, rows, steps):
        small = rows >> cls.HALVINGS
        return rows - small + small * (steps - cls.HALVINGS)

    def begin(self):
        self._down(0)

    def _down(self, step):
        where, bit = self.partners[step]
        if step < self.HALVINGS:
            size = self.size // 2
            mine = pl.multiple_of(self.offset + bit * size, 8)
            theirs = pl.multiple_of(self.offset + (1 - bit) * size, 8)
        else:
            size, mine, theirs = self.size, self.offset, self.offset
        copy = remote(
            self.acc.at[pl.ds(theirs, size), :],
            self.got.at[pl.ds(self.base, size), :],
            where,
            self.sems,
            step,
        )
        copy.start()
        self.flight = (copy, mine, size)

    def _up(self, step):
        mine, size, where = self.trail[step]
        part = self.out.at[pl.ds(mine, size), :]
        copy = remote(part, part, where, self.sems, self.steps + step)
        copy.start()
        self.flight = (copy, mine, size)

    def step(self):
        steps, total = self.steps, self.steps + self.HALVINGS
        if self.done >= total:
            return
        copy, mine, size = self.flight
        copy.wait()
        if self.done < steps:
            self.acc[pl.ds(mine, size), :] += self.got[pl.ds(self.base, size), :]
            self.trail.append((mine, size, self.partners[self.done][0]))
            self.offset, self.size = mine, size
            self.base += size
            if self.done + 1 < steps:
                self._down(self.done + 1)
            else:
                self.out[pl.ds(mine, size), :] = self.acc[pl.ds(mine, size), :]
                self._up(self.HALVINGS - 1)
        elif self.done + 1 < total:
            self._up(total - 2 - self.done)
        self.done += 1


def conv_back_kernel(
    steps,
    need,
    g0_ref,
    h1_ref,
    img_ref,
    stat_ref,
    split_ref,
    vec_ref,
    up_right_ref,
    up_left_ref,
    query_right_ref,
    query_left_ref,
    ql_state,
    qr_state,
    ul_state,
    ur_state,
    one_ref,
    two_ref,
    grad_ref,
    ql_new,
    ql_copy,
    qr_new,
    qr_copy,
    ul_new,
    ul_copy,
    ur_new,
    ur_copy,
    moments,
    sum_ref,
    one_buf,
    two_buf,
    wide,
    act,
    half_back,
    stat_send,
    stat_got,
    edge_send,
    edge_got,
    acc,
    got,
    half_row,
    load_sems,
    core_sems,
    sum_sems,
    back_sems,
):
    index = lax.axis_index("dp")
    side = lax.axis_index("mp")
    core = lax.rem(index, 2)
    partner = (index + 1 - 2 * core, side)
    neighbour = (index, 1 - side)
    diagonal = (index + 1 - 2 * core, 1 - side)
    share = g0_ref.shape[0]
    loads = []
    for slot, (src, dst) in enumerate(((two_ref, two_buf), (one_ref, one_buf))):
        load = pltpu.make_async_copy(src, dst, load_sems.at[slot])
        load.start()
        loads.append(load)
    total = Halving(steps, acc, got, sum_ref, sum_sems)
    barrier = pltpu.get_barrier_semaphore()
    for where, _ in total.partners:
        pl.semaphore_signal(barrier, inc=1, device_id=where, device_id_type=MESH)
    pl.semaphore_signal(barrier, inc=1, device_id=diagonal, device_id_type=MESH)
    need("g0", "up_right", "up_left", "query_right", "query_left")
    parts = []
    for member in range(2):
        for part in range(2):
            for block in range(up_right_ref.shape[3] // D):
                parts.append(up_right_ref[member, part, :, block * D : (block + 1) * D])
    for ref in (query_right_ref, up_left_ref, query_left_ref):
        parts += [ref[0], ref[1]]
    for spot, part in enumerate(parts):
        acc[8 * spot : 8 * spot + 8, :] = part
    acc[8 * len(parts) :, :] = jnp.zeros((acc.shape[0] - 8 * len(parts), D), F32)
    act[SIDE : SIDE + share, :] = g0_ref[...]
    pl.semaphore_wait(barrier, steps + 1)
    total.begin()
    swap_edges(act, edge_send, edge_got, core, partner, core_sems, 0)
    side_by_side(wide, act[...], (2, 1, 0))
    total.step()
    inner = act.at[SIDE : SIDE + share, :]
    loads[0].wait()
    for u in range(3):
        term = dot_nn(
            wide[u * SIDE : u * SIDE + share, :],
            two_buf[3 * (2 - u) : 3 * (2 - u) + 3].reshape(3 * D, D),
        )
        if u == 0:
            inner[...] = term
        else:
            inner[...] += term
        total.step()
    need("h1", "stats", "split")
    mean_two, inv_two = stat_ref[2:3, :], stat_ref[3:4, :]
    gain_two = 1.0 + split_ref[2:3, :]
    normal = (h1_ref[...] - mean_two) * inv_two
    scaled = inner[...] * silu_slope(normal * gain_two + split_ref[3:4, :]) * gain_two
    means = pair_means(scaled, normal, stat_send, stat_got, partner, core_sems, 1)
    inner[...] = inv_two * (scaled - means[0] - normal * means[1])
    swap_edges(act, edge_send, edge_got, core, partner, core_sems, 2)
    side_by_side(wide, act[...], (2, 1, 0))
    total.step()
    loads[1].wait()
    for u in range(3):
        term = None
        for spot in range(3):
            part = dot_nt(
                wide[u * SIDE : u * SIDE + share, spot * D : (spot + 1) * D],
                one_buf[3 * (2 - u) + spot],
            )
            term = part if term is None else term + part
        if u == 0:
            inner[...] = term
        else:
            inner[...] += term
        total.step()
    need("img", "vec")
    mean_one, inv_one = stat_ref[0:1, :], stat_ref[1:2, :]
    gain_one = 1.0 + vec_ref[0:1, :]
    normal = (img_ref[...].astype(F32) - mean_one) * inv_one
    scaled = inner[...] * silu_slope(normal * gain_one + vec_ref[1:2, :]) * gain_one
    means = pair_means(scaled, normal, stat_send, stat_got, partner, core_sems, 3)
    half_back[...] = (
        g0_ref[...] + inv_one * (scaled - means[0] - normal * means[1])
    ).astype(BF)
    mine = grad_ref.at[pl.ds(pl.multiple_of(core * share, share), share), :]
    home = core == side

    @pl.when(home)
    def _():
        remote(half_back, mine, neighbour, back_sems, core).start()
        pltpu.make_async_copy(half_back, mine, load_sems.at[2]).start()

    @pl.when(jnp.logical_not(home))
    def _():
        remote(half_back, mine, diagonal, back_sems, core).start()
        remote(half_back, mine, partner, back_sems, 2 + core).start()

    for _ in range(2 * steps):
        total.step()

    need("ql", "qr", "ul", "ur")
    blocks = up_right_ref.shape[3] // D
    base = 4 * blocks * 8

    def update(state, at, grads):
        return adamw_parts([state[(entry,) + at] for entry in range(4)], grads)

    def sided(values):
        size = values.shape[1] // 2

        @pl.when(side == 0)
        def _():
            half_row[...] = values[:, :size]

        @pl.when(side == 1)
        def _():
            half_row[...] = values[:, size:]

        return half_row[...]

    for member in range(2):
        at = pl.ds(base + 8 * member, 8)
        weight, moment, second, average = update(qr_state, (member,), sided(sum_ref[at, :]))
        qr_new[0, member] = weight
        qr_new[1, member] = average
        qr_copy[member] = weight.astype(BF)
        moments[1, 0, member] = moment
        moments[1, 1, member] = second
        at = pl.ds(base + 16 + 8 * member, 8)
        parts = update(ul_state, (member,), sum_ref[at, :])
        for entry in range(4):
            ul_new[entry, member] = parts[entry]
        ul_copy[member] = parts[0].astype(BF)
        at = pl.ds(base + 32 + 8 * member, 8)
        weight, moment, second, average = update(ql_state, (member,), sum_ref[at, :])
        ql_new[0, member] = weight
        ql_new[1, member] = average
        ql_copy[member] = weight.astype(BF)
        moments[0, 0, member] = sided(moment)
        moments[0, 1, member] = sided(second)
        for part_number in range(2):
            for block in range(blocks // 2):
                row = ((member * 2 + part_number) * blocks + side * (blocks // 2) + block) * 8
                grads = sum_ref[pl.ds(pl.multiple_of(row, 8), 8), :]
                cols = slice(block * D, (block + 1) * D)
                parts = adamw_parts(
                    [ur_state[entry, member, part_number, :, cols] for entry in range(4)], grads
                )
                for entry in range(4):
                    ur_new[entry, member, part_number, :, cols] = parts[entry]
                ur_copy[member, part_number, :, cols] = parts[0].astype(BF)

    def part(which):
        return grad_ref.at[pl.ds(pl.multiple_of(which * share, share), share), :]

    @pl.when(home)
    def _():
        remote(half_back, mine, neighbour, back_sems, core).wait_send()
        pltpu.make_async_copy(half_back, mine, load_sems.at[2]).wait()
        remote(half_back, part(1 - core), partner, back_sems, 3 - core).wait_recv()

    @pl.when(jnp.logical_not(home))
    def _():
        remote(half_back, mine, diagonal, back_sems, core).wait_send()
        remote(half_back, mine, partner, back_sems, 2 + core).wait_send()
        remote(half_back, part(core), neighbour, back_sems, core).wait_recv()
        remote(half_back, part(1 - core), diagonal, back_sems, 1 - core).wait_recv()


def pair_means(scaled, normal, stat_send, stat_got, partner, sems, slot):
    stat_send[0:1, :] = group_mean(col_mean(scaled))
    stat_send[1:2, :] = group_mean(col_mean(scaled * normal))
    copy = remote(stat_send, stat_got, partner, sems, slot)
    copy.start()
    copy.wait()
    both = 0.5 * (stat_send[...] + stat_got[...])
    return both[0:1, :], both[1:2, :]


def conv_back(g0, h1, img, stats, split, vectors, grads, states, one, two, devices):
    share = g0.shape[0]
    steps = devices.bit_length() - 1
    dma = pltpu.SemaphoreType.DMA
    unit = 8 << Halving.HALVINGS
    rows = -(-sum(g.size // D for g in grads) // unit) * unit
    ql, qr, ul, ur = states
    outs = {
        "grad": ((2 * share, D), BF, WHOLE),
        "ql_new": ((2,) + ql.shape[1:], F32, WHOLE),
        "ql_copy": (ql.shape[1:], BF, WHOLE),
        "qr_new": ((2,) + qr.shape[1:], F32, WHOLE),
        "qr_copy": (qr.shape[1:], BF, WHOLE),
        "ul_new": (ul.shape, F32, WHOLE),
        "ul_copy": (ul.shape[1:], BF, WHOLE),
        "ur_new": (ur.shape, F32, WHOLE),
        "ur_copy": (ur.shape[1:], BF, WHOLE),
        "moments": ((2, 2) + qr.shape[1:], F32, WHOLE),
    }
    scratch = {
        "sum": pltpu.VMEM((rows, D), F32),
        "one_buf": pltpu.VMEM((9, D, D), BF),
        "two_buf": pltpu.VMEM((9, D, D), BF),
        "wide": pltpu.VMEM((share + 2 * SIDE, 3 * D), BF),
        "act": pltpu.VMEM((share + 2 * SIDE, D), F32),
        "half_back": pltpu.VMEM((share, D), BF),
        "stat_send": pltpu.VMEM((8, D), F32),
        "stat_got": pltpu.VMEM((8, D), F32),
        "edge_send": pltpu.VMEM((SIDE, D), BF),
        "edge_got": pltpu.VMEM((SIDE, D), BF),
        "acc": pltpu.VMEM((rows, D), F32),
        "got": pltpu.VMEM((Halving.room(rows, steps), D), F32),
        "half_row": pltpu.VMEM(qr.shape[2:], F32),
        "load_sems": dma((3,)),
        "core_sems": dma((2, 4)),
        "sum_sems": dma((2, steps + Halving.HALVINGS)),
        "back_sems": dma((2, 4)),
    }
    given = dict(zip(("up_right", "up_left", "query_right", "query_left"), grads))
    given.update(g0=g0, h1=h1, img=img, stats=stats, split=split, vec=vectors)
    given.update(ql=ql, qr=qr, ul=ul, ur=ur)
    order = ("g0", "h1", "img", "stats", "split", "vec", "up_right", "up_left")
    order += ("query_right", "query_left", "ql", "qr", "ul", "ur")
    ins = {n: (given[n], None) for n in ("g0", "up_right", "up_left", "query_right", "query_left")}
    ins.update({n: (given[n], None) for n in order if n not in ins})
    anywhere = pl.BlockSpec(memory_space=pl.ANY)
    ins["one"] = (one, anywhere)
    ins["two"] = (two, anywhere)

    def body(r):
        refs = [getattr(r, n) for n in order + ("one", "two") + tuple(outs) + tuple(scratch)]
        conv_back_kernel(steps, r.need, *refs)

    return tuple(vars(call_named(body, "conv_back", ins, outs, scratch, 5)).values())


def shards(
    latents,
    out_grad,
    text_states,
    time_embed,
    group_ids,
    group_weights,
    timesteps,
    step_weights,
    vectors,
    split_vectors,
    up_bias,
    conv_one,
    conv_two,
    time_proj,
    self_query,
    self_kv,
    self_out,
    cross_query,
    cross_kv,
    cross_out,
    ff_up,
    ff_down,
    query_left_state,
    query_right_state,
    up_left_state,
    up_right_state,
):
    devices_dp = lax.axis_size("dp")
    chips = devices_dp // 2
    side = lax.axis_index("mp")

    def join_sides(values):
        other = lax.ppermute(values, "mp", [(0, 1), (1, 0)])
        first = jnp.where(side == 0, values, other)
        second = jnp.where(side == 0, other, values)
        return jnp.concatenate([first, second], axis=-1)

    pieces = [
        conv_one,
        time_proj[None],
        conv_two.transpose(0, 2, 1),
        self_query[None],
        self_kv.transpose(1, 0, 2),
        self_out.T[None],
        cross_query[None],
        cross_kv.transpose(1, 0, 2),
        cross_out.T[None],
        jnp.concatenate([ff_up.transpose(1, 0, 2), ff_down.T[None]], axis=0),
    ]
    gathers = all(piece.shape[1] % 8 == 0 for piece in pieces)
    full = None
    if not gathers:
        full = [lax.all_gather(join_sides(p), "dp", axis=1, tiled=True) for p in pieces]
    query_left_turned = query_left_state.transpose(0, 1, 3, 2)
    up_left_turned = up_left_state.transpose(0, 1, 3, 2)
    up_rows = up_right_state[0].transpose(2, 0, 1, 3)
    arrays = {
        "lat": latents[0],
        "emb": time_embed,
        "text": text_states[0],
        "split": split_vectors,
        "bias": up_bias,
        "qr": query_right_state[0].reshape(-1, query_right_state.shape[-1]),
        "ur": up_rows.reshape(-1, up_rows.shape[-1]),
        "ql": query_left_turned[0],
        "ul": up_left_turned[0],
        "vec": vectors,
        "cot": out_grad[0],
        "step": timesteps[:, None],
        "group": group_ids[:, None],
        "step_weights": step_weights[None],
        "group_weights": group_weights[None],
    }
    fwd = forward(arrays, pieces, full, chips)
    if not gathers:
        w_one, _, w_two_t, w_q, w_kv, w_so_t, w_cq, _, w_co_t, w_ff = full
    else:
        w_one, w_two_t, w_q, w_kv = fwd.full_one, fwd.full_two, fwd.full_q, fwd.full_kv
        w_so_t, w_cq, w_co_t, w_ff = fwd.full_so, fwd.full_cq, fwd.full_co, fwd.full_ff
    grad_up_right, grad_up_left = fwd.up_right, fwd.up_left
    cotangent, grad_query_right, grad_query_left, block_out = attention_back(
        fwd.g2,
        fwd.h,
        fwd.h2,
        vectors,
        w_q[0],
        fwd.yq,
        fwd.zq,
        w_kv,
        w_so_t[0],
        w_cq[0],
        w_co_t[0],
        fwd.q,
        fwd.kv,
        fwd.o,
        fwd.lse,
        fwd.cq,
        fwd.ckv,
        fwd.all_qr,
        query_left_turned[0],
        fwd.out_img,
    )
    block_out = block_out[None]
    (
        latents_grad,
        query_left_new,
        query_left_copy,
        query_right_new,
        query_right_copy,
        up_left_new,
        up_left_copy,
        up_right_new,
        up_right_copy,
        query_moments,
    ) = conv_back(
        cotangent,
        fwd.h1,
        fwd.img,
        fwd.stats,
        fwd.all_split,
        vectors,
        [grad_up_right, grad_up_left, grad_query_right, grad_query_left],
        [
            query_left_turned,
            query_right_state,
            up_left_turned,
            up_right_state.transpose(0, 1, 3, 2, 4),
        ],
        w_one,
        w_two_t,
        devices_dp * 2,
    )
    return (
        block_out,
        latents_grad[None],
        query_left_new.transpose(0, 1, 3, 2),
        query_left_copy.transpose(0, 2, 1),
        query_right_new,
        query_right_copy,
        up_left_new.transpose(0, 1, 3, 2),
        up_left_copy.transpose(0, 2, 1),
        up_right_new.transpose(0, 1, 3, 2, 4),
        up_right_copy.transpose(0, 2, 1, 3),
        query_moments,
    )


def solution(mesh):
    placed = (
        P("dp", None, None),
        P("dp", "mp", None),
        P("dp", None, None),
        P("dp", None),
        P("dp"),
        P(),
        P("dp"),
        P(),
        P(),
        P(None, "mp"),
        P(None, "mp"),
        P(None, "dp", "mp"),
        P(None, "mp", "dp"),
        P("dp", "mp"),
        P("dp", "mp"),
        P("dp", None, "mp"),
        P("mp", "dp"),
        P("dp", "mp"),
        P("dp", None, "mp"),
        P("mp", "dp"),
        P("dp", None, "mp"),
        P("mp", "dp"),
        P(),
        P(None, None, None, "mp"),
        P(),
        P(None, None, None, None, "mp"),
    )
    return jax.shard_map(
        shards,
        mesh=mesh,
        in_specs=placed,
        out_specs=(
            P("dp", "mp", None),
            P("dp", None, None),
            P(),
            P(),
            P(None, None, None, "mp"),
            P(None, None, "mp"),
            P(),
            P(),
            P(None, None, None, None, "mp"),
            P(None, None, None, "mp"),
            P(None, None, None, None, "mp"),
        ),
        check_vma=False,
    )
```

```python
import functools
import types

import jax
import jax.numpy as jnp
from jax import lax
from jax.experimental import pallas as pl
from jax.experimental.pallas import tpu as pltpu
from jax.sharding import PartitionSpec as P

D = 640
HEAD_DIM = 80
GROUPS = 32
SIDE = 32
ADAM_STEP = 10
LANES = 128

NORM_EPS = 1e-05
BETA_ONE = 0.9
BETA_TWO = 0.999
ADAM_EPS = 1e-08
DECAY_RATE = 0.01
LEARN_RATE = 0.06
EMA_KEEP = 0.995
INV_ROOT_TWO = 0.7071067811865476
INV_ROOT_TWOPI = 0.3989422804014327

MESH = pl.DeviceIdType.MESH
BF = jnp.bfloat16
F32 = jnp.float32


def adamw_parts(state, grads):
    weight, moment, second, average = (state[0], state[1], state[2], state[3])
    moment = BETA_ONE * moment + (1.0 - BETA_ONE) * grads
    second = BETA_TWO * second + (1.0 - BETA_TWO) * grads * grads
    moment_hat = moment / (1.0 - BETA_ONE**ADAM_STEP)
    second_hat = second / (1.0 - BETA_TWO**ADAM_STEP)
    weight = weight - LEARN_RATE * (
        moment_hat / (jnp.sqrt(second_hat) + ADAM_EPS) + DECAY_RATE * weight
    )
    average = EMA_KEEP * average + (1.0 - EMA_KEEP) * weight
    return (weight, moment, second, average)


def dot_nn(left, right):
    return jnp.dot(left, right, preferred_element_type=F32)


def dot_nt(left, right):
    return lax.dot_general(left, right, (((1,), (1,)), ((), ())), preferred_element_type=F32)


def dot_tn(left, right):
    return lax.dot_general(left, right, (((0,), (0,)), ((), ())), preferred_element_type=F32)


def silu_slope(values):
    sigma = jax.nn.sigmoid(values)
    return sigma * (1.0 + values * (1.0 - sigma))


def layer_norm(values, gain, bias):
    centred = values - jnp.mean(values, axis=1, keepdims=True)
    inv_std = lax.rsqrt(jnp.mean(centred * centred, axis=1, keepdims=True) + NORM_EPS)
    normal = centred * inv_std
    return (normal * gain + bias, normal, inv_std)


def layer_back(grads, normal, inv_std, gain):
    scaled = grads * gain
    return inv_std * (
        scaled
        - jnp.mean(scaled, axis=1, keepdims=True)
        - normal * jnp.mean(scaled * normal, axis=1, keepdims=True)
    )


def ring_chip(place, chips):
    place = lax.rem(place + 2 * chips, chips)
    return jnp.where(place < chips // 2, 2 * place, 2 * (chips - 1 - place) + 1)


def ring_place(chip, chips):
    column = chip // 2
    return jnp.where(lax.rem(chip, 2) == 0, column, chips - 1 - column)


WHOLE = pl.BlockSpec(memory_space=pltpu.VMEM)
VMEM_BYTES = 63 * 1024 * 1024
FACTOR = HEAD_DIM**-0.5
LOG_TWO_E = 1.4426950408889634
HEADS = D // HEAD_DIM
RANK_SQ = 64


def split_low(values):
    high = values.astype(BF)
    return high, (values - high.astype(F32)).astype(BF)


def to_heads(slots, values):
    blank = jnp.zeros((values.shape[0], LANES - HEAD_DIM), BF)
    for head in range(HEADS):
        part = values[:, HEAD_DIM * head : HEAD_DIM * (head + 1)]
        slots[head] = jnp.concatenate([part, blank], axis=1)


def from_heads(slots):
    return jnp.concatenate([slots[head][:, :HEAD_DIM] for head in range(HEADS)], axis=1)


def partner_barrier():
    index = lax.axis_index("dp")
    where = (index + 1 - 2 * lax.rem(index, 2), lax.axis_index("mp"))
    barrier = pltpu.get_barrier_semaphore()
    pl.semaphore_signal(barrier, inc=1, device_id=where, device_id_type=MESH)
    return lax.rem(index, 2), where, barrier


def send_to(where, src, dst, sems, slot):
    return pltpu.make_async_remote_copy(
        src_ref=src,
        dst_ref=dst,
        send_sem=sems.at[0, slot],
        recv_sem=sems.at[1, slot],
        device_id=where,
        device_id_type=MESH,
    )


TEXT = 77


def cross_probs(query, keys):
    scores = dot_nt(query, keys)
    column = lax.broadcasted_iota(jnp.int32, scores.shape, 1)
    scores = jnp.where(column < TEXT, scores, -1e30)
    top = jnp.max(scores, axis=1, keepdims=True)
    expo = jnp.exp2((scores - top) * (FACTOR * LOG_TWO_E))
    return expo * (1.0 / jnp.sum(expo, axis=1, keepdims=True))


def attention_back_kernel(
    need,
    g2_ref,
    h_ref,
    h2_ref,
    vec_ref,
    wq_ref,
    left_ref,
    right_ref,
    wkv_ref,
    wso_ref,
    wcq_ref,
    wco_ref,
    q_ref,
    kv_ref,
    o_ref,
    lse_ref,
    cq_ref,
    ckv_ref,
    rows_ref,
    cols_ref,
    image_ref,
    g0_ref,
    right_out,
    left_out,
    block_ref,
    wide,
    dout,
    cot,
    delta,
    dq_acc,
    dkv_acc,
    give,
    take,
    sems,
):
    core, where, barrier = partner_barrier()
    side = where[1]
    share = h_ref.shape[0]
    diagonal = (where[0], 1 - side)
    pl.semaphore_signal(barrier, inc=1, device_id=diagonal, device_id_type=MESH)
    pl.semaphore_wait(barrier, 2)
    home = core == side
    out_copy = remote(image_ref, block_ref, diagonal, sems, 1)
    need(*"akpqjcd")
    dco = dot_nn(g2_ref[...].astype(BF), wco_ref[...]).astype(BF)
    to_heads(dout, dco)

    def cross_head(head, carry):
        probs = cross_probs(cq_ref[head], ckv_ref[0, head])
        dprobs = dot_nt(dout[head], ckv_ref[1, head])
        shift = jnp.sum(dprobs * probs, axis=1, keepdims=True)
        dscores = (probs * (dprobs - shift)).astype(BF)
        dout[head] = (dot_nn(dscores, ckv_ref[0, head]) * FACTOR).astype(BF)
        return carry

    lax.fori_loop(0, HEADS, cross_head, 0)
    gain = 1.0 + vec_ref[5:6, :]
    _, normal, inv = layer_norm(h2_ref[...], gain, vec_ref[6:7, :])
    cot[...] = g2_ref[...] + layer_back(
        dot_nt(from_heads(dout), wcq_ref[...]), normal, inv, gain
    )
    need("t")

    @pl.when(home)
    def _():
        block_ref[...] = image_ref[...]

    @pl.when(jnp.logical_not(home))
    def _():
        out_copy.start()

    need(*"in")
    dso = dot_nn(cot[...].astype(BF), wso_ref[...]).astype(BF)
    to_heads(dout, dso)
    prod = dso.astype(F32) * o_ref[...].astype(F32)
    head_row = lax.broadcasted_iota(jnp.int32, (HEADS, D), 0)
    head_col = lax.broadcasted_iota(jnp.int32, (HEADS, D), 1)
    low_edge = head_row * HEAD_DIM
    mark = jnp.where((head_col >= low_edge) & (head_col < low_edge + HEAD_DIM), 1.0, 0.0).astype(BF)
    high, rest = split_low(prod)
    delta[...] = dot_nt(mark, high) + dot_nt(mark, rest)
    need(*"lmo")
    for turn in range(2):
        half = core if turn == 1 else 1 - core
        span = pl.ds(pl.multiple_of(half * share, share), share)

        def one_head(head, carry, turn=turn, span=span):
            keys = kv_ref[0, head, span, :]
            vals = kv_ref[1, head, span, :]
            query = q_ref[head]
            grad = dout[head]
            scores = dot_nt(keys, query)
            probs = jnp.exp2(scores * (FACTOR * LOG_TWO_E) - lse_ref[pl.ds(head, 1), :])
            dprobs = dot_nt(vals, grad)
            dscores = (probs * (dprobs - delta[pl.ds(head, 1), :])).astype(BF)
            dval = dot_nn(probs.astype(BF), grad)
            dkey = dot_nn(dscores, query) * FACTOR
            dquery = dot_tn(keys, dscores)
            if turn == 0:
                dq_acc[head] = dquery
                give[0, head] = dkey.astype(BF)
                give[1, head] = dval.astype(BF)
            else:
                dq_acc[head] += dquery
                dkv_acc[0, head] = dkey
                dkv_acc[1, head] = dval
            return carry

        lax.fori_loop(0, HEADS, one_head, 0)
        if turn == 0:
            copy = send_to(where, give, take, sems, 0)
            copy.start()
    need(*"befghrs")
    for head in range(HEADS):
        dout[head] = (dq_acc[head].T * FACTOR).astype(BF)
    dq = from_heads(dout)
    gain = 1.0 + vec_ref[3:4, :]
    norm, normal, inv = layer_norm(h_ref[...], gain, vec_ref[4:5, :])
    low = norm.astype(BF)
    wide[:D, :] = wq_ref[...]
    wide[D:, :] = right_ref[...]
    back = dot_nt(dq, wide[...])
    low_rank = back[:, D:].astype(BF)
    outer = dot_tn(dot_nn(low, left_ref[...]).astype(BF), dq)
    one, two = factor_rows(outer, rows_ref[0:8, :], rows_ref[8:16, :])
    right_out[0] = one
    right_out[1] = two
    one, two = factor_rows(dot_tn(low_rank, low), cols_ref[0], cols_ref[1])
    left_out[0] = one
    left_out[1] = two
    total = back[:, :D] + dot_nt(low_rank, left_ref[...])
    copy.wait()
    for part in range(2):
        for head in range(HEADS):
            dout[head] = (dkv_acc[part, head] + take[part, head].astype(F32)).astype(BF)
        total += dot_nt(from_heads(dout), wkv_ref[part])
    g0_ref[...] = cot[...] + layer_back(total, normal, inv, gain)

    @pl.when(jnp.logical_not(home))
    def _():
        out_copy.wait()


BACK_OPERANDS = tuple("abcdefghijklmnopqrst")
BACK_FETCHES = "akpqjcdtinlmobefghrs"


def attention_back(*operands):
    share = operands[0].shape[0]
    given = dict(zip(BACK_OPERANDS, operands))
    outs = [
        ((share, D), F32, WHOLE),
        ((2, 8, D), F32, WHOLE),
        ((2, 8, D), F32, WHOLE),
        ((share, D), BF, WHOLE),
    ]
    scratch = [
        pltpu.VMEM((D + RANK_SQ, D), BF),
        pltpu.VMEM((HEADS, share, LANES), BF),
        pltpu.VMEM((share, D), F32),
        pltpu.VMEM((HEADS, share), F32),
        pltpu.VMEM((HEADS, LANES, share), F32),
        pltpu.VMEM((2, HEADS, share, LANES), F32),
        pltpu.VMEM((2, HEADS, share, LANES), BF),
        pltpu.VMEM((2, HEADS, share, LANES), BF),
        pltpu.SemaphoreType.DMA((2, 2)),
    ]

    outs, scratch = numbered("o", outs), numbered("s", scratch)

    def body(r):
        refs = [getattr(r, n) for n in BACK_OPERANDS + tuple(outs) + tuple(scratch)]
        attention_back_kernel(r.need, *refs)

    ins = {n: (given[n], None) for n in BACK_FETCHES}
    r = call_named(body, "attention_back", ins, outs, scratch, 4)
    return tuple(vars(r).values())


class Ring:
    def __init__(self, chips, ring_sems, core_sems, side_sems, own_sems):
        self.chips = chips
        self.half = chips // 2
        index = lax.axis_index("dp")
        self.plane = lax.axis_index("mp")
        self.core = lax.rem(index, 2)
        self.place = ring_place(index // 2, chips)
        self.right = ring_chip(self.place + 1, chips) * 2 + self.core
        self.left = ring_chip(self.place - 1, chips) * 2 + self.core
        self.index = index
        self.partner = index + 1 - 2 * self.core
        self.ring_sems, self.core_sems = ring_sems, core_sems
        self.side_sems, self.own_sems = side_sems, own_sems
        self.pieces = []

    def add(self, source, target, via=None, turn=0):
        self.pieces.append((source, target, via, turn))
        return len(self.pieces) - 1

    def last(self, which):
        turn = self.pieces[which][3]
        return (self.half - turn, self.half - 1 + turn)

    def spot(self, which, hop):
        return self.pieces[which][1](ring_chip(self.place - hop, self.chips) * 2 + self.core)

    def ring_copy(self, which, way, step):
        sign = 1 if way == 0 else -1
        spot = self.spot(which, sign * (step - 1))
        return pltpu.make_async_remote_copy(
            src_ref=self.pieces[which][0] if step == 1 else spot,
            dst_ref=spot,
            send_sem=self.ring_sems.at[0, way, which, step - 1],
            recv_sem=self.ring_sems.at[1, way, which, step - 1],
            device_id=(self.right if way == 0 else self.left, self.plane),
            device_id_type=MESH,
        )

    def core_copy(self, which, slot, hop):
        spot = self.spot(which, hop)
        return pltpu.make_async_remote_copy(
            src_ref=self.pieces[which][0] if slot == 0 else spot,
            dst_ref=spot,
            send_sem=self.core_sems.at[0, which, slot],
            recv_sem=self.core_sems.at[1, which, slot],
            device_id=(self.partner, self.plane),
            device_id_type=MESH,
        )

    def side_copy(self, which, slot, hop):
        spot = self.spot(which, hop)
        return pltpu.make_async_remote_copy(
            src_ref=spot,
            dst_ref=spot,
            send_sem=self.side_sems.at[0, which, slot],
            recv_sem=self.side_sems.at[1, which, slot],
            device_id=(self.index, 1 - self.plane),
            device_id_type=MESH,
        )

    def own_copy(self, which):
        return pltpu.make_async_copy(
            self.pieces[which][0], self.spot(which, 0), self.own_sems.at[which]
        )

    def on_ring(self, which, inside, outside=None):
        via = self.pieces[which][2]
        if via is None:
            inside()
            return
        pl.when(self.plane == via)(inside)
        if outside is not None:
            pl.when(self.plane != via)(outside)

    def begin(self, which):
        def inside():
            self.ring_copy(which, 0, 1).start()
            self.ring_copy(which, 1, 1).start()

        self.on_ring(which, inside)
        self.core_copy(which, 0, 0).start()
        self.own_copy(which).start()

    def event(self, which, way, step):
        slot = step if way == 0 else self.last(which)[0] + step
        hop = step if way == 0 else -step

        def inside():
            self.ring_copy(which, way, step).wait_recv()
            if step < self.last(which)[way]:
                self.ring_copy(which, way, step + 1).start()
            if self.pieces[which][2] is not None:
                self.side_copy(which, slot, hop).start()
            self.core_copy(which, slot, hop).start()

        self.on_ring(which, inside)

    def relay(self, which, way, step):
        slot = step if way == 0 else self.last(which)[0] + step
        hop = step if way == 0 else -step

        def outside():
            self.side_copy(which, slot, hop).wait_recv()
            self.core_copy(which, slot, hop).start()

        self.on_ring(which, lambda: None, outside)

    def plan(self, groups, starts):
        turns = [[] for _ in range(max(starts, default=0) + self.half + 3)]
        for number, group in enumerate(groups):
            for step in range(1, self.half + 1):
                turns[starts[number] + step] += [
                    (number, which, way, step)
                    for which in group
                    for way in (0, 1)
                    if step <= self.last(which)[way]
                ]
        events, late = [], [[], []]
        for at, turn in enumerate(turns):
            events += [(None, g) for g in range(len(groups)) if starts[g] == at and at > 0]
            events += [(False,) + e for e in turn] + [(True,) + e for e in late.pop(0)]
            late.append([e for e in turn if self.pieces[e[1]][2] is not None])
        return events

    def arrived(self, which):
        for slot in range(self.chips):
            self.core_copy(which, slot, 0).wait_recv()
        self.own_copy(which).wait()

    def drain(self, which):
        last = self.last(which)

        def inside():
            for way in (0, 1):
                for step in range(1, last[way] + 1):
                    self.ring_copy(which, way, step).wait_send()
            if self.pieces[which][2] is not None:
                for slot in range(1, self.chips):
                    self.side_copy(which, slot, 0).wait_send()

        self.on_ring(which, inside)
        for slot in range(self.chips):
            self.core_copy(which, slot, 0).wait_send()


def remote(src, dst, where, sems, slot):
    return pltpu.make_async_remote_copy(
        src_ref=src,
        dst_ref=dst,
        send_sem=sems.at[0, slot],
        recv_sem=sems.at[1, slot],
        device_id=where,
        device_id_type=MESH,
    )


MEMBERS = D // GROUPS


def group_mean(column):
    column = jnp.broadcast_to(column, (8, D))
    lane = lax.broadcasted_iota(jnp.int32, (8, D), 1)
    first = lane == 0
    for group in range(1, GROUPS):
        first = first | (lane == group * MEMBERS)

    def shift(values, count):
        return pltpu.roll(values, count % D, 1)

    two = column + shift(column, -1)
    four = two + shift(two, -2)
    eight = four + shift(four, -4)
    whole = eight + shift(eight, -8) + shift(four, -16)
    whole = jnp.where(first, whole, 0.0)
    two = whole + shift(whole, 1)
    four = two + shift(two, 2)
    eight = four + shift(four, 4)
    spread = eight + shift(eight, 8) + shift(four, 16)
    return spread[0:1, :] * (1.0 / MEMBERS)


def col_mean(values):
    return jnp.sum(values, axis=0, keepdims=True) * (1.0 / values.shape[0])


def side_by_side(wide, values, order):
    rows = values.shape[0]
    column = lax.broadcasted_iota(jnp.int32, (rows, D), 0) & (SIDE - 1)
    before = jnp.where(column == 0, 0.0, pltpu.roll(values, 1, 0)).astype(BF)
    after = jnp.where(column == SIDE - 1, 0.0, pltpu.roll(values, rows - 1, 0)).astype(BF)
    parts = (before, values.astype(BF), after)
    for spot, part in enumerate(order):
        wide[:, spot * D : (spot + 1) * D] = parts[part]


def swap_edges(act, edge_send, edge_got, core, partner, sems, slot):
    share = act.shape[0] - 2 * SIDE
    start = pl.multiple_of(share - (share - SIDE) * core, SIDE)
    edge_send[...] = act[pl.ds(start, SIDE), :].astype(BF)
    copy = remote(edge_send, edge_got, partner, sems, slot)
    copy.start()
    copy.wait()
    border = edge_got[...].astype(F32)
    top = (core == 1).astype(F32)
    act[:SIDE, :] = border * top
    act[SIDE + share :, :] = border * (1.0 - top)


SHARDS = ("one", "time", "two", "q", "kv", "so", "cq", "ckv", "co", "ff")


def call_named(body, name, ins, outs, scratch, collective):
    anywhere = pl.BlockSpec(memory_space=pl.ANY)
    fetched = [n for n, i in ins.items() if i[1] is None]
    flushed = [n for n, o in outs.items() if o[2] is None]
    scratch = dict(scratch)
    for n in fetched:
        scratch[n] = pltpu.VMEM(ins[n][0].shape, ins[n][0].dtype)
    for n in flushed:
        scratch[n] = pltpu.VMEM(outs[n][0], outs[n][1])
    scratch["fetch_sems"] = pltpu.SemaphoreType.DMA((max(len(fetched), 1),))
    scratch["flush_sems"] = pltpu.SemaphoreType.DMA((max(len(flushed), 1),))
    held = lambda n, spec: "hbm_" + n if spec is None else n
    names = [held(n, i[1]) for n, i in ins.items()] + [held(n, o[2]) for n, o in outs.items()]
    names += list(scratch)

    def kernel(*refs):
        r = types.SimpleNamespace(**dict(zip(names, refs)))
        loads, stores = {}, []
        for slot, n in enumerate(fetched):
            copy = pltpu.make_async_copy(
                getattr(r, "hbm_" + n), getattr(r, n), r.fetch_sems.at[slot]
            )
            copy.start()
            loads[n] = copy

        def need(*wanted):
            for n in wanted:
                if n in loads:
                    loads.pop(n).wait()

        def flush(*done):
            for n in done:
                copy = pltpu.make_async_copy(
                    getattr(r, n), getattr(r, "hbm_" + n), r.flush_sems.at[flushed.index(n)]
                )
                copy.start()
                stores.append(copy)

        r.need, r.flush = need, flush
        body(r)
        need(*fetched)
        for copy in stores:
            copy.wait()

    results = pl.pallas_call(
        kernel,
        out_shape=[jax.ShapeDtypeStruct(o[0], o[1]) for o in outs.values()],
        in_specs=[i[1] or anywhere for i in ins.values()],
        out_specs=[o[2] or anywhere for o in outs.values()],
        scratch_shapes=list(scratch.values()),
        compiler_params=pltpu.CompilerParams(
            collective_id=collective, has_side_effects=True, vmem_limit_bytes=VMEM_BYTES
        ),
        name=name,
    )(*[i[0] for i in ins.values()])
    return types.SimpleNamespace(**dict(zip(outs, results)))


def numbered(mark, items):
    return {mark + str(spot): item for spot, item in enumerate(items)}


def expand_left(left, which):
    row = lax.broadcasted_iota(jnp.int32, (8, RANK_SQ), 0)
    col = lax.broadcasted_iota(jnp.int32, (8, RANK_SQ), 1)
    chosen = (col >> 3) if which == 0 else (col & 7)
    mark = jnp.where(row == chosen, 1.0, 0.0)
    return lax.dot_general(
        left,
        mark,
        (((0,), (0,)), ((), ())),
        precision=lax.Precision.HIGHEST,
        preferred_element_type=F32,
    )


def factor_rows(outer, first, second):
    grad_first = [
        jnp.sum(outer[8 * r : 8 * r + 8] * second, axis=0, keepdims=True) for r in range(8)
    ]
    grad_second = sum(outer[8 * r : 8 * r + 8] * first[r : r + 1] for r in range(8))
    return jnp.concatenate(grad_first, axis=0), grad_second


STARTS = (0, 2, 4, 5, 6, 7, 8, 9)


def forward_body(chips, gathers, r):
    ring = Ring(chips, r.ring_sems, r.pair_sems, r.over_sems, r.own_sems)
    core, side = ring.core, ring.plane
    neighbour = (ring.index, 1 - side)
    partner = (ring.partner, side)
    diagonal = (ring.partner, 1 - side)
    home = core == side
    away = jnp.logical_not(home)
    barrier = pltpu.get_barrier_semaphore()
    others = [partner, neighbour, diagonal]
    if gathers:
        others += [(ring.right, side), (ring.left, side)]
    for where in others:
        pl.semaphore_signal(barrier, inc=1, device_id=where, device_id_type=MESH)
    pl.semaphore_wait(barrier, len(others))

    shard = {name: getattr(r, "in_" + name) for name in SHARDS} if gathers else {}
    got = {name: getattr(r, "got_" + name) for name in shard}
    joined = {name: getattr(r, "wide_" + name) for name in shard}
    full = {name: getattr(r, "full_" + name) for name in SHARDS}
    side_copies = {}
    for slot, name in enumerate(shard):
        if name != "one":
            side_copies[name] = remote(
                getattr(r, "hbm_in_" + name), got[name], neighbour, r.side_sems, slot
            )
    first_copies = []
    if gathers:
        for u in range(3):
            part = slice(3 * u, 3 * u + 3)
            copy = remote(
                r.hbm_in_one.at[part], got["one"].at[part], neighbour, r.first_sems, u
            )
            copy.start()
            first_copies.append(copy)
    core_copies = {}
    for slot, name in enumerate(("lat", "emb", "text", "scale")):
        source = r.scale if name == "scale" else getattr(r, "hbm_" + name)
        core_copies[name] = remote(source, getattr(r, "got_" + name), partner, r.core_sems, slot)
    core_copies["lat"].start()
    core_copies["emb"].start()
    flat = ("split", "bias", "qr", "ur")
    for slot, name in enumerate(flat):
        side_copies["f_" + name] = remote(
            getattr(r, "hbm_" + name),
            getattr(r, "got_" + name),
            neighbour,
            r.side_sems,
            len(SHARDS) + slot,
        )
    core_copies["text"].start()

    def send(*names):
        for name in names:
            side_copies[name].start()

    if gathers:
        send("time", "two")
    send("f_split", "f_qr")

    def join(name, first=0, count=None):
        r.need("in_" + name)
        if count is None:
            side_copies[name].wait_recv()
        mine, theirs, out = shard[name], got[name], joined[name]
        for lead in range(first, first + (count or mine.shape[0])):

            @pl.when(side == 0)
            def _():
                out[lead] = jnp.concatenate([mine[lead], theirs[lead]], axis=1)

            @pl.when(side == 1)
            def _():
                out[lead] = jnp.concatenate([theirs[lead], mine[lead]], axis=1)

    def piece(name, start, size, via=None, turn=0, first=0, count=None):
        rows = shard[name].shape[1]
        count = joined[name].shape[2] if count is None else count

        def target(owner):
            at = pl.multiple_of(owner * rows, 8)
            return full[name].at[start : start + size, pl.ds(at, rows), first : first + count]

        source = joined[name].at[start : start + size, :, first : first + count]
        return ring.add(source, target, via, turn)

    def taps(name):
        return [piece(name, 0, 3, 0, 0), piece(name, 3, 3, 1, 0), piece(name, 6, 3, None, 1)]

    groups = []
    if gathers:
        quarter = joined["ff"].shape[2] // 4
        groups = [
            [piece("one", 3 * u, 3, None, u % 2) for u in range(3)],
            [piece("time", 0, 1)] + taps("two"),
            [
                piece("q", 0, 1),
                piece("kv", 0, 1, 0, 0),
                piece("kv", 1, 1, 1, 0),
                piece("so", 0, 1, None, 1),
            ],
            [
                piece("cq", 0, 1),
                piece("ckv", 0, 1, 0, 0),
                piece("ckv", 1, 1, 1, 0),
                piece("co", 0, 1, None, 1),
            ],
        ]
        for part in range(4):
            first = part * quarter
            groups.append(
                [
                    piece("ff", 0, 1, 0, 0, first, quarter),
                    piece("ff", 1, 1, 1, 0, first, quarter),
                    piece("ff", 2, 1, None, 1, first, quarter),
                ]
            )
    events = ring.plan(groups, STARTS[: len(groups)])

    def poll(limit=5):
        while events and limit > 0:
            kind, number, *rest = events.pop(0)
            if kind is None:
                for which in groups[number]:
                    ring.begin(which)
            elif kind:
                ring.relay(*rest)
            else:
                limit -= 1
                ring.event(*rest)

    def poll_group(number):
        while any(e[1] <= number for e in events):
            poll(1)

    def arrived(number, position):
        if gathers:
            ring.arrived(groups[number][position])

    def load(name, start, size, target, slot):
        copy = pltpu.make_async_copy(
            full[name].at[start : start + size] if size else full[name].at[start],
            target,
            r.load_sems.at[slot],
        )
        copy.start()
        return copy

    r.need("lat")
    core_copies["lat"].wait_recv()

    @pl.when(home)
    def _():
        r.image[...] = r.lat[...]

    @pl.when(away)
    def _():
        r.image[...] = r.got_lat[...]

    if gathers:
        for u in range(3):
            first_copies[u].wait_recv()
            join("one", 3 * u, 3)
            ring.begin(groups[0][u])
        send("q", "kv", "so", "cq", "ckv", "co")
    share = r.image.shape[0] // 2
    mine = pl.ds(pl.multiple_of(core * share, share), share)
    r.need("vec")
    pixels = r.image[...].astype(F32)
    mean_one = group_mean(col_mean(pixels))
    centred = pixels - mean_one
    inv_one = lax.rsqrt(group_mean(col_mean(centred * centred)) + NORM_EPS)
    slope = inv_one * (1.0 + r.vec[0:1, :])

    def first_act(values):
        pre = (values.astype(F32) - mean_one) * slope + r.vec[1:2, :]
        return pre * jax.nn.sigmoid(pre)

    r.img[...] = r.image[mine, :]
    r.flush("img")
    r.act[SIDE : SIDE + share, :] = first_act(r.image[mine, :])
    border = first_act(r.image[pl.ds(pl.multiple_of(share - SIDE * core, SIDE), SIDE), :])
    top = (core == 1).astype(F32)
    r.act[:SIDE, :] = border * top
    r.act[SIDE + share :, :] = border * (1.0 - top)
    side_by_side(r.wide, r.act[...], (0, 1, 2))
    if gathers:
        join("time")
        join("two")
        send("ff")
    send("f_bias", "f_ur")
    poll(6)
    for name in SHARDS[3:-1] if gathers else ():
        join(name)
    poll(6)
    if gathers:
        join("ff")

    r.need(*flat, "ql", "ul", "step", "group", "step_weights", "group_weights", "cot", "emb", "text")
    for name in flat:
        side_copies["f_" + name].wait_recv()
        own_part, got_part, whole = (
            getattr(r, name),
            getattr(r, "got_" + name),
            getattr(r, "all_" + name),
        )

        @pl.when(side == 0)
        def _():
            whole[...] = jnp.concatenate([own_part[...], got_part[...]], axis=1)

        @pl.when(side == 1)
        def _():
            whole[...] = jnp.concatenate([got_part[...], own_part[...]], axis=1)

    for row in range(8):
        rows = slice(8 * row, 8 * row + 8)
        r.zq[rows, :] = (r.all_qr[row : row + 1, :] * r.all_qr[8:16, :]).astype(BF)
        for part in range(2):
            base = 16 * part
            r.zu[part, rows, :] = (
                r.all_ur[base + row : base + row + 1, :] * r.all_ur[base + 8 : base + 16, :]
            ).astype(BF)
    poll()
    for left, pair in ((r.ql, r.yq), (r.ul, r.yu)):
        pair[...] = (expand_left(left[0], 0) * expand_left(left[1], 1)).astype(BF)

    poll()

    def chosen(table, spot):
        lane = lax.broadcasted_iota(jnp.int32, table.shape, 1)
        return jnp.sum(jnp.where(lane == spot[...], table[...], 0.0), axis=1, keepdims=True)

    scale = chosen(r.step_weights, r.step) * chosen(r.group_weights, r.group)
    r.scale[...] = jnp.broadcast_to(scale, r.scale.shape)
    core_copies["scale"].start()
    cot_copy = remote(r.hbm_cot, r.all_cot, diagonal, r.core_sems, 6)

    @pl.when(home)
    def _():
        r.all_cot[...] = r.cot[...]

    @pl.when(away)
    def _():
        cot_copy.start()

    core_copies["emb"].wait_recv()
    core_copies["text"].wait_recv()
    core_copies["scale"].wait_recv()
    own = home.astype(F32)
    r.scale_out[...] = r.scale[...] * own + r.got_scale[...] * (1.0 - own)
    count = r.text.shape[0]

    @pl.when(home)
    def _():
        r.text_all[:count, :] = r.text[...]

    @pl.when(away)
    def _():
        r.text_all[:count, :] = r.got_text[...]

    r.text_all[count:, :] = jnp.zeros((LANES - count, r.text.shape[1]), BF)
    poll_group(0)

    loads = []
    for u in range(3):
        arrived(0, u)
        loads.append(load("one", 3 * u, 3, r.kernels.at[3 * u : 3 * u + 3], u))
    for u in range(3):
        loads[u].wait()
        term = dot_nn(
            r.wide[u * SIDE : u * SIDE + share, :],
            r.kernels[3 * u : 3 * u + 3].reshape(3 * D, D),
        )
        if u == 0:
            r.h1[...] = term
        else:
            r.h1[...] += term
        poll()
    while any(len(e) > 2 and e[2] == groups[1][0] for e in events):
        poll(1)
    arrived(1, 0)
    time_load = load("time", 0, 0, r.time_buf, 3)
    time_load.wait()
    embed = r.emb[...] * own + r.got_emb[...] * (1.0 - own)
    embed = (embed * jax.nn.sigmoid(embed)).astype(BF)
    shift = dot_nn(jnp.broadcast_to(embed, (8, embed.shape[1])), r.time_buf[...])[0:1, :]
    inner = r.h1[...] + (r.all_split[0:1, :] + (shift + r.all_split[1:2, :]))
    r.h1[...] = inner
    r.flush("h1")
    poll()
    local_mean = group_mean(col_mean(inner))
    local_dev = inner - local_mean
    local_var = group_mean(col_mean(local_dev * local_dev))
    r.stat_send[0:1, :] = local_mean
    r.stat_send[1:2, :] = local_var
    stat_copy = remote(r.stat_send, r.stat_got, partner, r.core_sems, 4)
    stat_copy.start()
    poll()
    stat_copy.wait()
    other_mean, other_var = r.stat_got[0:1, :], r.stat_got[1:2, :]
    mean_two = 0.5 * (local_mean + other_mean)
    gap = 0.5 * (local_mean - other_mean)
    inv_two = lax.rsqrt(0.5 * (local_var + other_var) + gap * gap + NORM_EPS)
    r.stats[0:1, :] = mean_one
    r.stats[1:2, :] = inv_one
    r.stats[2:3, :] = mean_two
    r.stats[3:4, :] = inv_two
    r.stats[4:8, :] = jnp.zeros((4, D), F32)
    pre = (r.h1[...] - mean_two) * (inv_two * (1.0 + r.all_split[2:3, :])) + r.all_split[3:4, :]
    r.act[SIDE : SIDE + share, :] = pre * jax.nn.sigmoid(pre)
    swap_edges(r.act, r.edge_send, r.edge_got, core, partner, r.core_sems, 5)
    side_by_side(r.wide, r.act[...], (0, 1, 2))
    poll_group(1)

    loads = []
    for u in range(3):
        arrived(1, 1 + u)
        loads.append(load("two", 3 * u, 3, r.kernels.at[3 * u : 3 * u + 3], u))
    for u in range(3):
        loads[u].wait()
        term = None
        for w in range(3):
            part = dot_nt(
                r.wide[u * SIDE : u * SIDE + share, w * D : (w + 1) * D], r.kernels[3 * u + w]
            )
            term = part if term is None else term + part
        if u == 0:
            r.h[...] = term
        else:
            r.h[...] += term
        poll()
    r.h[...] = r.img[...].astype(F32) + (r.h[...] + r.vec[2:3, :])
    r.flush("h")

    poll_group(2)
    loads = []
    for slot, (name, spots, at, size) in enumerate(
        (("kv", (1, 2), 1, 2), ("q", (0,), 0, 1), ("so", (3,), 3, 1))
    ):
        for spot in spots:
            arrived(2, spot)
        loads.append(load(name, 0, size, r.kernels.at[at : at + size], slot))
    norm, _, _ = layer_norm(r.h[...], 1.0 + r.vec[3:4, :], r.vec[4:5, :])
    low = norm.astype(BF)
    loads[0].wait()
    for part in range(2):
        proj = dot_nn(low, r.kernels[1 + part]).astype(BF)
        blank = jnp.zeros((share, LANES - HEAD_DIM), BF)
        for head in range(HEADS):
            span = proj[:, HEAD_DIM * head : HEAD_DIM * (head + 1)]
            r.kv[part, head, mine, :] = jnp.concatenate([span, blank], axis=1)
    kv_copy = remote(r.kv.at[:, :, mine, :], r.kv.at[:, :, mine, :], partner, r.core_sems, 7)
    kv_copy.start()
    poll()
    loads[1].wait()
    r.ext_act[:, :D] = low
    r.ext_act[:, D:] = dot_nn(low, r.yq[...]).astype(BF)
    r.ext_w[:D, :] = r.kernels[0]
    r.ext_w[D:, :] = r.zq[...]
    to_heads(r.q, dot_nn(r.ext_act[...], r.ext_w[...]).astype(BF))
    poll()
    kv_copy.wait()
    r.flush("kv", "q")
    lane = lax.broadcasted_iota(jnp.int32, (share, LANES), 1)
    r.lse_cols[...] = jnp.zeros_like(r.lse_cols)

    def one_head(head, carry):
        scores = dot_nt(r.q[head], r.kv[0, head])
        peak = jnp.max(scores, axis=1, keepdims=True)
        expo = jnp.exp2((scores - peak) * (FACTOR * LOG_TWO_E))
        total = jnp.sum(expo, axis=1, keepdims=True)
        probs = (expo * (1.0 / total)).astype(BF)
        r.heads[head] = dot_nn(probs, r.kv[1, head]).astype(BF)
        row = peak * (FACTOR * LOG_TWO_E) + jnp.log2(total)
        r.lse_cols[...] = jnp.where(lane == head, row, r.lse_cols[...])
        return carry

    for first in range(0, HEADS, 2):
        lax.fori_loop(first, first + 2, one_head, 0)
        poll()
    r.lse[...] = r.lse_cols[...].T
    merged = from_heads(r.heads)
    r.o[...] = merged
    r.flush("lse", "o")
    loads[2].wait()
    r.h2[...] = r.h[...] + (dot_nt(merged, r.kernels[3]) + r.vec[9:10, :])
    r.flush("h2")

    poll()
    poll_group(3)
    for position in range(4):
        arrived(3, position)
    loads = [
        load("cq", 0, 1, r.kernels.at[4:5], 0),
        load("ckv", 0, 2, r.text_kv, 1),
        load("co", 0, 1, r.kernels.at[5:6], 2),
    ]
    norm, _, _ = layer_norm(r.h2[...], 1.0 + r.vec[5:6, :], r.vec[6:7, :])
    poll()
    loads[0].wait()
    to_heads(r.cq, dot_nn(norm.astype(BF), r.kernels[4]).astype(BF))
    loads[1].wait()
    for part in range(2):
        to_heads(r.ckv.at[part], dot_nn(r.text_all[...], r.text_kv[part]).astype(BF))

    poll()

    def cross_head(head, carry):
        probs = cross_probs(r.cq[head], r.ckv[0, head])
        r.heads[head] = dot_nn(probs.astype(BF), r.ckv[1, head]).astype(BF)
        return carry

    lax.fori_loop(0, HEADS, cross_head, 0)
    loads[2].wait()
    r.h3[...] = r.h2[...] + (dot_nt(from_heads(r.heads), r.kernels[5]) + r.vec[10:11, :])

    r.flush("cq", "ckv")
    poll()

    gain = 1.0 + r.vec[7:8, :]
    norm, _, _ = layer_norm(r.h3[...], gain, r.vec[8:9, :])
    low = norm.astype(BF)
    r.ext_act[:, :D] = low
    r.ext_act[:, D:] = dot_nn(low, r.yu[...]).astype(BF)

    @pl.when(away)
    def _():
        cot_copy.wait()

    r.cot_low[...] = (r.all_cot[...].astype(F32) * r.scale_out[0:1, 0:1]).astype(BF)
    down_acc = r.act.at[:share, :]
    quarter = full["ff"].shape[2] // 4
    for part in range(4):
        poll_group(4 + part)
        for position in range(3):
            arrived(4 + part, position)
        first = part * quarter
        span = slice(first, first + quarter)
        slots = r.kernels.at[3 * (part % 2) : 3 * (part % 2) + 3]
        copy = pltpu.make_async_copy(full["ff"].at[:, :, span], slots, r.load_sems.at[part])
        copy.start()
        copy.wait()
        for half in range(2):
            cols = slice(half * quarter, (half + 1) * quarter)
            r.ff_wide[:D, cols] = slots[half]
            r.ff_wide[D:, cols] = r.zu[half, :, span]
        poll(4)
        mixed = dot_nn(r.ext_act[...], r.ff_wide[...])
        value = mixed[:, :quarter] + r.all_bias[0:1, span]
        gate = mixed[:, quarter:] + r.all_bias[1:2, span]
        cdf = 0.5 * (1.0 + lax.erf(gate * INV_ROOT_TWO))
        gelu = gate * cdf
        slope = cdf + gate * jnp.exp(-0.5 * gate * gate) * INV_ROOT_TWOPI
        poll(4)
        hidden_grad = dot_nn(r.cot_low[...], slots[2])
        r.ff_grads[:, :quarter] = (hidden_grad * gelu).astype(BF)
        r.ff_grads[:, quarter:] = (hidden_grad * value * slope).astype(BF)
        down = dot_nt((value * gelu).astype(BF), slots[2])
        poll(4)
        outer = dot_tn(r.ext_act[:, D:], r.ff_grads[...])
        for half in range(2):
            base = 16 * half
            one, two = factor_rows(
                outer[:, half * quarter : (half + 1) * quarter],
                r.all_ur[base : base + 8, span],
                r.all_ur[base + 8 : base + 16, span],
            )
            r.up_right[0, half, :, span] = one
            r.up_right[1, half, :, span] = two
        back = dot_nt(r.ff_grads[...], r.ff_wide[...])
        if part == 0:
            down_acc[...] = down
            r.back_acc[...] = back
        else:
            down_acc[...] += down
            r.back_acc[...] += back
        poll(4)
    r.flush("up_right")
    r.out_img[...] = (r.h3[...] + (down_acc[...] + r.vec[11:12, :])).astype(BF)
    r.flush("out_img")
    low_rank = r.back_acc[:, D:].astype(BF)
    one, two = factor_rows(dot_tn(low_rank, r.ext_act[:, :D]), r.ul[0], r.ul[1])
    r.up_left[0] = one
    r.up_left[1] = two
    normed_grad = r.back_acc[:, :D] + dot_nt(low_rank, r.yu[...])
    _, normal, inv = layer_norm(r.h3[...], gain, r.vec[8:9, :])
    cot = r.all_cot[...].astype(F32) * r.scale_out[0:1, 0:1]
    r.g2[...] = cot + layer_back(normed_grad, normal, inv, gain)
    r.flush("g2")
    poll(len(events))
    for group in groups:
        for which in group:
            ring.drain(which)
    for copy in first_copies + list(side_copies.values()) + list(core_copies.values()):
        copy.wait_send()


def forward(arrays, shards, full, chips):
    gathers = full is None
    share = arrays["lat"].shape[0] // 2
    anywhere = pl.BlockSpec(memory_space=pl.ANY)
    dma = pltpu.SemaphoreType.DMA
    ins = {name: (arrays[name], None) for name in ("lat", "vec")}
    if gathers:
        ins["in_one"] = (shards[0], None)
    ins.update({name: (value, None) for name, value in arrays.items()})
    text_rows, text_width = arrays["text"].shape
    time_width = arrays["emb"].shape[1]

    def double(name):
        rows, cols = arrays[name].shape
        return (rows, 2 * cols)

    outs = {
        "h": ((share, D), F32, None),
        "h1": ((share, D), F32, None),
        "img": ((share, D), BF, None),
        "stats": ((8, D), F32, WHOLE),
        "h2": ((share, D), F32, None),
        "q": ((HEADS, share, LANES), BF, None),
        "kv": ((2, HEADS, 2 * share, LANES), BF, None),
        "o": ((share, D), BF, None),
        "lse": ((LANES, share), F32, None),
        "cq": ((HEADS, share, LANES), BF, None),
        "ckv": ((2, HEADS, LANES, LANES), BF, None),
        "all_split": (double("split"), F32, WHOLE),
        "all_qr": (double("qr"), F32, WHOLE),
        "yq": ((D, RANK_SQ), BF, WHOLE),
        "zq": ((RANK_SQ, D), BF, WHOLE),
        "out_img": ((share, D), BF, None),
        "g2": ((share, D), F32, None),
        "up_right": ((2, 2, 8, double("ur")[1]), F32, None),
        "up_left": ((2, 8, D), F32, WHOLE),
    }
    scratch = {}
    if gathers:
        for name, value in zip(SHARDS, shards):
            lead, rows, cols = value.shape
            ins["in_" + name] = (value, None)
            outs["full_" + name] = ((lead, rows * chips * 2, 2 * cols), BF, anywhere)
            scratch["got_" + name] = pltpu.VMEM(value.shape, BF)
            scratch["wide_" + name] = pltpu.VMEM((lead, rows, 2 * cols), BF)
    else:
        for name, value in zip(SHARDS, full):
            ins["full_" + name] = (value, anywhere)
    for name in ("lat", "emb", "text", "split", "bias", "qr", "ur"):
        value = arrays[name]
        scratch["got_" + name] = pltpu.VMEM(value.shape, value.dtype)
    pieces = 27 if gathers else 1
    hidden = double("ur")[1]
    scratch.update(
        image=pltpu.VMEM(arrays["lat"].shape, BF),
        kernels=pltpu.VMEM((9, D, D), BF),
        time_buf=pltpu.VMEM((time_width, D), BF),
        text_kv=pltpu.VMEM((2, text_width, D), BF),
        text_all=pltpu.VMEM((LANES, text_width), BF),
        wide=pltpu.VMEM((share + 2 * SIDE, 3 * D), BF),
        act=pltpu.VMEM((share + 2 * SIDE, D), F32),
        scale=pltpu.VMEM((8, LANES), F32),
        got_scale=pltpu.VMEM((8, LANES), F32),
        stat_send=pltpu.VMEM((8, D), F32),
        stat_got=pltpu.VMEM((8, D), F32),
        edge_send=pltpu.VMEM((SIDE, D), BF),
        edge_got=pltpu.VMEM((SIDE, D), BF),
        ext_act=pltpu.VMEM((share, D + RANK_SQ), BF),
        ext_w=pltpu.VMEM((D + RANK_SQ, D), BF),
        heads=pltpu.VMEM((HEADS, share, LANES), BF),
        lse_cols=pltpu.VMEM((share, LANES), F32),
        h3=pltpu.VMEM((share, D), F32),
        all_bias=pltpu.VMEM(double("bias"), F32),
        all_ur=pltpu.VMEM(double("ur"), F32),
        yu=pltpu.VMEM((D, RANK_SQ), BF),
        zu=pltpu.VMEM((2, RANK_SQ, hidden), BF),
        all_cot=pltpu.VMEM((share, D), BF),
        scale_out=pltpu.VMEM((8, LANES), F32),
        cot_low=pltpu.VMEM((share, D), BF),
        ff_wide=pltpu.VMEM((D + RANK_SQ, hidden // 2), BF),
        ff_grads=pltpu.VMEM((share, hidden // 2), BF),
        back_acc=pltpu.VMEM((share, D + RANK_SQ), F32),
        first_sems=dma((2, 3)),
        side_sems=dma((2, len(SHARDS) + 4)),
        core_sems=dma((2, 8)),
        load_sems=dma((4,)),
        ring_sems=dma((2, 2, pieces, chips // 2)),
        pair_sems=dma((2, pieces, chips)),
        over_sems=dma((2, pieces, chips)),
        own_sems=dma((pieces,)),
    )
    return call_named(
        functools.partial(forward_body, chips, gathers), "forward", ins, outs, scratch, 1
    )


class Halving:
    HALVINGS = 3

    def __init__(self, steps, acc, got, out, sems):
        self.acc, self.got, self.out, self.sems, self.steps = acc, got, out, sems, steps
        index = lax.axis_index("dp")
        plane = lax.axis_index("mp")
        core = lax.rem(index, 2)
        chip = index // 2
        self.partners = [((index + 1 - 2 * core, plane), core), ((index, 1 - plane), plane)]
        span = 1
        for _ in range(steps - 2):
            bit = lax.rem(chip // span, 2)
            self.partners.append((((chip + span - 2 * span * bit) * 2 + core, plane), bit))
            span *= 2
        self.offset, self.size, self.base = 0, acc.shape[0], 0
        self.trail = []
        self.flight = None
        self.done = 0

    @classmethod
    def room(cls, rows, steps):
        small = rows >> cls.HALVINGS
        return rows - small + small * (steps - cls.HALVINGS)

    def begin(self):
        self._down(0)

    def _down(self, step):
        where, bit = self.partners[step]
        if step < self.HALVINGS:
            size = self.size // 2
            mine = pl.multiple_of(self.offset + bit * size, 8)
            theirs = pl.multiple_of(self.offset + (1 - bit) * size, 8)
        else:
            size, mine, theirs = self.size, self.offset, self.offset
        copy = remote(
            self.acc.at[pl.ds(theirs, size), :],
            self.got.at[pl.ds(self.base, size), :],
            where,
            self.sems,
            step,
        )
        copy.start()
        self.flight = (copy, mine, size)

    def _up(self, step):
        mine, size, where = self.trail[step]
        part = self.out.at[pl.ds(mine, size), :]
        copy = remote(part, part, where, self.sems, self.steps + step)
        copy.start()
        self.flight = (copy, mine, size)

    def step(self):
        steps, total = self.steps, self.steps + self.HALVINGS
        if self.done >= total:
            return
        copy, mine, size = self.flight
        copy.wait()
        if self.done < steps:
            self.acc[pl.ds(mine, size), :] += self.got[pl.ds(self.base, size), :]
            self.trail.append((mine, size, self.partners[self.done][0]))
            self.offset, self.size = mine, size
            self.base += size
            if self.done + 1 < steps:
                self._down(self.done + 1)
            else:
                self.out[pl.ds(mine, size), :] = self.acc[pl.ds(mine, size), :]
                self._up(self.HALVINGS - 1)
        elif self.done + 1 < total:
            self._up(total - 2 - self.done)
        self.done += 1


def conv_back_kernel(
    steps,
    need,
    g0_ref,
    h1_ref,
    img_ref,
    stat_ref,
    split_ref,
    vec_ref,
    up_right_ref,
    up_left_ref,
    query_right_ref,
    query_left_ref,
    ql_state,
    qr_state,
    ul_state,
    ur_state,
    one_ref,
    two_ref,
    grad_ref,
    ql_new,
    ql_copy,
    qr_new,
    qr_copy,
    ul_new,
    ul_copy,
    ur_new,
    ur_copy,
    moments,
    sum_ref,
    one_buf,
    two_buf,
    wide,
    act,
    half_back,
    stat_send,
    stat_got,
    edge_send,
    edge_got,
    acc,
    got,
    half_row,
    load_sems,
    core_sems,
    sum_sems,
    back_sems,
):
    index = lax.axis_index("dp")
    side = lax.axis_index("mp")
    core = lax.rem(index, 2)
    partner = (index + 1 - 2 * core, side)
    neighbour = (index, 1 - side)
    diagonal = (index + 1 - 2 * core, 1 - side)
    share = g0_ref.shape[0]
    loads = []
    for slot, (src, dst) in enumerate(((two_ref, two_buf), (one_ref, one_buf))):
        load = pltpu.make_async_copy(src, dst, load_sems.at[slot])
        load.start()
        loads.append(load)
    total = Halving(steps, acc, got, sum_ref, sum_sems)
    barrier = pltpu.get_barrier_semaphore()
    for where, _ in total.partners:
        pl.semaphore_signal(barrier, inc=1, device_id=where, device_id_type=MESH)
    pl.semaphore_signal(barrier, inc=1, device_id=diagonal, device_id_type=MESH)
    need("g0", "up_right", "up_left", "query_right", "query_left")
    parts = []
    for member in range(2):
        for part in range(2):
            for block in range(up_right_ref.shape[3] // D):
                parts.append(up_right_ref[member, part, :, block * D : (block + 1) * D])
    for ref in (query_right_ref, up_left_ref, query_left_ref):
        parts += [ref[0], ref[1]]
    for spot, part in enumerate(parts):
        acc[8 * spot : 8 * spot + 8, :] = part
    acc[8 * len(parts) :, :] = jnp.zeros((acc.shape[0] - 8 * len(parts), D), F32)
    act[SIDE : SIDE + share, :] = g0_ref[...]
    pl.semaphore_wait(barrier, steps + 1)
    total.begin()
    swap_edges(act, edge_send, edge_got, core, partner, core_sems, 0)
    side_by_side(wide, act[...], (2, 1, 0))
    total.step()
    inner = act.at[SIDE : SIDE + share, :]
    loads[0].wait()
    for u in range(3):
        term = dot_nn(
            wide[u * SIDE : u * SIDE + share, :],
            two_buf[3 * (2 - u) : 3 * (2 - u) + 3].reshape(3 * D, D),
        )
        if u == 0:
            inner[...] = term
        else:
            inner[...] += term
        total.step()
    need("h1", "stats", "split")
    mean_two, inv_two = stat_ref[2:3, :], stat_ref[3:4, :]
    gain_two = 1.0 + split_ref[2:3, :]
    normal = (h1_ref[...] - mean_two) * inv_two
    scaled = inner[...] * silu_slope(normal * gain_two + split_ref[3:4, :]) * gain_two
    means = pair_means(scaled, normal, stat_send, stat_got, partner, core_sems, 1)
    inner[...] = inv_two * (scaled - means[0] - normal * means[1])
    swap_edges(act, edge_send, edge_got, core, partner, core_sems, 2)
    side_by_side(wide, act[...], (2, 1, 0))
    total.step()
    loads[1].wait()
    for u in range(3):
        term = None
        for spot in range(3):
            part = dot_nt(
                wide[u * SIDE : u * SIDE + share, spot * D : (spot + 1) * D],
                one_buf[3 * (2 - u) + spot],
            )
            term = part if term is None else term + part
        if u == 0:
            inner[...] = term
        else:
            inner[...] += term
        total.step()
    need("img", "vec")
    mean_one, inv_one = stat_ref[0:1, :], stat_ref[1:2, :]
    gain_one = 1.0 + vec_ref[0:1, :]
    normal = (img_ref[...].astype(F32) - mean_one) * inv_one
    scaled = inner[...] * silu_slope(normal * gain_one + vec_ref[1:2, :]) * gain_one
    means = pair_means(scaled, normal, stat_send, stat_got, partner, core_sems, 3)
    half_back[...] = (
        g0_ref[...] + inv_one * (scaled - means[0] - normal * means[1])
    ).astype(BF)
    mine = grad_ref.at[pl.ds(pl.multiple_of(core * share, share), share), :]
    home = core == side

    @pl.when(home)
    def _():
        remote(half_back, mine, neighbour, back_sems, core).start()
        pltpu.make_async_copy(half_back, mine, load_sems.at[2]).start()

    @pl.when(jnp.logical_not(home))
    def _():
        remote(half_back, mine, diagonal, back_sems, core).start()
        remote(half_back, mine, partner, back_sems, 2 + core).start()

    for _ in range(2 * steps):
        total.step()

    need("ql", "qr", "ul", "ur")
    blocks = up_right_ref.shape[3] // D
    base = 4 * blocks * 8

    def update(state, at, grads):
        return adamw_parts([state[(entry,) + at] for entry in range(4)], grads)

    def sided(values):
        size = values.shape[1] // 2

        @pl.when(side == 0)
        def _():
            half_row[...] = values[:, :size]

        @pl.when(side == 1)
        def _():
            half_row[...] = values[:, size:]

        return half_row[...]

    for member in range(2):
        at = pl.ds(base + 8 * member, 8)
        weight, moment, second, average = update(qr_state, (member,), sided(sum_ref[at, :]))
        qr_new[0, member] = weight
        qr_new[1, member] = average
        qr_copy[member] = weight.astype(BF)
        moments[1, 0, member] = moment
        moments[1, 1, member] = second
        at = pl.ds(base + 16 + 8 * member, 8)
        parts = update(ul_state, (member,), sum_ref[at, :])
        for entry in range(4):
            ul_new[entry, member] = parts[entry]
        ul_copy[member] = parts[0].astype(BF)
        at = pl.ds(base + 32 + 8 * member, 8)
        weight, moment, second, average = update(ql_state, (member,), sum_ref[at, :])
        ql_new[0, member] = weight
        ql_new[1, member] = average
        ql_copy[member] = weight.astype(BF)
        moments[0, 0, member] = sided(moment)
        moments[0, 1, member] = sided(second)
        for part_number in range(2):
            for block in range(blocks // 2):
                row = ((member * 2 + part_number) * blocks + side * (blocks // 2) + block) * 8
                grads = sum_ref[pl.ds(pl.multiple_of(row, 8), 8), :]
                cols = slice(block * D, (block + 1) * D)
                parts = adamw_parts(
                    [ur_state[entry, member, part_number, :, cols] for entry in range(4)], grads
                )
                for entry in range(4):
                    ur_new[entry, member, part_number, :, cols] = parts[entry]
                ur_copy[member, part_number, :, cols] = parts[0].astype(BF)

    def part(which):
        return grad_ref.at[pl.ds(pl.multiple_of(which * share, share), share), :]

    @pl.when(home)
    def _():
        remote(half_back, mine, neighbour, back_sems, core).wait_send()
        pltpu.make_async_copy(half_back, mine, load_sems.at[2]).wait()
        remote(half_back, part(1 - core), partner, back_sems, 3 - core).wait_recv()

    @pl.when(jnp.logical_not(home))
    def _():
        remote(half_back, mine, diagonal, back_sems, core).wait_send()
        remote(half_back, mine, partner, back_sems, 2 + core).wait_send()
        remote(half_back, part(core), neighbour, back_sems, core).wait_recv()
        remote(half_back, part(1 - core), diagonal, back_sems, 1 - core).wait_recv()


def pair_means(scaled, normal, stat_send, stat_got, partner, sems, slot):
    stat_send[0:1, :] = group_mean(col_mean(scaled))
    stat_send[1:2, :] = group_mean(col_mean(scaled * normal))
    copy = remote(stat_send, stat_got, partner, sems, slot)
    copy.start()
    copy.wait()
    both = 0.5 * (stat_send[...] + stat_got[...])
    return both[0:1, :], both[1:2, :]


def conv_back(g0, h1, img, stats, split, vectors, grads, states, one, two, devices):
    share = g0.shape[0]
    steps = devices.bit_length() - 1
    dma = pltpu.SemaphoreType.DMA
    unit = 8 << Halving.HALVINGS
    rows = -(-sum(g.size // D for g in grads) // unit) * unit
    ql, qr, ul, ur = states
    outs = [
        ((2 * share, D), BF, WHOLE),
        ((2,) + ql.shape[1:], F32, WHOLE),
        (ql.shape[1:], BF, WHOLE),
        ((2,) + qr.shape[1:], F32, WHOLE),
        (qr.shape[1:], BF, WHOLE),
        (ul.shape, F32, WHOLE),
        (ul.shape[1:], BF, WHOLE),
        (ur.shape, F32, WHOLE),
        (ur.shape[1:], BF, WHOLE),
        ((2, 2) + qr.shape[1:], F32, WHOLE),
    ]
    scratch = [
        pltpu.VMEM((rows, D), F32),
        pltpu.VMEM((9, D, D), BF),
        pltpu.VMEM((9, D, D), BF),
        pltpu.VMEM((share + 2 * SIDE, 3 * D), BF),
        pltpu.VMEM((share + 2 * SIDE, D), F32),
        pltpu.VMEM((share, D), BF),
        pltpu.VMEM((8, D), F32),
        pltpu.VMEM((8, D), F32),
        pltpu.VMEM((SIDE, D), BF),
        pltpu.VMEM((SIDE, D), BF),
        pltpu.VMEM((rows, D), F32),
        pltpu.VMEM((Halving.room(rows, steps), D), F32),
        pltpu.VMEM(qr.shape[2:], F32),
        dma((3,)),
        dma((2, 4)),
        dma((2, steps + Halving.HALVINGS)),
        dma((2, 4)),
    ]
    outs, scratch = numbered("o", outs), numbered("s", scratch)
    order = ("g0", "h1", "img", "stats", "split", "vec", "up_right", "up_left")
    order += ("query_right", "query_left", "ql", "qr", "ul", "ur")
    given = dict(zip(order, (g0, h1, img, stats, split, vectors, *grads, *states)))
    ins = {n: (given[n], None) for n in order[:1] + order[6:10] + order[1:6] + order[10:]}
    anywhere = pl.BlockSpec(memory_space=pl.ANY)
    ins["one"] = (one, anywhere)
    ins["two"] = (two, anywhere)

    def body(r):
        refs = [getattr(r, n) for n in order + ("one", "two") + tuple(outs) + tuple(scratch)]
        conv_back_kernel(steps, r.need, *refs)

    return tuple(vars(call_named(body, "conv_back", ins, outs, scratch, 5)).values())


def shards(
    latents,
    out_grad,
    text_states,
    time_embed,
    group_ids,
    group_weights,
    timesteps,
    step_weights,
    vectors,
    split_vectors,
    up_bias,
    conv_one,
    conv_two,
    time_proj,
    self_query,
    self_kv,
    self_out,
    cross_query,
    cross_kv,
    cross_out,
    ff_up,
    ff_down,
    query_left_state,
    query_right_state,
    up_left_state,
    up_right_state,
):
    devices_dp = lax.axis_size("dp")
    chips = devices_dp // 2
    side = lax.axis_index("mp")

    def join_sides(values):
        other = lax.ppermute(values, "mp", [(0, 1), (1, 0)])
        first = jnp.where(side == 0, values, other)
        second = jnp.where(side == 0, other, values)
        return jnp.concatenate([first, second], axis=-1)

    pieces = [
        conv_one,
        time_proj[None],
        conv_two.transpose(0, 2, 1),
        self_query[None],
        self_kv.transpose(1, 0, 2),
        self_out.T[None],
        cross_query[None],
        cross_kv.transpose(1, 0, 2),
        cross_out.T[None],
        jnp.concatenate([ff_up.transpose(1, 0, 2), ff_down.T[None]], axis=0),
    ]
    gathers = all(piece.shape[1] % 8 == 0 for piece in pieces)
    full = None
    if not gathers:
        full = [lax.all_gather(join_sides(p), "dp", axis=1, tiled=True) for p in pieces]
    query_left_turned = query_left_state.transpose(0, 1, 3, 2)
    up_left_turned = up_left_state.transpose(0, 1, 3, 2)
    up_rows = up_right_state[0].transpose(2, 0, 1, 3)
    arrays = {
        "lat": latents[0],
        "emb": time_embed,
        "text": text_states[0],
        "split": split_vectors,
        "bias": up_bias,
        "qr": query_right_state[0].reshape(-1, query_right_state.shape[-1]),
        "ur": up_rows.reshape(-1, up_rows.shape[-1]),
        "ql": query_left_turned[0],
        "ul": up_left_turned[0],
        "vec": vectors,
        "cot": out_grad[0],
        "step": timesteps[:, None],
        "group": group_ids[:, None],
        "step_weights": step_weights[None],
        "group_weights": group_weights[None],
    }
    fwd = forward(arrays, pieces, full, chips)
    if not gathers:
        w_one, _, w_two_t, w_q, w_kv, w_so_t, w_cq, _, w_co_t, w_ff = full
    else:
        w_one, w_two_t, w_q, w_kv = fwd.full_one, fwd.full_two, fwd.full_q, fwd.full_kv
        w_so_t, w_cq, w_co_t, w_ff = fwd.full_so, fwd.full_cq, fwd.full_co, fwd.full_ff
    grad_up_right, grad_up_left = fwd.up_right, fwd.up_left
    cotangent, grad_query_right, grad_query_left, block_out = attention_back(
        fwd.g2,
        fwd.h,
        fwd.h2,
        vectors,
        w_q[0],
        fwd.yq,
        fwd.zq,
        w_kv,
        w_so_t[0],
        w_cq[0],
        w_co_t[0],
        fwd.q,
        fwd.kv,
        fwd.o,
        fwd.lse,
        fwd.cq,
        fwd.ckv,
        fwd.all_qr,
        query_left_turned[0],
        fwd.out_img,
    )
    block_out = block_out[None]
    (
        latents_grad,
        query_left_new,
        query_left_copy,
        query_right_new,
        query_right_copy,
        up_left_new,
        up_left_copy,
        up_right_new,
        up_right_copy,
        query_moments,
    ) = conv_back(
        cotangent,
        fwd.h1,
        fwd.img,
        fwd.stats,
        fwd.all_split,
        vectors,
        [grad_up_right, grad_up_left, grad_query_right, grad_query_left],
        [
            query_left_turned,
            query_right_state,
            up_left_turned,
            up_right_state.transpose(0, 1, 3, 2, 4),
        ],
        w_one,
        w_two_t,
        devices_dp * 2,
    )
    return (
        block_out,
        latents_grad[None],
        query_left_new.transpose(0, 1, 3, 2),
        query_left_copy.transpose(0, 2, 1),
        query_right_new,
        query_right_copy,
        up_left_new.transpose(0, 1, 3, 2),
        up_left_copy.transpose(0, 2, 1),
        up_right_new.transpose(0, 1, 3, 2, 4),
        up_right_copy.transpose(0, 2, 1, 3),
        query_moments,
    )


def solution(mesh):
    placed = (
        P("dp", None, None),
        P("dp", "mp", None),
        P("dp", None, None),
        P("dp", None),
        P("dp"),
        P(),
        P("dp"),
        P(),
        P(),
        P(None, "mp"),
        P(None, "mp"),
        P(None, "dp", "mp"),
        P(None, "mp", "dp"),
        P("dp", "mp"),
        P("dp", "mp"),
        P("dp", None, "mp"),
        P("mp", "dp"),
        P("dp", "mp"),
        P("dp", None, "mp"),
        P("mp", "dp"),
        P("dp", None, "mp"),
        P("mp", "dp"),
        P(),
        P(None, None, None, "mp"),
        P(),
        P(None, None, None, None, "mp"),
    )
    return jax.shard_map(
        shards,
        mesh=mesh,
        in_specs=placed,
        out_specs=(
            P("dp", "mp", None),
            P("dp", None, None),
            P(),
            P(),
            P(None, None, None, "mp"),
            P(None, None, "mp"),
            P(),
            P(),
            P(None, None, None, None, "mp"),
            P(None, None, None, "mp"),
            P(None, None, None, None, "mp"),
        ),
        check_vma=False,
    )
```
